32 devices in a mesh: row: 8 (over y, x, core), col: 4 (over z).
Axes of the slice: x: 2, y: 2, z: 4, core: 2. Of those that a mesh axis runs over, the one named last changes fastest.
Arguments:
- eigvec: float32 [8192, 1024], P('row', 'col'), may hold values from -6 to 6
- refl: float32 [4, 8192, 256], P(None, ('row', 'col')), may hold values from -0.25 to 0.25
- tfac: float32 [4, 4096, 256], P(None, ('row', 'col')), may hold values from -0.375 to 0.375
- sched: int32 [16, 4], P('row'), may hold values from 0 to 3, each once within a row
Outputs:
- result: float32 [8192, 1024], P('row', 'col')
The draws below stay inside these ranges and needn't reach their ends.
Inputs may be any that keep to these rules, and one draw needn't show every extreme that they name: Each row of sched names every slot 0 to 3 exactly once.
All inputs are finite; a program needn't handle non-finite values.
Results may differ from the reference program's by a relative error of at most 0.0002.
Values sent between devices are 32-bit elements; how exact they have to be, the bound alone decides.
A program may use at most 64 MiB of HBM per device.

```python
import jax
import jax.numpy as jnp
from jax import lax

B = 512
W = 256
STEPS = 4
GROUPS = 16
ORDER = 8192
EVECS = 1024


def levels(stream_key, shape, cuts, least, top_value):
    def one(dim, parts):
        heights = jax.random.uniform(jax.random.fold_in(jax.random.fold_in(stream_key, 6), dim), (parts,), jnp.float32, least / len(cuts), top_value / len(cuts))
        return jnp.repeat(jnp.exp(heights), shape[dim] // parts).reshape((-1,) + (1,) * (len(shape) - dim - 1))

    gain = one(*cuts[0])
    for cut in cuts[1:]:
        gain = gain * one(*cut)
    return gain


def centred(stream_key, shape, width, limit, shards=(), kind=jnp.bfloat16):
    entries = jax.random.normal(stream_key, shape, jnp.float32) * width
    if len(shards) > 0:
        entries = levels(stream_key, shape, shards, -0.22, 0.18) * entries
    return jnp.clip(entries, min=-limit, max=limit).astype(kind)


def setup_inputs(seed: int = 0) -> dict:
    key_of = jax.random.split(jax.random.key(seed), 5)
    return {
        "eigvec": centred(key_of[0], (ORDER, EVECS), 1.0, 6.0, ((0, 8), (1, 4)), jnp.float32),
        "refl": centred(key_of[1], (STEPS, ORDER, W), B ** -0.5, 0.25, ((1, 32),), jnp.float32),
        "tfac": centred(key_of[2], (STEPS, GROUPS * W, W), W ** -0.5, 0.375, ((1, 32),), jnp.float32),
        "sched": jax.vmap(lambda own: jax.random.permutation(own, STEPS))(jax.random.split(key_of[3], GROUPS)).reshape((GROUPS, STEPS)).astype(jnp.int32),
    }


def apply_blocks(field, vectors, factor):
    coupling = jnp.einsum('gbw,gbe->gwe', vectors, field, precision=lax.Precision.HIGHEST)
    coeffs = jnp.einsum('gvw,gwe->gve', factor, coupling, precision=lax.Precision.HIGHEST)
    return field - jnp.einsum('gbw,gwe->gbe', vectors, coeffs, precision=lax.Precision.HIGHEST)


def reference(eigvec, refl, tfac, sched):
    groups = sched.shape[0]
    evcount = eigvec.shape[1]
    stacked_v = refl.reshape(STEPS, groups, B, W)
    stacked_t = tfac.reshape(STEPS, groups, W, W)
    group_ids = jnp.arange(groups).astype(jnp.int32)
    field = eigvec
    for step_no in range(STEPS):
        slots = sched[:, step_no].astype(jnp.int32)
        vectors = stacked_v[slots, group_ids]
        factor = stacked_t[slots, group_ids]
        if step_no % 2 == 0:
            field = apply_blocks(field.reshape(groups, B, evcount), vectors, factor).reshape(groups * B, evcount)
        else:
            middle = field[W:groups * B - W].reshape(groups - 1, B, evcount)
            middle = apply_blocks(middle, vectors[:-1], factor[:-1]).reshape((groups - 1) * B, evcount)
            field = jnp.concatenate([field[:W], middle, field[groups * B - W:]], axis=0)
    return field
```

```python
import functools

import jax
import jax.numpy as jnp
from jax import lax
from jax.experimental import pallas as pl
from jax.experimental.pallas import tpu as pltpu
from jax.sharding import PartitionSpec as P

B = 512
W = 256
MESH = pl.DeviceIdType.MESH


def split(x):
    high = x.astype(jnp.bfloat16)
    low = (x - high.astype(jnp.float32)).astype(jnp.bfloat16)
    return high, low


def product(left, right, dims):
    def one(a, b):
        return lax.dot_general(a, b, (dims, ((), ())), preferred_element_type=jnp.float32)

    return one(left[0], right[0]) + (one(left[0], right[1]) + one(left[1], right[0]))


def pick_kernel(slots, refl, tfac, packed, hold, in_sem, out_sem):
    steps = packed.shape[0]
    v_rows = refl.shape[1]
    t_rows = tfac.shape[1]
    loads, stores = [], []
    for s in range(steps):
        slot = slots[s]
        loads.append(
            (
                pltpu.make_async_copy(refl.at[slot], hold.at[s, pl.ds(0, v_rows)], in_sem.at[s, 0]),
                pltpu.make_async_copy(tfac.at[slot], hold.at[s, pl.ds(v_rows, t_rows)], in_sem.at[s, 1]),
            )
        )
        stores.append(pltpu.make_async_copy(hold.at[s], packed.at[s], out_sem.at[s]))
    for pair in loads:
        for copy in pair:
            copy.start()
    for pair, store in zip(loads, stores):
        for copy in pair:
            copy.wait()
        store.start()
    for store in stores:
        store.wait()


def main_kernel(n, rows_n, groups, packed, eig, out, field, buf, inb, back, landed, own_sem, eig_sem, out_sem,
                ring_send, ring_recv, up_send, up_recv, down_send, down_recv):
    steps, piece, _ = packed.shape
    v_rows = groups * B // n
    per_group = n // groups
    half = piece // 2
    hops = n // 2
    row = lax.axis_index("row")
    col = lax.axis_index("col")
    right = lax.rem(col + 1, n)
    left = lax.rem(col + n - 1, n)
    has_down = row < rows_n - 1
    has_up = row > 0
    down = jnp.minimum(row + 1, rows_n - 1)
    up = jnp.maximum(row - 1, 0)

    eig_copy = pltpu.make_async_copy(eig, field, eig_sem)
    eig_copy.start()

    barrier = pltpu.get_barrier_semaphore()
    pl.semaphore_signal(barrier, inc=1, device_id=(row, left), device_id_type=MESH)
    pl.semaphore_signal(barrier, inc=1, device_id=(row, right), device_id_type=MESH)

    @pl.when(has_up)
    def _():
        pl.semaphore_signal(barrier, inc=1, device_id=(up, col), device_id_type=MESH)

    @pl.when(has_down)
    def _():
        pl.semaphore_signal(barrier, inc=1, device_id=(down, col), device_id_type=MESH)

    pl.semaphore_wait(barrier, 2 + jnp.minimum(row, 1) + jnp.minimum(rows_n - 1 - row, 1))

    def ring_copy(s, way, hop, part):
        target = right if way == 0 else left
        owner = lax.rem(col + n - hop, n) if way == 0 else lax.rem(col + hop, n)
        span = pl.ds(part * half, half)
        src = packed.at[s, span] if hop == 0 else buf.at[s, owner, span]
        return pltpu.make_async_remote_copy(
            src_ref=src,
            dst_ref=buf.at[s, owner, span],
            send_sem=ring_send.at[s, way, hop, part],
            recv_sem=ring_recv.at[s, way, hop, part],
            device_id=(row, target),
            device_id_type=MESH,
        )

    def parts_of(way, hop):
        order = (0, 1) if way == 0 else (1, 0)
        return order[:1] if hop == hops - 1 else order

    def send_own(s):
        for k in range(len(parts_of(0, 0))):
            for way in (0, 1):
                ring_copy(s, way, 0, parts_of(way, 0)[k]).start()

    def forward(s):
        for hop in range(1, hops):
            for k in range(len(parts_of(0, hop))):
                for way in (0, 1):
                    part = parts_of(way, hop)[k]
                    ring_copy(s, way, hop - 1, part).wait_recv()
                    ring_copy(s, way, hop, part).start()

    def finish(s):
        for hop in range(hops):
            for way in (0, 1):
                done = parts_of(way, hop + 1) if hop + 1 < hops else ()
                for part in parts_of(way, hop):
                    if part not in done:
                        ring_copy(s, way, hop, part).wait_recv()

    def vectors_of(s, g):
        block = buf[s, g * per_group:(g + 1) * per_group, :v_rows]
        return split(block.reshape(B, W))

    def factor_of(s, g):
        block = buf[s, g * per_group:(g + 1) * per_group, v_rows:]
        return split(block.reshape(W, W))

    def coeffs_of(s, g, vectors, rows):
        coupling = product(vectors, split(rows), ((0,), (0,)))
        return split(product(factor_of(s, g), split(coupling), ((1,), (0,))))

    def apply_local(s, g, start):
        vectors = vectors_of(s, g)
        rows = field[start:start + B]
        coeffs = coeffs_of(s, g, vectors, rows)
        field[start:start + B] = rows - product(vectors, coeffs, ((1,), (0,)))

    def up_copy(i):
        return pltpu.make_async_remote_copy(
            src_ref=field.at[pl.ds(0, W)], dst_ref=inb.at[i],
            send_sem=up_send.at[i], recv_sem=up_recv.at[i],
            device_id=(up, col), device_id_type=MESH,
        )

    def down_copy(i):
        return pltpu.make_async_remote_copy(
            src_ref=back.at[i], dst_ref=landed.at[i],
            send_sem=down_send.at[i], recv_sem=down_recv.at[i],
            device_id=(down, col), device_id_type=MESH,
        )

    low = groups * B - W

    send_own(0)
    own = [pltpu.make_async_copy(packed.at[s], buf.at[s, col], own_sem.at[s]) for s in range(steps)]
    for copy in own:
        copy.start()
    eig_copy.wait()
    for s in range(steps):
        forward(s)
        if s + 1 < steps:
            send_own(s + 1)
        own[s].wait()
        finish(s)
        i = s // 2
        if s % 2 == 0:
            for g in range(groups):
                apply_local(s, g, g * B)
                if g == 0 and s + 1 < steps:
                    @pl.when(has_up)
                    def _():
                        up_copy(i).start()
        else:
            @pl.when(has_down)
            def _():
                up_copy(i).wait_recv()
                g = groups - 1
                vectors = vectors_of(s, g)
                rows = jnp.concatenate([field[low:], inb[i]], axis=0)
                coeffs = coeffs_of(s, g, vectors, rows)
                bottom = (vectors[0][W:], vectors[1][W:])
                back[i] = rows[W:] - product(bottom, coeffs, ((1,), (0,)))
                down_copy(i).start()
                top = (vectors[0][:W], vectors[1][:W])
                field[low:] = rows[:W] - product(top, coeffs, ((1,), (0,)))

            for g in range(groups - 1):
                apply_local(s, g, W + g * B)

            @pl.when(has_up)
            def _():
                up_copy(i).wait_send()
                down_copy(i).wait_recv()
                field[:W] = landed[i]

    store = pltpu.make_async_copy(field, out, out_sem)
    store.start()
    for s in range(steps):
        for way in (0, 1):
            for hop in range(hops):
                for part in parts_of(way, hop):
                    ring_copy(s, way, hop, part).wait_send()

    @pl.when(has_down)
    def _():
        for i in range(steps // 2):
            down_copy(i).wait_send()

    store.wait()


def line_kernel(rows_n, sched, refl, tfac, eig, out, refl_in, tfac_in, field, buf, fed, inb, back, landed,
                load_sem, eig_sem, out_sem, feed_send, feed_recv, cols_send, cols_recv, own_send, own_recv,
                relay_send, relay_recv, hand_send, hand_recv, up_send, up_recv, down_send, down_recv,
                res_send, res_recv, share_send, share_recv, state_send, state_recv):
    steps, v_rows, _ = refl.shape
    low = B + W
    last = steps - 1
    row = lax.axis_index("row")
    col = lax.axis_index("col")
    odd = lax.rem(row, 2)
    inner = (col == 1) | (col == 2)
    partner = col + 1 - 2 * lax.rem(col, 2)
    other = 3 - col
    mate = row + 1 - 2 * odd
    beyond = row - 1 + 2 * odd
    has_beyond = (beyond >= 0) & (beyond < rows_n)
    beyond = jnp.clip(beyond, 0, rows_n - 1)
    own_first = (col == 1) == (odd == 0)
    has_down = row < rows_n - 1
    has_up = row > 0
    down = jnp.minimum(row + 1, rows_n - 1)
    up = jnp.maximum(row - 1, 0)

    def remote(src, dst, send, recv, target):
        return pltpu.make_async_remote_copy(
            src_ref=src, dst_ref=dst, send_sem=send, recv_sem=recv,
            device_id=target, device_id_type=MESH,
        )

    refl_load = pltpu.make_async_copy(refl, refl_in, load_sem.at[0])
    tfac_load = pltpu.make_async_copy(tfac, tfac_in, load_sem.at[1])
    eig_load = pltpu.make_async_copy(eig, field.at[0], eig_sem)
    refl_load.start()
    tfac_load.start()

    barrier = pltpu.get_barrier_semaphore()

    def greet(target):
        pl.semaphore_signal(barrier, inc=1, device_id=target, device_id_type=MESH)

    greet((row, partner))
    greet((mate, partner))
    greet((mate, col))

    @pl.when(has_beyond)
    def _():
        greet((beyond, col))
        greet((beyond, partner))

    @pl.when(inner)
    def _():
        greet((row, other))
        greet((mate, other))
        eig_load.start()

    refl_load.wait()
    tfac_load.wait()
    for s in range(steps):
        slot = sched[col // 2, s]
        buf[s, col, :v_rows] = refl_in[slot]
        buf[s, col, v_rows:] = tfac_in[slot]

    pl.semaphore_wait(barrier, 3 + 2 * has_beyond.astype(jnp.int32) + 2 * inner.astype(jnp.int32))

    cuts = (3, 1, 1, 3)
    piece = buf.shape[2]

    def span(s, k):
        size = piece // cuts[s]
        return pl.ds(k * size, size)

    def feed(s, k):
        return remote(buf.at[s, col, span(s, k)], fed.at[s, span(s, k)],
                      feed_send.at[s, k], feed_recv.at[s, k], (mate, partner))

    def columns(g):
        rows = pl.ds(g * B, B)
        return remote(eig.at[rows], field.at[1, rows], cols_send.at[g], cols_recv.at[g], (row, partner))

    def own(s):
        return remote(buf.at[s, col], buf.at[s, col], own_send.at[s], own_recv.at[s], (row, other))

    def own_arrival(s):
        return remote(buf.at[s, other], buf.at[s, other], own_send.at[s], own_recv.at[s], (row, other))

    def relay(s, k):
        return remote(fed.at[s, span(s, k)], buf.at[s, partner, span(s, k)],
                      relay_send.at[s, k], relay_recv.at[s, k], (mate, other))

    def relay_arrival(s, k):
        owner = 3 - partner
        return remote(fed.at[s, span(s, k)], buf.at[s, owner, span(s, k)],
                      relay_send.at[s, k], relay_recv.at[s, k], (mate, other))

    def hand(s, k):
        return remote(fed.at[s, span(s, k)], buf.at[s, partner, span(s, k)],
                      hand_send.at[s, k], hand_recv.at[s, k], (mate, col))

    def result(part, src, target_row):
        rows = (pl.ds(0, W), pl.ds(W, B), pl.ds(low, W))[part]
        return remote(src, out.at[rows], res_send.at[part], res_recv.at[part], (target_row, partner))

    def vectors_of(s, g):
        return split(buf[s, 2 * g:2 * g + 2, :v_rows].reshape(B, W))

    def factor_of(s, g):
        return split(buf[s, 2 * g:2 * g + 2, v_rows:].reshape(W, W))

    def coeffs_of(vectors, factor, rows):
        coupling = product(vectors, split(rows), ((0,), (0,)))
        return split(product(factor, split(coupling), ((1,), (0,))))

    def load(zs, start, size):
        return jnp.concatenate([field[z, start:start + size] for z in zs], axis=1)

    def save(zs, start, value):
        cols = value.shape[1] // len(zs)
        for k, z in enumerate(zs):
            field[z, start:start + value.shape[0]] = value[:, k * cols:(k + 1) * cols]

    def apply_local(s, g, zs, start):
        vectors = vectors_of(s, g)
        rows = load(zs, start, B)
        coeffs = coeffs_of(vectors, factor_of(s, g), rows)
        save(zs, start, rows - product(vectors, coeffs, ((1,), (0,))))

    def up_copy(i, z):
        return remote(field.at[z, pl.ds(0, W)], inb.at[i, z], up_send.at[i, z], up_recv.at[i, z], (up, col))

    def down_copy(z):
        return remote(back.at[0, z], landed.at[z], down_send.at[0, z], down_recv.at[0, z], (down, col))

    def down_final():
        return remote(back.at[1, 0], out.at[pl.ds(0, W)], down_send.at[1, 0], down_recv.at[1, 0], (down, col))

    def send_up(s, zs):
        @pl.when(has_up)
        def _():
            for z in zs:
                up_copy(s // 2, z).start()

    def straddle_body(s, zs, send):
        i = s // 2
        vectors = vectors_of(s, 1)
        below = jnp.concatenate([inb[i, z] for z in zs], axis=1)
        rows = jnp.concatenate([load(zs, low, W), below], axis=0)
        coeffs = coeffs_of(vectors, factor_of(s, 1), rows)
        bottom = (vectors[0][W:], vectors[1][W:])
        value = rows[W:] - product(bottom, coeffs, ((1,), (0,)))
        cols = value.shape[1] // len(zs)
        for k, z in enumerate(zs):
            back[i, z] = value[:, k * cols:(k + 1) * cols]
        send()
        top = (vectors[0][:W], vectors[1][:W])
        save(zs, low, rows[:W] - product(top, coeffs, ((1,), (0,))))

    def straddle(s, zs, send):
        @pl.when(has_down)
        def _():
            for z in zs:
                up_copy(s // 2, z).wait_recv()
            straddle_body(s, zs, send)

    def settle(z):
        @pl.when(has_up)
        def _():
            up_copy(0, z).wait_send()
            down_copy(z).wait_recv()
            field[z, :W] = landed[z]

    def pass_chunk(s, k):
        feed(s, k).wait_recv()
        relay(s, k).start()
        hand(s, k).start()

    def passed(s):
        for k in range(cuts[s]):
            pass_chunk(s, k)

    def own_before(s):
        @pl.when(own_first)
        def _():
            own(s).start()

    def own_after(s):
        @pl.when(jnp.logical_not(own_first))
        def _():
            own(s).start()

    def near(s):
        for k in range(cuts[s]):
            hand(s, k).wait_recv()

    def far(s):
        own_arrival(s).wait_recv()
        for k in range(cuts[s]):
            relay_arrival(s, k).wait_recv()

    def store(part):
        rows = (pl.ds(0, W), pl.ds(W, B), pl.ds(low, W))[part]
        return pltpu.make_async_copy(field.at[0, rows], out.at[rows], out_sem.at[part])

    def share():
        return remote(buf.at[last, col], buf.at[last, col], share_send, share_recv, (row, partner))

    def share_arrival():
        return remote(buf.at[last, partner], buf.at[last, partner], share_send, share_recv, (row, partner))

    def state(part, start):
        rows = pl.ds(start, W)
        return remote(field.at[1, rows], field.at[0, rows], state_send.at[part], state_recv.at[part], (row, partner))

    def state_up():
        return remote(field.at[1, pl.ds(0, W)], inb.at[1, 0], state_send.at[1], state_recv.at[1], (up, partner))

    def bottom_result():
        return remote(back.at[1, 0], out.at[pl.ds(0, W)], res_send.at[0], res_recv.at[0], (down, col))

    @pl.when(jnp.logical_not(inner))
    def _():
        for kind, k in (("feed", 0), ("feed", 1), ("feed", 2), ("cols", 0), ("cols", 1), ("feed", 3)):
            if kind == "feed":
                for c in range(cuts[k]):
                    feed(k, c).start()
            else:
                columns(k).start()
        share_arrival().wait_recv()
        state(0, W).wait_recv()

        @pl.when(col == 0)
        def _():
            state(1, W).wait_recv()
            apply_local(last, 0, (0,), W)
            store(1).start()
            result(0, field.at[0, pl.ds(0, W)], row).wait_recv()
            result(2, field.at[0, pl.ds(0, W)], row).wait_recv()
            store(1).wait()

        @pl.when(col == 3)
        def _():
            @pl.when(has_down)
            def _():
                state_up().wait_recv()
                straddle_body(last, (0,), lambda: bottom_result().start())

            store(2).start()
            result(0, field.at[0, pl.ds(0, W)], row).wait_recv()
            result(1, field.at[0, pl.ds(0, B)], row).wait_recv()
            store(2).wait()

            @pl.when(has_down)
            def _():
                bottom_result().wait_send()

        for s in range(steps):
            for k in range(cuts[s]):
                feed(s, k).wait_send()
        columns(0).wait_send()
        columns(1).wait_send()

    early = jnp.logical_not(own_first)

    @pl.when(inner)
    def _():
        own(0).start()
        share().start()
        passed(0)
        own_before(1)
        eig_load.wait()
        near(0)

        @pl.when(col == 1)
        def _():
            apply_local(0, 0, (0,), 0)
            send_up(0, (0,))

        @pl.when(col == 2)
        def _():
            apply_local(0, 1, (0,), B)

        passed(1)
        own_after(1)
        own_before(2)
        far(0)
        near(1)

        @pl.when(col == 1)
        def _():
            apply_local(0, 1, (0,), B)
            apply_local(1, 0, (0,), W)

        @pl.when(col == 2)
        def _():
            apply_local(0, 0, (0,), 0)
            send_up(0, (0,))
            straddle(1, (0,), lambda: down_copy(0).start())

        passed(2)
        own_after(2)
        own_before(3)
        far(1)

        @pl.when(col == 1)
        def _():
            straddle(1, (0,), lambda: down_copy(0).start())

        @pl.when(col == 2)
        def _():
            apply_local(1, 0, (0,), W)

        columns(0).wait_recv()
        apply_local(0, 0, (1,), 0)
        send_up(0, (1,))
        settle(0)
        near(2)

        @pl.when(col == 1)
        def _():
            apply_local(2, 0, (0,), 0)
            send_up(2, (0,))

        @pl.when(col == 2)
        def _():
            apply_local(2, 1, (0,), B)

        def far_even():
            @pl.when(col == 1)
            def _():
                apply_local(2, 1, (0,), B)

            @pl.when(col == 2)
            def _():
                apply_local(2, 0, (0,), 0)
                send_up(2, (0,))

        @pl.when(early)
        def _():
            far(2)
            far_even()

        columns(1).wait_recv()
        apply_local(0, 1, (1,), B)
        straddle(1, (1,), lambda: down_copy(1).start())
        pass_chunk(3, 0)
        apply_local(1, 0, (1,), W)

        @pl.when(col == 2)
        def _():
            apply_local(2, 1, (1,), B)
            state(0, low).start()

        @pl.when(own_first)
        def _():
            far(2)

        @pl.when(col == 1)
        def _():
            apply_local(2, 1, (1,), B)
            state(0, B).start()

        pass_chunk(3, 1)
        settle(1)
        apply_local(2, 0, (1,), 0)

        @pl.when(col == 1)
        def _():
            state(1, W).start()
            send_up(2, (1,))

        @pl.when((col == 2) & has_up)
        def _():
            state_up().start()

        pass_chunk(3, 2)
        own_after(3)

        @pl.when(own_first)
        def _():
            far_even()

        @pl.when(jnp.logical_not(has_up))
        def _():
            result(0, field.at[1, pl.ds(0, W)], row).start()
            store(0).start()

        near(3)

        @pl.when(col == 1)
        def _():
            apply_local(last, 0, (0,), W)
            store(1).start()
            far(3)
            straddle(last, (1,), lambda: result(0, back.at[1, 1], down).start())
            result(2, field.at[1, pl.ds(low, W)], row).start()
            straddle(last, (0,), lambda: down_final().start())
            store(2).start()

        @pl.when(col == 2)
        def _():
            straddle(last, (0,), lambda: down_final().start())
            store(2).start()
            far(3)
            apply_local(last, 0, (1,), W)
            result(1, field.at[1, pl.ds(W, B)], row).start()
            apply_local(last, 0, (0,), W)
            store(1).start()

        share().wait_send()
        state(0, W).wait_send()
        for s in range(steps):
            own(s).wait_send()
            for k in range(cuts[s]):
                relay(s, k).wait_send()
                hand(s, k).wait_send()

        @pl.when(has_up)
        def _():
            up_copy(last // 2, 0).wait_send()
            down_final().wait_recv()

        @pl.when(has_down)
        def _():
            down_copy(0).wait_send()
            down_copy(1).wait_send()
            down_final().wait_send()

        @pl.when(jnp.logical_not(has_up))
        def _():
            result(0, field.at[1, pl.ds(0, W)], row).wait_send()
            store(0).wait()

        @pl.when(col == 1)
        def _():
            state(1, W).wait_send()

            @pl.when(has_up)
            def _():
                up_copy(last // 2, 1).wait_send()

            @pl.when(has_down)
            def _():
                result(0, back.at[1, 1], down).wait_send()

            result(2, field.at[1, pl.ds(low, W)], row).wait_send()

        @pl.when(col == 2)
        def _():
            @pl.when(has_up)
            def _():
                state_up().wait_send()

            result(1, field.at[1, pl.ds(W, B)], row).wait_send()

        store(1).wait()
        store(2).wait()


def on_device(n, rows_n, eigvec, refl, tfac, sched):
    steps, v_rows, _ = refl.shape
    t_rows = tfac.shape[1]
    groups = sched.shape[0]
    evcount = eigvec.shape[1]
    piece = v_rows + t_rows
    hops = n // 2
    half_steps = steps // 2
    anywhere = pl.BlockSpec(memory_space=pl.ANY)
    if n == 4 and groups == 2 and steps == 4 and rows_n % 2 == 0:
        two = (half_steps, 2)
        chunks = (steps, 3)
        dma = pltpu.SemaphoreType.DMA
        return pl.pallas_call(
            functools.partial(line_kernel, rows_n),
            out_shape=jax.ShapeDtypeStruct(eigvec.shape, jnp.float32),
            in_specs=[pl.BlockSpec(memory_space=pltpu.SMEM), anywhere, anywhere, anywhere],
            out_specs=anywhere,
            scratch_shapes=[
                pltpu.VMEM(refl.shape, jnp.float32),
                pltpu.VMEM(tfac.shape, jnp.float32),
                pltpu.VMEM((2, *eigvec.shape), jnp.float32),
                pltpu.VMEM((steps, n, piece, W), jnp.float32),
                pltpu.VMEM((steps, piece, W), jnp.float32),
                pltpu.VMEM((*two, W, evcount), jnp.float32),
                pltpu.VMEM((*two, W, evcount), jnp.float32),
                pltpu.VMEM((2, W, evcount), jnp.float32),
                dma((2,)),
                dma,
                dma((3,)),
                dma(chunks),
                dma(chunks),
                dma((2,)),
                dma((2,)),
                dma((steps,)),
                dma((steps,)),
                dma(chunks),
                dma(chunks),
                dma(chunks),
                dma(chunks),
                dma(two),
                dma(two),
                dma(two),
                dma(two),
                dma((3,)),
                dma((3,)),
                dma,
                dma,
                dma((2,)),
                dma((2,)),
            ],
            compiler_params=pltpu.CompilerParams(
                collective_id=0, has_side_effects=True, vmem_limit_bytes=60 << 20
            ),
            name="sweep",
        )(sched, refl, tfac, eigvec)
    owner = lax.axis_index("col") * v_rows // B
    slots = lax.dynamic_index_in_dim(sched, owner, 0, keepdims=False)
    packed = pl.pallas_call(
        pick_kernel,
        out_shape=jax.ShapeDtypeStruct((steps, piece, W), jnp.float32),
        in_specs=[pl.BlockSpec(memory_space=pltpu.SMEM), anywhere, anywhere],
        out_specs=anywhere,
        scratch_shapes=[
            pltpu.VMEM((steps, piece, W), jnp.float32),
            pltpu.SemaphoreType.DMA((steps, 2)),
            pltpu.SemaphoreType.DMA((steps,)),
        ],
        name="pick",
    )(slots, refl, tfac)
    return pl.pallas_call(
        functools.partial(main_kernel, n, rows_n, groups),
        out_shape=jax.ShapeDtypeStruct(eigvec.shape, jnp.float32),
        in_specs=[anywhere, anywhere],
        out_specs=anywhere,
        scratch_shapes=[
            pltpu.VMEM(eigvec.shape, jnp.float32),
            pltpu.VMEM((steps, n, piece, W), jnp.float32),
            pltpu.VMEM((half_steps, W, evcount), jnp.float32),
            pltpu.VMEM((half_steps, W, evcount), jnp.float32),
            pltpu.VMEM((half_steps, W, evcount), jnp.float32),
            pltpu.SemaphoreType.DMA((steps,)),
            pltpu.SemaphoreType.DMA,
            pltpu.SemaphoreType.DMA,
            pltpu.SemaphoreType.DMA((steps, 2, hops, 2)),
            pltpu.SemaphoreType.DMA((steps, 2, hops, 2)),
            pltpu.SemaphoreType.DMA((half_steps,)),
            pltpu.SemaphoreType.DMA((half_steps,)),
            pltpu.SemaphoreType.DMA((half_steps,)),
            pltpu.SemaphoreType.DMA((half_steps,)),
        ],
        compiler_params=pltpu.CompilerParams(
            collective_id=0, has_side_effects=True, vmem_limit_bytes=48 << 20
        ),
        name="sweep",
    )(packed, eigvec)


def solution(mesh):
    placed = (
        P("row", "col"),
        P(None, ("row", "col"), None),
        P(None, ("row", "col"), None),
        P("row", None),
    )
    body = functools.partial(on_device, mesh.shape["col"], mesh.shape["row"])
    return jax.shard_map(body, mesh=mesh, in_specs=placed, out_specs=P("row", "col"), check_vma=False)
```

```python
import functools

import jax
import jax.numpy as jnp
from jax import lax
from jax.experimental import pallas as pl
from jax.experimental.pallas import tpu as pltpu
from jax.sharding import PartitionSpec as P

B = 512
W = 256
MESH = pl.DeviceIdType.MESH


def split(x):
    high = x.astype(jnp.bfloat16)
    low = (x - high.astype(jnp.float32)).astype(jnp.bfloat16)
    return high, low


def product(left, right, dims):
    def one(a, b):
        return lax.dot_general(a, b, (dims, ((), ())), preferred_element_type=jnp.float32)

    return one(left[0], right[0]) + (one(left[0], right[1]) + one(left[1], right[0]))


def pick_kernel(slots, refl, tfac, packed, hold, in_sem, out_sem):
    steps = packed.shape[0]
    v_rows = refl.shape[1]
    t_rows = tfac.shape[1]
    loads, stores = [], []
    for s in range(steps):
        slot = slots[s]
        loads.append(
            (
                pltpu.make_async_copy(refl.at[slot], hold.at[s, pl.ds(0, v_rows)], in_sem.at[s, 0]),
                pltpu.make_async_copy(tfac.at[slot], hold.at[s, pl.ds(v_rows, t_rows)], in_sem.at[s, 1]),
            )
        )
        stores.append(pltpu.make_async_copy(hold.at[s], packed.at[s], out_sem.at[s]))
    for pair in loads:
        for copy in pair:
            copy.start()
    for pair, store in zip(loads, stores):
        for copy in pair:
            copy.wait()
        store.start()
    for store in stores:
        store.wait()


def main_kernel(n, rows_n, groups, packed, eig, out, field, buf, inb, back, landed, own_sem, eig_sem, out_sem,
                ring_send, ring_recv, up_send, up_recv, down_send, down_recv):
    steps, piece, _ = packed.shape
    v_rows = groups * B // n
    per_group = n // groups
    half = piece // 2
    hops = n // 2
    row = lax.axis_index("row")
    col = lax.axis_index("col")
    right = lax.rem(col + 1, n)
    left = lax.rem(col + n - 1, n)
    has_down = row < rows_n - 1
    has_up = row > 0
    down = jnp.minimum(row + 1, rows_n - 1)
    up = jnp.maximum(row - 1, 0)

    eig_copy = pltpu.make_async_copy(eig, field, eig_sem)
    eig_copy.start()

    barrier = pltpu.get_barrier_semaphore()
    pl.semaphore_signal(barrier, inc=1, device_id=(row, left), device_id_type=MESH)
    pl.semaphore_signal(barrier, inc=1, device_id=(row, right), device_id_type=MESH)

    @pl.when(has_up)
    def _():
        pl.semaphore_signal(barrier, inc=1, device_id=(up, col), device_id_type=MESH)

    @pl.when(has_down)
    def _():
        pl.semaphore_signal(barrier, inc=1, device_id=(down, col), device_id_type=MESH)

    pl.semaphore_wait(barrier, 2 + jnp.minimum(row, 1) + jnp.minimum(rows_n - 1 - row, 1))

    def ring_copy(s, way, hop, part):
        target = right if way == 0 else left
        owner = lax.rem(col + n - hop, n) if way == 0 else lax.rem(col + hop, n)
        span = pl.ds(part * half, half)
        src = packed.at[s, span] if hop == 0 else buf.at[s, owner, span]
        return pltpu.make_async_remote_copy(
            src_ref=src,
            dst_ref=buf.at[s, owner, span],
            send_sem=ring_send.at[s, way, hop, part],
            recv_sem=ring_recv.at[s, way, hop, part],
            device_id=(row, target),
            device_id_type=MESH,
        )

    def parts_of(way, hop):
        order = (0, 1) if way == 0 else (1, 0)
        return order[:1] if hop == hops - 1 else order

    def send_own(s):
        for k in range(len(parts_of(0, 0))):
            for way in (0, 1):
                ring_copy(s, way, 0, parts_of(way, 0)[k]).start()

    def forward(s):
        for hop in range(1, hops):
            for k in range(len(parts_of(0, hop))):
                for way in (0, 1):
                    part = parts_of(way, hop)[k]
                    ring_copy(s, way, hop - 1, part).wait_recv()
                    ring_copy(s, way, hop, part).start()

    def finish(s):
        for hop in range(hops):
            for way in (0, 1):
                done = parts_of(way, hop + 1) if hop + 1 < hops else ()
                for part in parts_of(way, hop):
                    if part not in done:
                        ring_copy(s, way, hop, part).wait_recv()

    def vectors_of(s, g):
        block = buf[s, g * per_group:(g + 1) * per_group, :v_rows]
        return split(block.reshape(B, W))

    def factor_of(s, g):
        block = buf[s, g * per_group:(g + 1) * per_group, v_rows:]
        return split(block.reshape(W, W))

    def coeffs_of(s, g, vectors, rows):
        coupling = product(vectors, split(rows), ((0,), (0,)))
        return split(product(factor_of(s, g), split(coupling), ((1,), (0,))))

    def apply_local(s, g, start):
        vectors = vectors_of(s, g)
        rows = field[start:start + B]
        coeffs = coeffs_of(s, g, vectors, rows)
        field[start:start + B] = rows - product(vectors, coeffs, ((1,), (0,)))

    def up_copy(i):
        return pltpu.make_async_remote_copy(
            src_ref=field.at[pl.ds(0, W)], dst_ref=inb.at[i],
            send_sem=up_send.at[i], recv_sem=up_recv.at[i],
            device_id=(up, col), device_id_type=MESH,
        )

    def down_copy(i):
        return pltpu.make_async_remote_copy(
            src_ref=back.at[i], dst_ref=landed.at[i],
            send_sem=down_send.at[i], recv_sem=down_recv.at[i],
            device_id=(down, col), device_id_type=MESH,
        )

    low = groups * B - W

    send_own(0)
    own = [pltpu.make_async_copy(packed.at[s], buf.at[s, col], own_sem.at[s]) for s in range(steps)]
    for copy in own:
        copy.start()
    eig_copy.wait()
    for s in range(steps):
        forward(s)
        if s + 1 < steps:
            send_own(s + 1)
        own[s].wait()
        finish(s)
        i = s // 2
        if s % 2 == 0:
            for g in range(groups):
                apply_local(s, g, g * B)
                if g == 0 and s + 1 < steps:
                    @pl.when(has_up)
                    def _():
                        up_copy(i).start()
        else:
            @pl.when(has_down)
            def _():
                up_copy(i).wait_recv()
                g = groups - 1
                vectors = vectors_of(s, g)
                rows = jnp.concatenate([field[low:], inb[i]], axis=0)
                coeffs = coeffs_of(s, g, vectors, rows)
                bottom = (vectors[0][W:], vectors[1][W:])
                back[i] = rows[W:] - product(bottom, coeffs, ((1,), (0,)))
                down_copy(i).start()
                top = (vectors[0][:W], vectors[1][:W])
                field[low:] = rows[:W] - product(top, coeffs, ((1,), (0,)))

            for g in range(groups - 1):
                apply_local(s, g, W + g * B)

            @pl.when(has_up)
            def _():
                up_copy(i).wait_send()
                down_copy(i).wait_recv()
                field[:W] = landed[i]

    store = pltpu.make_async_copy(field, out, out_sem)
    store.start()
    for s in range(steps):
        for way in (0, 1):
            for hop in range(hops):
                for part in parts_of(way, hop):
                    ring_copy(s, way, hop, part).wait_send()

    @pl.when(has_down)
    def _():
        for i in range(steps // 2):
            down_copy(i).wait_send()

    store.wait()


def line_kernel(rows_n, sched_all, refl, tfac, eig, out, sched, refl_in, tfac_in, field, buf, fed, inb, back, landed,
                load_sem, eig_sem, out_sem, feed_send, feed_recv, cols_send, cols_recv, own_send, own_recv,
                relay_send, relay_recv, hand_send, hand_recv, up_send, up_recv, down_send, down_recv,
                res_send, res_recv, share_send, share_recv, state_send, state_recv, turn_sem):
    steps, v_rows, _ = refl.shape
    low = B + W
    last = steps - 1
    row = lax.axis_index("row")
    col = lax.axis_index("col")
    odd = lax.rem(row, 2)
    inner = (col == 1) | (col == 2)
    partner = col + 1 - 2 * lax.rem(col, 2)
    other = 3 - col
    mate = row + 1 - 2 * odd
    beyond = row - 1 + 2 * odd
    has_beyond = (beyond >= 0) & (beyond < rows_n)
    beyond = jnp.clip(beyond, 0, rows_n - 1)
    own_first = (col == 1) == (odd == 0)
    has_down = row < rows_n - 1
    has_up = row > 0
    down = jnp.minimum(row + 1, rows_n - 1)
    up = jnp.maximum(row - 1, 0)

    def remote(src, dst, send, recv, target):
        return pltpu.make_async_remote_copy(
            src_ref=src, dst_ref=dst, send_sem=send, recv_sem=recv,
            device_id=target, device_id_type=MESH,
        )

    refl_load = pltpu.make_async_copy(refl, refl_in, load_sem.at[0])
    tfac_load = pltpu.make_async_copy(tfac, tfac_in, load_sem.at[1])
    eig_load = pltpu.make_async_copy(eig, field.at[0], eig_sem)
    sched_load = pltpu.make_async_copy(sched_all, sched, load_sem.at[2])
    sched_load.start()
    refl_load.start()
    tfac_load.start()

    barrier = pltpu.get_barrier_semaphore()

    def greet(target):
        pl.semaphore_signal(barrier, inc=1, device_id=target, device_id_type=MESH)

    greet((row, partner))
    greet((mate, partner))
    greet((mate, col))

    @pl.when(has_beyond)
    def _():
        greet((beyond, col))
        greet((beyond, partner))

    @pl.when(inner)
    def _():
        greet((row, other))
        greet((mate, other))

    sched_load.wait()
    refl_load.wait()
    tfac_load.wait()

    @pl.when(inner)
    def _():
        eig_load.start()

    for s in range(steps):
        slot = sched[col // 2, s]
        buf[s, col, :v_rows] = refl_in[slot]
        buf[s, col, v_rows:] = tfac_in[slot]

    pl.semaphore_wait(barrier, 3 + 2 * has_beyond.astype(jnp.int32) + 2 * inner.astype(jnp.int32))

    cuts = (3, 1, 1, 3)
    piece = buf.shape[2]

    def span(s, k):
        size = piece // cuts[s]
        return pl.ds(k * size, size)

    def feed(s, k):
        return remote(buf.at[s, col, span(s, k)], fed.at[s, span(s, k)],
                      feed_send.at[s, k], feed_recv.at[s, k], (mate, partner))

    column_rows = ((0, B), (B, W), (B + W, W))

    def columns(g):
        rows = pl.ds(*column_rows[g])
        return remote(eig.at[rows], field.at[1, rows], cols_send.at[g], cols_recv.at[g], (row, partner))

    own_cuts = (1, 1, 1, 3)

    def own_span(s, k):
        size = piece // own_cuts[s]
        return pl.ds(k * size, size)

    def own(s, k):
        part = buf.at[s, col, own_span(s, k)]
        return remote(part, part, own_send.at[s, k], own_recv.at[s, k], (row, other))

    def own_arrival(s, k):
        part = buf.at[s, other, own_span(s, k)]
        return remote(part, part, own_send.at[s, k], own_recv.at[s, k], (row, other))

    def send_own(s, ks):
        for k in ks:
            own(s, k).start()

    def relay(s, k):
        return remote(fed.at[s, span(s, k)], buf.at[s, partner, span(s, k)],
                      relay_send.at[s, k], relay_recv.at[s, k], (mate, other))

    def relay_arrival(s, k):
        owner = 3 - partner
        return remote(fed.at[s, span(s, k)], buf.at[s, owner, span(s, k)],
                      relay_send.at[s, k], relay_recv.at[s, k], (mate, other))

    def hand(s, k):
        return remote(fed.at[s, span(s, k)], buf.at[s, partner, span(s, k)],
                      hand_send.at[s, k], hand_recv.at[s, k], (mate, col))

    def result(part, src, target_row):
        rows = (pl.ds(0, W), pl.ds(W, B), pl.ds(low, W))[part]
        return remote(src, out.at[rows], res_send.at[part], res_recv.at[part], (target_row, partner))

    def vectors_of(s, g):
        return split(buf[s, 2 * g:2 * g + 2, :v_rows].reshape(B, W))

    def factor_of(s, g):
        return split(buf[s, 2 * g:2 * g + 2, v_rows:].reshape(W, W))

    def coeffs_of(vectors, factor, rows):
        coupling = product(vectors, split(rows), ((0,), (0,)))
        return split(product(factor, split(coupling), ((1,), (0,))))

    def load(zs, start, size):
        return jnp.concatenate([field[z, start:start + size] for z in zs], axis=1)

    def save(zs, start, value):
        cols = value.shape[1] // len(zs)
        for k, z in enumerate(zs):
            field[z, start:start + value.shape[0]] = value[:, k * cols:(k + 1) * cols]

    def apply_local(s, g, zs, start):
        vectors = vectors_of(s, g)
        rows = load(zs, start, B)
        coeffs = coeffs_of(vectors, factor_of(s, g), rows)
        save(zs, start, rows - product(vectors, coeffs, ((1,), (0,))))

    def up_copy(i, z):
        return remote(field.at[z, pl.ds(0, W)], inb.at[i, z], up_send.at[i, z], up_recv.at[i, z], (up, col))

    def down_copy(z):
        return remote(back.at[0, z], landed.at[z], down_send.at[0, z], down_recv.at[0, z], (down, col))

    def down_final():
        return remote(back.at[1, 0], out.at[pl.ds(0, W)], down_send.at[1, 0], down_recv.at[1, 0], (down, col))

    def send_up(s, zs):
        @pl.when(has_up)
        def _():
            for z in zs:
                up_copy(s // 2, z).start()

    def straddle_body(s, zs, send):
        i = s // 2
        vectors = vectors_of(s, 1)
        below = jnp.concatenate([inb[i, z] for z in zs], axis=1)
        rows = jnp.concatenate([load(zs, low, W), below], axis=0)
        coeffs = coeffs_of(vectors, factor_of(s, 1), rows)
        bottom = (vectors[0][W:], vectors[1][W:])
        value = rows[W:] - product(bottom, coeffs, ((1,), (0,)))
        cols = value.shape[1] // len(zs)
        for k, z in enumerate(zs):
            back[i, z] = value[:, k * cols:(k + 1) * cols]
        send()
        top = (vectors[0][:W], vectors[1][:W])
        save(zs, low, rows[:W] - product(top, coeffs, ((1,), (0,))))

    def straddle(s, zs, send):
        @pl.when(has_down)
        def _():
            for z in zs:
                up_copy(s // 2, z).wait_recv()
            straddle_body(s, zs, send)

    def settle(z):
        @pl.when(has_up)
        def _():
            up_copy(0, z).wait_send()
            down_copy(z).wait_recv()
            field[z, :W] = landed[z]

    def pass_chunk(s, k):
        feed(s, k).wait_recv()
        relay(s, k).start()
        hand(s, k).start()

    def passed(s):
        for k in range(cuts[s]):
            pass_chunk(s, k)

    def near(s):
        for k in range(cuts[s]):
            hand(s, k).wait_recv()

    def far(s):
        for k in range(own_cuts[s]):
            own_arrival(s, k).wait_recv()
        for k in range(cuts[s]):
            relay_arrival(s, k).wait_recv()

    def store(part):
        rows = (pl.ds(0, W), pl.ds(W, B), pl.ds(low, W))[part]
        return pltpu.make_async_copy(field.at[0, rows], out.at[rows], out_sem.at[part])

    def share():
        return remote(buf.at[last, col], buf.at[last, col], share_send, share_recv, (row, partner))

    def share_arrival():
        return remote(buf.at[last, partner], buf.at[last, partner], share_send, share_recv, (row, partner))

    def state(part, start):
        rows = pl.ds(start, W)
        return remote(field.at[1, rows], field.at[0, rows], state_send.at[part], state_recv.at[part], (row, partner))

    def state_up():
        return remote(field.at[1, pl.ds(0, W)], inb.at[1, 0], state_send.at[1], state_recv.at[1], (up, partner))

    def bottom_result():
        return remote(back.at[1, 0], out.at[pl.ds(0, W)], res_send.at[0], res_recv.at[0], (down, col))

    @pl.when(jnp.logical_not(inner))
    def _():
        def turn():
            pl.semaphore_signal(turn_sem, inc=1, device_id=(mate, col), device_id_type=MESH)

        for k in range(last):
            for c in range(cuts[k]):
                feed(k, c).start()
        columns(0).start()

        @pl.when(odd == 0)
        def _():
            pl.semaphore_wait(turn_sem, 1)

        columns(1).start()
        columns(2).start()
        columns(1).wait_send()

        @pl.when(odd == 0)
        def _():
            columns(2).wait_send()

        turn()

        @pl.when(odd == 1)
        def _():
            pl.semaphore_wait(turn_sem, 1)
            columns(2).wait_send()

        for c in range(cuts[last]):
            feed(last, c).start()
        share_arrival().wait_recv()
        state(0, W).wait_recv()

        @pl.when(col == 0)
        def _():
            state(1, W).wait_recv()
            apply_local(last, 0, (0,), W)
            store(1).start()
            result(0, field.at[0, pl.ds(0, W)], row).wait_recv()
            result(2, field.at[0, pl.ds(0, W)], row).wait_recv()
            store(1).wait()

        @pl.when(col == 3)
        def _():
            @pl.when(has_down)
            def _():
                state_up().wait_recv()
                straddle_body(last, (0,), lambda: bottom_result().start())

            store(2).start()
            result(0, field.at[0, pl.ds(0, W)], row).wait_recv()
            result(1, field.at[0, pl.ds(0, B)], row).wait_recv()
            store(2).wait()

            @pl.when(has_down)
            def _():
                bottom_result().wait_send()

        for s in range(steps):
            for k in range(cuts[s]):
                feed(s, k).wait_send()
        columns(0).wait_send()

    early = jnp.logical_not(own_first)

    @pl.when(inner)
    def _():
        send_own(0, (0,))
        share().start()
        passed(0)
        send_own(1, (0,))
        eig_load.wait()
        near(0)

        @pl.when(col == 1)
        def _():
            apply_local(0, 0, (0,), 0)
            send_up(0, (0,))

        @pl.when(col == 2)
        def _():
            apply_local(0, 1, (0,), B)

        passed(1)

        @pl.when(own_first)
        def _():
            send_own(2, (0,))

        far(0)
        near(1)

        @pl.when(col == 1)
        def _():
            apply_local(0, 1, (0,), B)
            apply_local(1, 0, (0,), W)

        @pl.when(col == 2)
        def _():
            apply_local(0, 0, (0,), 0)
            send_up(0, (0,))
            straddle(1, (0,), lambda: down_copy(0).start())

        passed(2)

        @pl.when(own_first)
        def _():
            send_own(3, (0, 1, 2))

        @pl.when(early)
        def _():
            send_own(2, (0,))
            send_own(3, (0,))

        far(1)

        @pl.when(col == 1)
        def _():
            straddle(1, (0,), lambda: down_copy(0).start())

        @pl.when(col == 2)
        def _():
            apply_local(1, 0, (0,), W)

        columns(0).wait_recv()
        apply_local(0, 0, (1,), 0)
        send_up(0, (1,))
        settle(0)
        near(2)

        @pl.when(col == 1)
        def _():
            apply_local(2, 0, (0,), 0)
            send_up(2, (0,))

        @pl.when(col == 2)
        def _():
            apply_local(2, 1, (0,), B)

        def far_even():
            @pl.when(col == 1)
            def _():
                apply_local(2, 1, (0,), B)

            @pl.when(col == 2)
            def _():
                apply_local(2, 0, (0,), 0)
                send_up(2, (0,))

        @pl.when(early)
        def _():
            far(2)
            far_even()

        columns(1).wait_recv()
        columns(2).wait_recv()
        apply_local(0, 1, (1,), B)
        straddle(1, (1,), lambda: down_copy(1).start())

        @pl.when(odd == 0)
        def _():
            pass_chunk(3, 0)

        apply_local(1, 0, (1,), W)

        @pl.when(col == 2)
        def _():
            apply_local(2, 1, (1,), B)
            state(0, low).start()

        @pl.when(own_first)
        def _():
            far(2)

        @pl.when(col == 1)
        def _():
            apply_local(2, 1, (1,), B)
            state(0, B).start()


        @pl.when(odd == 1)
        def _():
            pass_chunk(3, 0)

        pass_chunk(3, 1)
        settle(1)
        apply_local(2, 0, (1,), 0)

        @pl.when(col == 1)
        def _():
            state(1, W).start()
            send_up(2, (1,))

        @pl.when((col == 2) & has_up)
        def _():
            state_up().start()

        pass_chunk(3, 2)

        @pl.when(early)
        def _():
            send_own(3, (1, 2))


        @pl.when(own_first)
        def _():
            far_even()

        @pl.when(jnp.logical_not(has_up))
        def _():
            result(0, field.at[1, pl.ds(0, W)], row).start()
            store(0).start()

        near(3)

        @pl.when(col == 1)
        def _():
            apply_local(last, 0, (0,), W)
            store(1).start()

            far(3)
            straddle(last, (1,), lambda: result(0, back.at[1, 1], down).start())
            result(2, field.at[1, pl.ds(low, W)], row).start()
            straddle(last, (0,), lambda: down_final().start())
            store(2).start()

        @pl.when(col == 2)
        def _():
            straddle(last, (0,), lambda: down_final().start())
            store(2).start()
            far(3)
            apply_local(last, 0, (1,), W)
            result(1, field.at[1, pl.ds(W, B)], row).start()
            apply_local(last, 0, (0,), W)
            store(1).start()

        share().wait_send()
        state(0, W).wait_send()
        for s in range(steps):
            for k in range(own_cuts[s]):
                own(s, k).wait_send()
            for k in range(cuts[s]):
                relay(s, k).wait_send()
                hand(s, k).wait_send()

        @pl.when(has_up)
        def _():
            up_copy(last // 2, 0).wait_send()
            down_final().wait_recv()

        @pl.when(has_down)
        def _():
            down_copy(0).wait_send()
            down_copy(1).wait_send()
            down_final().wait_send()

        @pl.when(jnp.logical_not(has_up))
        def _():
            result(0, field.at[1, pl.ds(0, W)], row).wait_send()
            store(0).wait()

        @pl.when(col == 1)
        def _():
            state(1, W).wait_send()

            @pl.when(has_up)
            def _():
                up_copy(last // 2, 1).wait_send()

            @pl.when(has_down)
            def _():
                result(0, back.at[1, 1], down).wait_send()

            result(2, field.at[1, pl.ds(low, W)], row).wait_send()

        @pl.when(col == 2)
        def _():
            @pl.when(has_up)
            def _():
                state_up().wait_send()

            result(1, field.at[1, pl.ds(W, B)], row).wait_send()

        store(1).wait()
        store(2).wait()


def on_device(n, rows_n, eigvec, refl, tfac, sched):
    steps, v_rows, _ = refl.shape
    t_rows = tfac.shape[1]
    groups = sched.shape[0]
    evcount = eigvec.shape[1]
    piece = v_rows + t_rows
    hops = n // 2
    half_steps = steps // 2
    anywhere = pl.BlockSpec(memory_space=pl.ANY)
    if n == 4 and groups == 2 and steps == 4 and rows_n % 2 == 0:
        two = (half_steps, 2)
        chunks = (steps, 3)
        dma = pltpu.SemaphoreType.DMA
        return pl.pallas_call(
            functools.partial(line_kernel, rows_n),
            out_shape=pltpu.VMEM(eigvec.shape, jnp.float32),
            in_specs=[anywhere, anywhere, anywhere, anywhere],
            out_specs=anywhere,
            scratch_shapes=[
                pltpu.SMEM(sched.shape, jnp.int32),
                pltpu.VMEM(refl.shape, jnp.float32),
                pltpu.VMEM(tfac.shape, jnp.float32),
                pltpu.VMEM((2, *eigvec.shape), jnp.float32),
                pltpu.VMEM((steps, n, piece, W), jnp.float32),
                pltpu.VMEM((steps, piece, W), jnp.float32),
                pltpu.VMEM((*two, W, evcount), jnp.float32),
                pltpu.VMEM((*two, W, evcount), jnp.float32),
                pltpu.VMEM((2, W, evcount), jnp.float32),
                dma((3,)),
                dma,
                dma((3,)),
                dma(chunks),
                dma(chunks),
                dma((3,)),
                dma((3,)),
                dma(chunks),
                dma(chunks),
                dma(chunks),
                dma(chunks),
                dma(chunks),
                dma(chunks),
                dma(two),
                dma(two),
                dma(two),
                dma(two),
                dma((3,)),
                dma((3,)),
                dma,
                dma,
                dma((2,)),
                dma((2,)),
                pltpu.SemaphoreType.REGULAR,
            ],
            compiler_params=pltpu.CompilerParams(
                collective_id=0, has_side_effects=True, vmem_limit_bytes=60 << 20
            ),
            name="sweep",
        )(sched, refl, tfac, eigvec)
    owner = lax.axis_index("col") * v_rows // B
    slots = lax.dynamic_index_in_dim(sched, owner, 0, keepdims=False)
    packed = pl.pallas_call(
        pick_kernel,
        out_shape=jax.ShapeDtypeStruct((steps, piece, W), jnp.float32),
        in_specs=[pl.BlockSpec(memory_space=pltpu.SMEM), anywhere, anywhere],
        out_specs=anywhere,
        scratch_shapes=[
            pltpu.VMEM((steps, piece, W), jnp.float32),
            pltpu.SemaphoreType.DMA((steps, 2)),
            pltpu.SemaphoreType.DMA((steps,)),
        ],
        name="pick",
    )(slots, refl, tfac)
    return pl.pallas_call(
        functools.partial(main_kernel, n, rows_n, groups),
        out_shape=jax.ShapeDtypeStruct(eigvec.shape, jnp.float32),
        in_specs=[anywhere, anywhere],
        out_specs=anywhere,
        scratch_shapes=[
            pltpu.VMEM(eigvec.shape, jnp.float32),
            pltpu.VMEM((steps, n, piece, W), jnp.float32),
            pltpu.VMEM((half_steps, W, evcount), jnp.float32),
            pltpu.VMEM((half_steps, W, evcount), jnp.float32),
            pltpu.VMEM((half_steps, W, evcount), jnp.float32),
            pltpu.SemaphoreType.DMA((steps,)),
            pltpu.SemaphoreType.DMA,
            pltpu.SemaphoreType.DMA,
            pltpu.SemaphoreType.DMA((steps, 2, hops, 2)),
            pltpu.SemaphoreType.DMA((steps, 2, hops, 2)),
            pltpu.SemaphoreType.DMA((half_steps,)),
            pltpu.SemaphoreType.DMA((half_steps,)),
            pltpu.SemaphoreType.DMA((half_steps,)),
            pltpu.SemaphoreType.DMA((half_steps,)),
        ],
        compiler_params=pltpu.CompilerParams(
            collective_id=0, has_side_effects=True, vmem_limit_bytes=48 << 20
        ),
        name="sweep",
    )(packed, eigvec)


def solution(mesh):
    placed = (
        P("row", "col"),
        P(None, ("row", "col"), None),
        P(None, ("row", "col"), None),
        P("row", None),
    )
    body = functools.partial(on_device, mesh.shape["col"], mesh.shape["row"])
    return jax.shard_map(body, mesh=mesh, in_specs=placed, out_specs=P("row", "col"), check_vma=False)
```

```python
import functools

import jax
import jax.numpy as jnp
from jax import lax
from jax.experimental import pallas as pl
from jax.experimental.pallas import tpu as pltpu
from jax.sharding import PartitionSpec as P

B = 512
W = 256
MESH = pl.DeviceIdType.MESH


def split(x):
    high = x.astype(jnp.bfloat16)
    low = (x - high.astype(jnp.float32)).astype(jnp.bfloat16)
    return high, low


def product(left, right, dims):
    def one(a, b):
        return lax.dot_general(a, b, (dims, ((), ())), preferred_element_type=jnp.float32)

    return one(left[0], right[0]) + (one(left[0], right[1]) + one(left[1], right[0]))


def pick_kernel(slots, refl, tfac, packed, hold, in_sem, out_sem):
    steps = packed.shape[0]
    v_rows = refl.shape[1]
    t_rows = tfac.shape[1]
    loads, stores = [], []
    for s in range(steps):
        slot = slots[s]
        loads.append(
            (
                pltpu.make_async_copy(refl.at[slot], hold.at[s, pl.ds(0, v_rows)], in_sem.at[s, 0]),
                pltpu.make_async_copy(tfac.at[slot], hold.at[s, pl.ds(v_rows, t_rows)], in_sem.at[s, 1]),
            )
        )
        stores.append(pltpu.make_async_copy(hold.at[s], packed.at[s], out_sem.at[s]))
    for pair in loads:
        for copy in pair:
            copy.start()
    for pair, store in zip(loads, stores):
        for copy in pair:
            copy.wait()
        store.start()
    for store in stores:
        store.wait()


def main_kernel(n, rows_n, groups, packed, eig, out, field, buf, inb, back, landed, own_sem, eig_sem, out_sem,
                ring_send, ring_recv, up_send, up_recv, down_send, down_recv):
    steps, piece, _ = packed.shape
    v_rows = groups * B // n
    per_group = n // groups
    half = piece // 2
    hops = n // 2
    row = lax.axis_index("row")
    col = lax.axis_index("col")
    right = lax.rem(col + 1, n)
    left = lax.rem(col + n - 1, n)
    has_down = row < rows_n - 1
    has_up = row > 0
    down = jnp.minimum(row + 1, rows_n - 1)
    up = jnp.maximum(row - 1, 0)

    eig_copy = pltpu.make_async_copy(eig, field, eig_sem)
    eig_copy.start()

    barrier = pltpu.get_barrier_semaphore()
    pl.semaphore_signal(barrier, inc=1, device_id=(row, left), device_id_type=MESH)
    pl.semaphore_signal(barrier, inc=1, device_id=(row, right), device_id_type=MESH)

    @pl.when(has_up)
    def _():
        pl.semaphore_signal(barrier, inc=1, device_id=(up, col), device_id_type=MESH)

    @pl.when(has_down)
    def _():
        pl.semaphore_signal(barrier, inc=1, device_id=(down, col), device_id_type=MESH)

    pl.semaphore_wait(barrier, 2 + jnp.minimum(row, 1) + jnp.minimum(rows_n - 1 - row, 1))

    def ring_copy(s, way, hop, part):
        target = right if way == 0 else left
        owner = lax.rem(col + n - hop, n) if way == 0 else lax.rem(col + hop, n)
        span = pl.ds(part * half, half)
        src = packed.at[s, span] if hop == 0 else buf.at[s, owner, span]
        return pltpu.make_async_remote_copy(
            src_ref=src,
            dst_ref=buf.at[s, owner, span],
            send_sem=ring_send.at[s, way, hop, part],
            recv_sem=ring_recv.at[s, way, hop, part],
            device_id=(row, target),
            device_id_type=MESH,
        )

    def parts_of(way, hop):
        order = (0, 1) if way == 0 else (1, 0)
        return order[:1] if hop == hops - 1 else order

    def send_own(s):
        for k in range(len(parts_of(0, 0))):
            for way in (0, 1):
                ring_copy(s, way, 0, parts_of(way, 0)[k]).start()

    def forward(s):
        for hop in range(1, hops):
            for k in range(len(parts_of(0, hop))):
                for way in (0, 1):
                    part = parts_of(way, hop)[k]
                    ring_copy(s, way, hop - 1, part).wait_recv()
                    ring_copy(s, way, hop, part).start()

    def finish(s):
        for hop in range(hops):
            for way in (0, 1):
                done = parts_of(way, hop + 1) if hop + 1 < hops else ()
                for part in parts_of(way, hop):
                    if part not in done:
                        ring_copy(s, way, hop, part).wait_recv()

    def vectors_of(s, g):
        block = buf[s, g * per_group:(g + 1) * per_group, :v_rows]
        return split(block.reshape(B, W))

    def factor_of(s, g):
        block = buf[s, g * per_group:(g + 1) * per_group, v_rows:]
        return split(block.reshape(W, W))

    def coeffs_of(s, g, vectors, rows):
        coupling = product(vectors, split(rows), ((0,), (0,)))
        return split(product(factor_of(s, g), split(coupling), ((1,), (0,))))

    def apply_local(s, g, start):
        vectors = vectors_of(s, g)
        rows = field[start:start + B]
        coeffs = coeffs_of(s, g, vectors, rows)
        field[start:start + B] = rows - product(vectors, coeffs, ((1,), (0,)))

    def up_copy(i):
        return pltpu.make_async_remote_copy(
            src_ref=field.at[pl.ds(0, W)], dst_ref=inb.at[i],
            send_sem=up_send.at[i], recv_sem=up_recv.at[i],
            device_id=(up, col), device_id_type=MESH,
        )

    def down_copy(i):
        return pltpu.make_async_remote_copy(
            src_ref=back.at[i], dst_ref=landed.at[i],
            send_sem=down_send.at[i], recv_sem=down_recv.at[i],
            device_id=(down, col), device_id_type=MESH,
        )

    low = groups * B - W

    send_own(0)
    own = [pltpu.make_async_copy(packed.at[s], buf.at[s, col], own_sem.at[s]) for s in range(steps)]
    for copy in own:
        copy.start()
    eig_copy.wait()
    for s in range(steps):
        forward(s)
        if s + 1 < steps:
            send_own(s + 1)
        own[s].wait()
        finish(s)
        i = s // 2
        if s % 2 == 0:
            for g in range(groups):
                apply_local(s, g, g * B)
                if g == 0 and s + 1 < steps:
                    @pl.when(has_up)
                    def _():
                        up_copy(i).start()
        else:
            @pl.when(has_down)
            def _():
                up_copy(i).wait_recv()
                g = groups - 1
                vectors = vectors_of(s, g)
                rows = jnp.concatenate([field[low:], inb[i]], axis=0)
                coeffs = coeffs_of(s, g, vectors, rows)
                bottom = (vectors[0][W:], vectors[1][W:])
                back[i] = rows[W:] - product(bottom, coeffs, ((1,), (0,)))
                down_copy(i).start()
                top = (vectors[0][:W], vectors[1][:W])
                field[low:] = rows[:W] - product(top, coeffs, ((1,), (0,)))

            for g in range(groups - 1):
                apply_local(s, g, W + g * B)

            @pl.when(has_up)
            def _():
                up_copy(i).wait_send()
                down_copy(i).wait_recv()
                field[:W] = landed[i]

    store = pltpu.make_async_copy(field, out, out_sem)
    store.start()
    for s in range(steps):
        for way in (0, 1):
            for hop in range(hops):
                for part in parts_of(way, hop):
                    ring_copy(s, way, hop, part).wait_send()

    @pl.when(has_down)
    def _():
        for i in range(steps // 2):
            down_copy(i).wait_send()

    store.wait()


def line_kernel(rows_n, sched_all, refl, tfac, eig, out, sched, refl_in, tfac_in, field, buf, fed, inb, back, landed,
                local, eig_sem, sends, recvs, turn_sem):
    steps, v_rows, _ = refl.shape
    low = B + W
    last = steps - 1
    row = lax.axis_index("row")
    col = lax.axis_index("col")
    odd = lax.rem(row, 2)
    inner = (col == 1) | (col == 2)
    partner = col + 1 - 2 * lax.rem(col, 2)
    other = 3 - col
    mate = row + 1 - 2 * odd
    beyond = row - 1 + 2 * odd
    has_beyond = (beyond >= 0) & (beyond < rows_n)
    beyond = jnp.clip(beyond, 0, rows_n - 1)
    own_first = (col == 1) == (odd == 0)
    has_down = row < rows_n - 1
    has_up = row > 0
    down = jnp.minimum(row + 1, rows_n - 1)
    up = jnp.maximum(row - 1, 0)

    def remote(src, dst, send, recv, target):
        return pltpu.make_async_remote_copy(
            src_ref=src, dst_ref=dst, send_sem=send, recv_sem=recv,
            device_id=target, device_id_type=MESH,
        )

    refl_load = pltpu.make_async_copy(refl, refl_in, local.at[0])
    tfac_load = pltpu.make_async_copy(tfac, tfac_in, local.at[1])
    eig_load = pltpu.make_async_copy(eig, field.at[0], eig_sem)
    sched_load = pltpu.make_async_copy(sched_all, sched, local.at[2])
    sched_load.start()
    refl_load.start()
    tfac_load.start()

    barrier = pltpu.get_barrier_semaphore()

    def greet(target):
        pl.semaphore_signal(barrier, inc=1, device_id=target, device_id_type=MESH)

    greet((row, partner))
    greet((mate, partner))
    greet((mate, col))

    @pl.when(has_beyond)
    def _():
        greet((beyond, col))
        greet((beyond, partner))

    @pl.when(inner)
    def _():
        greet((row, other))
        greet((mate, other))

    sched_load.wait()
    refl_load.wait()
    tfac_load.wait()

    @pl.when(inner)
    def _():
        eig_load.start()

    for s in range(steps):
        slot = sched[col // 2, s]
        buf[s, col, :v_rows] = refl_in[slot]
        buf[s, col, v_rows:] = tfac_in[slot]

    pl.semaphore_wait(barrier, 3 + 2 * has_beyond.astype(jnp.int32) + 2 * inner.astype(jnp.int32))

    cuts = (3, 1, 1, 3)
    piece = buf.shape[2]

    def span(s, k):
        size = piece // cuts[s]
        return pl.ds(k * size, size)

    def feed(s, k):
        slot = sum(cuts[:s]) + k
        return remote(buf.at[s, col, span(s, k)], fed.at[s, span(s, k)],
                      sends.at[1 + k if s == last else 0], recvs.at[slot], (mate, partner))

    def feeds():
        return remote(buf.at[pl.ds(0, last), col], fed.at[pl.ds(0, last)], sends.at[0], recvs.at[0], (mate, partner))

    column_rows = ((0, B), (B, W), (B + W, W))

    def columns(g):
        rows = pl.ds(*column_rows[g])
        return remote(eig.at[rows], field.at[1, rows], sends.at[4 + g], recvs.at[8 + g], (row, partner))

    def own(s):
        return remote(buf.at[s, col], buf.at[s, col], sends.at[0], recvs.at[11 + s], (row, other))

    def own_arrival(s):
        return remote(buf.at[s, other], buf.at[s, other], sends.at[0], recvs.at[11 + s], (row, other))

    def own_all():
        return remote(buf.at[:, col], buf.at[:, col], sends.at[0], recvs.at[11], (row, other))

    def relay(s, k):
        return remote(fed.at[s, span(s, k)], buf.at[s, partner, span(s, k)],
                      sends.at[1], recvs.at[15 + s], (mate, other))

    def relay_arrival(s):
        return remote(fed.at[s], buf.at[s, 3 - partner], sends.at[1], recvs.at[15 + s], (mate, other))

    def relay_all():
        return remote(fed, buf.at[:, partner], sends.at[1], recvs.at[15], (mate, other))

    def hand(s, k):
        return remote(fed.at[s, span(s, k)], buf.at[s, partner, span(s, k)],
                      sends.at[2], recvs.at[19 + s], (mate, col))

    def hand_arrival(s):
        return remote(fed.at[s], buf.at[s, partner], sends.at[2], recvs.at[19 + s], (mate, col))

    def hand_all():
        return remote(fed, buf.at[:, partner], sends.at[2], recvs.at[19], (mate, col))

    def result(part, src, target_row):
        rows = (pl.ds(0, W), pl.ds(W, B), pl.ds(low, W))[part]
        return remote(src, out.at[rows], sends.at[10 + part], recvs.at[5 + part], (target_row, partner))

    def vectors_of(s, g):
        return split(buf[s, 2 * g:2 * g + 2, :v_rows].reshape(B, W))

    def factor_of(s, g):
        return split(buf[s, 2 * g:2 * g + 2, v_rows:].reshape(W, W))

    def coeffs_of(vectors, factor, rows):
        coupling = product(vectors, split(rows), ((0,), (0,)))
        return split(product(factor, split(coupling), ((1,), (0,))))

    def load(zs, start, size):
        return jnp.concatenate([field[z, start:start + size] for z in zs], axis=1)

    def save(zs, start, value):
        cols = value.shape[1] // len(zs)
        for k, z in enumerate(zs):
            field[z, start:start + value.shape[0]] = value[:, k * cols:(k + 1) * cols]

    def apply_local(s, g, zs, start):
        vectors = vectors_of(s, g)
        rows = load(zs, start, B)
        coeffs = coeffs_of(vectors, factor_of(s, g), rows)
        save(zs, start, rows - product(vectors, coeffs, ((1,), (0,))))

    def up_copy(i, z):
        return remote(field.at[z, pl.ds(0, W)], inb.at[i, z], sends.at[3 + 2 * i + z], recvs.at[23 + 2 * i + z], (up, col))

    def down_copy(z):
        return remote(back.at[0, z], landed.at[z], sends.at[7 + z], recvs.at[27 + z], (down, col))

    def down_final():
        return remote(back.at[1, 0], out.at[pl.ds(0, W)], sends.at[9], recvs.at[29], (down, col))

    def send_up(s, zs):
        @pl.when(has_up)
        def _():
            for z in zs:
                up_copy(s // 2, z).start()

    def straddle_body(s, zs, send):
        i = s // 2
        vectors = vectors_of(s, 1)
        below = jnp.concatenate([inb[i, z] for z in zs], axis=1)
        rows = jnp.concatenate([load(zs, low, W), below], axis=0)
        coeffs = coeffs_of(vectors, factor_of(s, 1), rows)
        bottom = (vectors[0][W:], vectors[1][W:])
        value = rows[W:] - product(bottom, coeffs, ((1,), (0,)))
        cols = value.shape[1] // len(zs)
        for k, z in enumerate(zs):
            back[i, z] = value[:, k * cols:(k + 1) * cols]
        send()
        top = (vectors[0][:W], vectors[1][:W])
        save(zs, low, rows[:W] - product(top, coeffs, ((1,), (0,))))

    def straddle(s, zs, send):
        @pl.when(has_down)
        def _():
            for z in zs:
                up_copy(s // 2, z).wait_recv()
            straddle_body(s, zs, send)

    def settle(z):
        @pl.when(has_up)
        def _():
            up_copy(0, z).wait_send()
            down_copy(z).wait_recv()
            field[z, :W] = landed[z]

    def pass_chunk(s, k):
        feed(s, k).wait_recv()
        relay(s, k).start()
        hand(s, k).start()

    def passed(s):
        for k in range(cuts[s]):
            pass_chunk(s, k)

    def near(s):
        hand_arrival(s).wait_recv()

    def far(s):
        own_arrival(s).wait_recv()
        relay_arrival(s).wait_recv()

    def store(part):
        rows = (pl.ds(0, W), pl.ds(W, B), pl.ds(low, W))[part]
        return pltpu.make_async_copy(field.at[0, rows], out.at[rows], local.at[part])

    top_row = (col < 2) & (row == 0)
    share_slot = {last: 0, 0: 1, 2: 2}

    def share(s):
        part = buf.at[s, col]
        return remote(part, part, sends.at[13 + share_slot[s]], recvs.at[share_slot[s]], (row, partner))

    def share_arrival(s):
        part = buf.at[s, partner]
        return remote(part, part, sends.at[13 + share_slot[s]], recvs.at[share_slot[s]], (row, partner))

    def state(part, start):
        rows = pl.ds(start, W)
        return remote(field.at[1, rows], field.at[0, rows], sends.at[16 + part], recvs.at[3 + part], (row, partner))

    def state_up():
        return remote(field.at[1, pl.ds(0, W)], inb.at[1, 0], sends.at[17], recvs.at[4], (up, partner))

    def bottom_result():
        return remote(back.at[1, 0], out.at[pl.ds(0, W)], sends.at[10], recvs.at[5], (down, col))

    @pl.when(jnp.logical_not(inner))
    def _():
        def turn():
            pl.semaphore_signal(turn_sem, inc=1, device_id=(mate, col), device_id_type=MESH)

        for k in range(last):
            for c in range(cuts[k]):
                feed(k, c).start()
        columns(0).start()

        def wait_turn():
            pl.semaphore_wait(turn_sem, 1)

        def last_feed():
            for c in range(cuts[last]):
                feed(last, c).start()

        feeds_first = (col == 0) == (odd == 0)

        @pl.when(odd == 0)
        def _():
            wait_turn()

        columns(1).start()
        columns(2).start()
        columns(1).wait_send()

        @pl.when(odd == 1)
        def _():
            turn()

            @pl.when(feeds_first)
            def _():
                wait_turn()

            columns(2).wait_send()

        @pl.when(odd == 0)
        def _():
            @pl.when(feeds_first)
            def _():
                last_feed()

            columns(2).wait_send()

            @pl.when(jnp.logical_not(feeds_first))
            def _():
                turn()

        @pl.when(feeds_first)
        def _():
            @pl.when(odd == 1)
            def _():
                last_feed()

            feed(last, 1).wait_send()
            turn()
            feed(last, 0).wait_send()
            feed(last, 2).wait_send()

        @pl.when(jnp.logical_not(feeds_first))
        def _():
            wait_turn()
            last_feed()
            for c in range(cuts[last]):
                feed(last, c).wait_send()

        share_arrival(last).wait_recv()

        @pl.when(top_row)
        def _():
            share_arrival(0).wait_recv()
            share_arrival(2).wait_recv()
            top_load = pltpu.make_async_copy(eig.at[pl.ds(0, B)], field.at[1, pl.ds(0, B)], eig_sem)
            top_load.start()
            top_load.wait()
            apply_local(0, 0, (1,), 0)
            field[0, :W] = field[1, :W]
            state(1, W).wait_recv()
            apply_local(2, 0, (0,), 0)
            store(0).start()

        state(0, W).wait_recv()

        @pl.when(col == 0)
        def _():
            @pl.when(has_up)
            def _():
                state(1, W).wait_recv()

            apply_local(last, 0, (0,), W)
            store(1).start()

            @pl.when(has_up)
            def _():
                result(0, field.at[0, pl.ds(0, W)], row).wait_recv()

            @pl.when(jnp.logical_not(has_up))
            def _():
                store(0).wait()

            result(2, field.at[0, pl.ds(0, W)], row).wait_recv()
            store(1).wait()

        @pl.when(col == 3)
        def _():
            @pl.when(has_down)
            def _():
                state_up().wait_recv()
                straddle_body(last, (0,), lambda: bottom_result().start())

            store(2).start()
            result(0, field.at[0, pl.ds(0, W)], row).wait_recv()
            result(1, field.at[0, pl.ds(0, B)], row).wait_recv()
            store(2).wait()

            @pl.when(has_down)
            def _():
                bottom_result().wait_send()

        feeds().wait_send()
        columns(0).wait_send()

    early = jnp.logical_not(own_first)

    @pl.when(inner)
    def _():
        own(0).start()
        passed(0)
        own(1).start()
        eig_load.wait()
        near(0)

        @pl.when(col == 1)
        def _():
            apply_local(0, 0, (0,), 0)
            send_up(0, (0,))

        @pl.when(col == 2)
        def _():
            apply_local(0, 1, (0,), B)

        passed(1)
        share(last).start()

        @pl.when(top_row)
        def _():
            share(0).start()
            share(2).start()


        @pl.when(own_first)
        def _():
            own(2).start()

        far(0)
        near(1)

        @pl.when(col == 1)
        def _():
            apply_local(0, 1, (0,), B)
            apply_local(1, 0, (0,), W)

        @pl.when(col == 2)
        def _():
            apply_local(0, 0, (0,), 0)
            send_up(0, (0,))
            straddle(1, (0,), lambda: down_copy(0).start())

        passed(2)

        @pl.when(own_first)
        def _():
            own(3).start()

        @pl.when(early)
        def _():
            own(2).start()

        far(1)

        @pl.when(col == 1)
        def _():
            straddle(1, (0,), lambda: down_copy(0).start())

        @pl.when(col == 2)
        def _():
            apply_local(1, 0, (0,), W)

        columns(0).wait_recv()
        apply_local(0, 0, (1,), 0)
        send_up(0, (1,))
        settle(0)
        near(2)

        @pl.when(col == 1)
        def _():
            apply_local(2, 0, (0,), 0)
            send_up(2, (0,))

        @pl.when(col == 2)
        def _():
            apply_local(2, 1, (0,), B)

        def far_even():
            @pl.when(col == 1)
            def _():
                apply_local(2, 1, (0,), B)

            @pl.when(col == 2)
            def _():
                apply_local(2, 0, (0,), 0)
                send_up(2, (0,))

        @pl.when(early)
        def _():
            far(2)
            far_even()

        columns(1).wait_recv()
        columns(2).wait_recv()
        apply_local(0, 1, (1,), B)
        straddle(1, (1,), lambda: down_copy(1).start())

        @pl.when(early & (odd == 0))
        def _():
            pass_chunk(3, 0)

        apply_local(1, 0, (1,), W)

        @pl.when(top_row)
        def _():
            state(1, W).start()

        @pl.when(early & (odd == 1))
        def _():
            pass_chunk(3, 0)

        @pl.when(early & (odd == 0))
        def _():
            pass_chunk(3, 1)

        @pl.when(col == 2)
        def _():
            apply_local(2, 1, (1,), B)
            state(0, low).start()

        @pl.when(own_first)
        def _():
            far(2)

        @pl.when(col == 1)
        def _():
            apply_local(2, 1, (1,), B)
            state(0, B).start()


        @pl.when(early & (odd == 1))
        def _():
            pass_chunk(3, 1)

        settle(1)

        @pl.when(early)
        def _():
            pass_chunk(3, 2)
            own(3).start()

        @pl.when(jnp.logical_not(top_row))
        def _():
            apply_local(2, 0, (1,), 0)

        @pl.when((col == 1) & has_up)
        def _():
            state(1, W).start()
            up_copy(1, 1).start()

        @pl.when((col == 2) & has_up)
        def _():
            state_up().start()


        @pl.when(own_first)
        def _():
            passed(3)


        @pl.when(own_first)
        def _():
            far_even()

        @pl.when(jnp.logical_not(has_up))
        def _():
            store(0).start()

        @pl.when((col == 2) & jnp.logical_not(has_up))
        def _():
            result(0, field.at[1, pl.ds(0, W)], row).start()

        def near_last():
            near(3)

            @pl.when(col == 1)
            def _():
                apply_local(last, 0, (0,), W)
                store(1).start()

            @pl.when(col == 2)
            def _():
                straddle(last, (0,), lambda: down_final().start())
                store(2).start()

        @pl.when(own_first)
        def _():
            near_last()

        far(3)

        @pl.when(col == 1)
        def _():
            straddle(last, (1,), lambda: result(0, back.at[1, 1], down).start())
            result(2, field.at[1, pl.ds(low, W)], row).start()

        @pl.when(col == 2)
        def _():
            apply_local(last, 0, (1,), W)
            result(1, field.at[1, pl.ds(W, B)], row).start()

        @pl.when(early)
        def _():
            near_last()

        @pl.when(col == 1)
        def _():
            straddle(last, (0,), lambda: down_final().start())
            store(2).start()

        @pl.when(col == 2)
        def _():
            apply_local(last, 0, (0,), W)
            store(1).start()

        share(last).wait_send()

        @pl.when(top_row)
        def _():
            share(0).wait_send()
            share(2).wait_send()

        state(0, W).wait_send()
        own_all().wait_send()
        relay_all().wait_send()
        hand_all().wait_send()

        @pl.when(has_up)
        def _():
            up_copy(last // 2, 0).wait_send()
            down_final().wait_recv()

        @pl.when(has_down)
        def _():
            down_copy(0).wait_send()
            down_copy(1).wait_send()
            down_final().wait_send()

        @pl.when(jnp.logical_not(has_up))
        def _():
            store(0).wait()

        @pl.when(col == 1)
        def _():
            state(1, W).wait_send()

            @pl.when(has_up)
            def _():
                up_copy(last // 2, 1).wait_send()

            @pl.when(has_down)
            def _():
                result(0, back.at[1, 1], down).wait_send()

            result(2, field.at[1, pl.ds(low, W)], row).wait_send()

        @pl.when(col == 2)
        def _():
            @pl.when(has_up)
            def _():
                state_up().wait_send()

            @pl.when(jnp.logical_not(has_up))
            def _():
                result(0, field.at[1, pl.ds(0, W)], row).wait_send()

            result(1, field.at[1, pl.ds(W, B)], row).wait_send()

        store(1).wait()
        store(2).wait()


def on_device(n, rows_n, eigvec, refl, tfac, sched):
    steps, v_rows, _ = refl.shape
    t_rows = tfac.shape[1]
    groups = sched.shape[0]
    evcount = eigvec.shape[1]
    piece = v_rows + t_rows
    hops = n // 2
    half_steps = steps // 2
    anywhere = pl.BlockSpec(memory_space=pl.ANY)
    if n == 4 and groups == 2 and steps == 4 and rows_n % 2 == 0:
        two = (half_steps, 2)
        dma = pltpu.SemaphoreType.DMA
        return pl.pallas_call(
            functools.partial(line_kernel, rows_n),
            out_shape=pltpu.VMEM(eigvec.shape, jnp.float32),
            in_specs=[anywhere, anywhere, anywhere, anywhere],
            out_specs=anywhere,
            scratch_shapes=[
                pltpu.SMEM(sched.shape, jnp.int32),
                pltpu.VMEM(refl.shape, jnp.float32),
                pltpu.VMEM(tfac.shape, jnp.float32),
                pltpu.VMEM((2, *eigvec.shape), jnp.float32),
                pltpu.VMEM((steps, n, piece, W), jnp.float32),
                pltpu.VMEM((steps, piece, W), jnp.float32),
                pltpu.VMEM((*two, W, evcount), jnp.float32),
                pltpu.VMEM((*two, W, evcount), jnp.float32),
                pltpu.VMEM((2, W, evcount), jnp.float32),
                dma((3,)),
                dma,
                dma((18,)),
                dma((30,)),
                pltpu.SemaphoreType.REGULAR,
            ],
            compiler_params=pltpu.CompilerParams(
                collective_id=0, has_side_effects=True, vmem_limit_bytes=60 << 20
            ),
            name="sweep",
        )(sched, refl, tfac, eigvec)
    owner = lax.axis_index("col") * v_rows // B
    slots = lax.dynamic_index_in_dim(sched, owner, 0, keepdims=False)
    packed = pl.pallas_call(
        pick_kernel,
        out_shape=jax.ShapeDtypeStruct((steps, piece, W), jnp.float32),
        in_specs=[pl.BlockSpec(memory_space=pltpu.SMEM), anywhere, anywhere],
        out_specs=anywhere,
        scratch_shapes=[
            pltpu.VMEM((steps, piece, W), jnp.float32),
            pltpu.SemaphoreType.DMA((steps, 2)),
            pltpu.SemaphoreType.DMA((steps,)),
        ],
        name="pick",
    )(slots, refl, tfac)
    return pl.pallas_call(
        functools.partial(main_kernel, n, rows_n, groups),
        out_shape=jax.ShapeDtypeStruct(eigvec.shape, jnp.float32),
        in_specs=[anywhere, anywhere],
        out_specs=anywhere,
        scratch_shapes=[
            pltpu.VMEM(eigvec.shape, jnp.float32),
            pltpu.VMEM((steps, n, piece, W), jnp.float32),
            pltpu.VMEM((half_steps, W, evcount), jnp.float32),
            pltpu.VMEM((half_steps, W, evcount), jnp.float32),
            pltpu.VMEM((half_steps, W, evcount), jnp.float32),
            pltpu.SemaphoreType.DMA((steps,)),
            pltpu.SemaphoreType.DMA,
            pltpu.SemaphoreType.DMA,
            pltpu.SemaphoreType.DMA((steps, 2, hops, 2)),
            pltpu.SemaphoreType.DMA((steps, 2, hops, 2)),
            pltpu.SemaphoreType.DMA((half_steps,)),
            pltpu.SemaphoreType.DMA((half_steps,)),
            pltpu.SemaphoreType.DMA((half_steps,)),
            pltpu.SemaphoreType.DMA((half_steps,)),
        ],
        compiler_params=pltpu.CompilerParams(
            collective_id=0, has_side_effects=True, vmem_limit_bytes=48 << 20
        ),
        name="sweep",
    )(packed, eigvec)


def solution(mesh):
    placed = (
        P("row", "col"),
        P(None, ("row", "col"), None),
        P(None, ("row", "col"), None),
        P("row", None),
    )
    body = functools.partial(on_device, mesh.shape["col"], mesh.shape["row"])
    return jax.shard_map(body, mesh=mesh, in_specs=placed, out_specs=P("row", "col"), check_vma=False)
```

```python
import functools

import jax
import jax.numpy as jnp
from jax import lax
from jax.experimental import pallas as pl
from jax.experimental.pallas import tpu as pltpu
from jax.sharding import PartitionSpec as P

B = 512
W = 256
MESH = pl.DeviceIdType.MESH


def split(x):
    high = x.astype(jnp.bfloat16)
    low = (x - high.astype(jnp.float32)).astype(jnp.bfloat16)
    return high, low


def product(left, right, dims):
    def one(a, b):
        return lax.dot_general(a, b, (dims, ((), ())), preferred_element_type=jnp.float32)

    return one(left[0], right[0]) + (one(left[0], right[1]) + one(left[1], right[0]))


def pick_kernel(slots, refl, tfac, packed, hold, in_sem, out_sem):
    steps = packed.shape[0]
    v_rows = refl.shape[1]
    t_rows = tfac.shape[1]
    loads, stores = [], []
    for s in range(steps):
        slot = slots[s]
        loads.append(
            (
                pltpu.make_async_copy(refl.at[slot], hold.at[s, pl.ds(0, v_rows)], in_sem.at[s, 0]),
                pltpu.make_async_copy(tfac.at[slot], hold.at[s, pl.ds(v_rows, t_rows)], in_sem.at[s, 1]),
            )
        )
        stores.append(pltpu.make_async_copy(hold.at[s], packed.at[s], out_sem.at[s]))
    for pair in loads:
        for copy in pair:
            copy.start()
    for pair, store in zip(loads, stores):
        for copy in pair:
            copy.wait()
        store.start()
    for store in stores:
        store.wait()


def main_kernel(n, rows_n, groups, packed, eig, out, field, buf, inb, back, landed, own_sem, eig_sem, out_sem,
                ring_send, ring_recv, up_send, up_recv, down_send, down_recv):
    steps, piece, _ = packed.shape
    v_rows = groups * B // n
    per_group = n // groups
    half = piece // 2
    hops = n // 2
    row = lax.axis_index("row")
    col = lax.axis_index("col")
    right = lax.rem(col + 1, n)
    left = lax.rem(col + n - 1, n)
    has_down = row < rows_n - 1
    has_up = row > 0
    down = jnp.minimum(row + 1, rows_n - 1)
    up = jnp.maximum(row - 1, 0)

    eig_copy = pltpu.make_async_copy(eig, field, eig_sem)
    eig_copy.start()

    barrier = pltpu.get_barrier_semaphore()
    pl.semaphore_signal(barrier, inc=1, device_id=(row, left), device_id_type=MESH)
    pl.semaphore_signal(barrier, inc=1, device_id=(row, right), device_id_type=MESH)

    @pl.when(has_up)
    def _():
        pl.semaphore_signal(barrier, inc=1, device_id=(up, col), device_id_type=MESH)

    @pl.when(has_down)
    def _():
        pl.semaphore_signal(barrier, inc=1, device_id=(down, col), device_id_type=MESH)

    pl.semaphore_wait(barrier, 2 + jnp.minimum(row, 1) + jnp.minimum(rows_n - 1 - row, 1))

    def ring_copy(s, way, hop, part):
        target = right if way == 0 else left
        owner = lax.rem(col + n - hop, n) if way == 0 else lax.rem(col + hop, n)
        span = pl.ds(part * half, half)
        src = packed.at[s, span] if hop == 0 else buf.at[s, owner, span]
        return pltpu.make_async_remote_copy(
            src_ref=src,
            dst_ref=buf.at[s, owner, span],
            send_sem=ring_send.at[s, way, hop, part],
            recv_sem=ring_recv.at[s, way, hop, part],
            device_id=(row, target),
            device_id_type=MESH,
        )

    def parts_of(way, hop):
        order = (0, 1) if way == 0 else (1, 0)
        return order[:1] if hop == hops - 1 else order

    def send_own(s):
        for k in range(len(parts_of(0, 0))):
            for way in (0, 1):
                ring_copy(s, way, 0, parts_of(way, 0)[k]).start()

    def forward(s):
        for hop in range(1, hops):
            for k in range(len(parts_of(0, hop))):
                for way in (0, 1):
                    part = parts_of(way, hop)[k]
                    ring_copy(s, way, hop - 1, part).wait_recv()
                    ring_copy(s, way, hop, part).start()

    def finish(s):
        for hop in range(hops):
            for way in (0, 1):
                done = parts_of(way, hop + 1) if hop + 1 < hops else ()
                for part in parts_of(way, hop):
                    if part not in done:
                        ring_copy(s, way, hop, part).wait_recv()

    def vectors_of(s, g):
        block = buf[s, g * per_group:(g + 1) * per_group, :v_rows]
        return split(block.reshape(B, W))

    def factor_of(s, g):
        block = buf[s, g * per_group:(g + 1) * per_group, v_rows:]
        return split(block.reshape(W, W))

    def coeffs_of(s, g, vectors, rows):
        coupling = product(vectors, split(rows), ((0,), (0,)))
        return split(product(factor_of(s, g), split(coupling), ((1,), (0,))))

    def apply_local(s, g, start):
        vectors = vectors_of(s, g)
        rows = field[start:start + B]
        coeffs = coeffs_of(s, g, vectors, rows)
        field[start:start + B] = rows - product(vectors, coeffs, ((1,), (0,)))

    def up_copy(i):
        return pltpu.make_async_remote_copy(
            src_ref=field.at[pl.ds(0, W)], dst_ref=inb.at[i],
            send_sem=up_send.at[i], recv_sem=up_recv.at[i],
            device_id=(up, col), device_id_type=MESH,
        )

    def down_copy(i):
        return pltpu.make_async_remote_copy(
            src_ref=back.at[i], dst_ref=landed.at[i],
            send_sem=down_send.at[i], recv_sem=down_recv.at[i],
            device_id=(down, col), device_id_type=MESH,
        )

    low = groups * B - W

    send_own(0)
    own = [pltpu.make_async_copy(packed.at[s], buf.at[s, col], own_sem.at[s]) for s in range(steps)]
    for copy in own:
        copy.start()
    eig_copy.wait()
    for s in range(steps):
        forward(s)
        if s + 1 < steps:
            send_own(s + 1)
        own[s].wait()
        finish(s)
        i = s // 2
        if s % 2 == 0:
            for g in range(groups):
                apply_local(s, g, g * B)
                if g == 0 and s + 1 < steps:
                    @pl.when(has_up)
                    def _():
                        up_copy(i).start()
        else:
            @pl.when(has_down)
            def _():
                up_copy(i).wait_recv()
                g = groups - 1
                vectors = vectors_of(s, g)
                rows = jnp.concatenate([field[low:], inb[i]], axis=0)
                coeffs = coeffs_of(s, g, vectors, rows)
                bottom = (vectors[0][W:], vectors[1][W:])
                back[i] = rows[W:] - product(bottom, coeffs, ((1,), (0,)))
                down_copy(i).start()
                top = (vectors[0][:W], vectors[1][:W])
                field[low:] = rows[:W] - product(top, coeffs, ((1,), (0,)))

            for g in range(groups - 1):
                apply_local(s, g, W + g * B)

            @pl.when(has_up)
            def _():
                up_copy(i).wait_send()
                down_copy(i).wait_recv()
                field[:W] = landed[i]

    store = pltpu.make_async_copy(field, out, out_sem)
    store.start()
    for s in range(steps):
        for way in (0, 1):
            for hop in range(hops):
                for part in parts_of(way, hop):
                    ring_copy(s, way, hop, part).wait_send()

    @pl.when(has_down)
    def _():
        for i in range(steps // 2):
            down_copy(i).wait_send()

    store.wait()


def line_kernel(rows_n, sched_all, refl, tfac, eig, out, sched, refl_in, tfac_in, field, buf, fed, inb, back, landed,
                local, eig_sem, sends, recvs, turn_sem):
    steps, v_rows, _ = refl.shape
    low = B + W
    last = steps - 1
    row = lax.axis_index("row")
    col = lax.axis_index("col")
    odd = lax.rem(row, 2)
    inner = (col == 1) | (col == 2)
    partner = col + 1 - 2 * lax.rem(col, 2)
    other = 3 - col
    mate = row + 1 - 2 * odd
    beyond = row - 1 + 2 * odd
    has_beyond = (beyond >= 0) & (beyond < rows_n)
    beyond = jnp.clip(beyond, 0, rows_n - 1)
    early = odd == 0
    late = odd == 1
    has_down = row < rows_n - 1
    has_up = row > 0
    down = jnp.minimum(row + 1, rows_n - 1)
    up = jnp.maximum(row - 1, 0)

    def remote(src, dst, send, recv, target):
        return pltpu.make_async_remote_copy(
            src_ref=src, dst_ref=dst, send_sem=send, recv_sem=recv,
            device_id=target, device_id_type=MESH,
        )

    refl_load = pltpu.make_async_copy(refl, refl_in, local.at[0])
    tfac_load = pltpu.make_async_copy(tfac, tfac_in, local.at[1])
    eig_load = pltpu.make_async_copy(eig, field.at[0], eig_sem)
    sched_load = pltpu.make_async_copy(sched_all, sched, local.at[2])
    sched_load.start()
    refl_load.start()
    tfac_load.start()

    barrier = pltpu.get_barrier_semaphore()

    def greet(target):
        pl.semaphore_signal(barrier, inc=1, device_id=target, device_id_type=MESH)

    greet((row, partner))
    greet((mate, partner))
    greet((mate, col))

    @pl.when(has_beyond)
    def _():
        greet((beyond, col))
        greet((beyond, partner))

    @pl.when(inner)
    def _():
        greet((row, other))
        greet((mate, other))

    sched_load.wait()
    refl_load.wait()
    tfac_load.wait()

    @pl.when(inner)
    def _():
        eig_load.start()

    for s in range(steps):
        slot = sched[col // 2, s]
        buf[s, col, :v_rows] = refl_in[slot]
        buf[s, col, v_rows:] = tfac_in[slot]

    pl.semaphore_wait(barrier, 3 + 2 * has_beyond.astype(jnp.int32) + 2 * inner.astype(jnp.int32))

    cuts = (3, 1, 1, 3)
    piece = buf.shape[2]

    def span(s, k):
        size = piece // cuts[s]
        return pl.ds(k * size, size)

    def feed(s, k):
        slot = sum(cuts[:s]) + k
        return remote(buf.at[s, col, span(s, k)], fed.at[s, span(s, k)],
                      sends.at[1 + k if s == last else 0], recvs.at[slot], (mate, partner))

    def feeds():
        return remote(buf.at[pl.ds(0, last), col], fed.at[pl.ds(0, last)], sends.at[0], recvs.at[0], (mate, partner))

    column_rows = ((0, B), (B, W), (B + W, W))

    def columns(g):
        rows = pl.ds(*column_rows[g])
        return remote(eig.at[rows], field.at[1, rows], sends.at[4 + g], recvs.at[8 + g], (row, partner))

    def own(s):
        return remote(buf.at[s, col], buf.at[s, col], sends.at[0], recvs.at[11 + s], (row, other))

    def own_arrival(s):
        return remote(buf.at[s, other], buf.at[s, other], sends.at[0], recvs.at[11 + s], (row, other))

    def own_all():
        return remote(buf.at[:, col], buf.at[:, col], sends.at[0], recvs.at[11], (row, other))

    def relay(s, k):
        return remote(fed.at[s, span(s, k)], buf.at[s, partner, span(s, k)],
                      sends.at[1], recvs.at[15 + s], (mate, other))

    def relay_arrival(s):
        return remote(fed.at[s], buf.at[s, 3 - partner], sends.at[1], recvs.at[15 + s], (mate, other))

    def relay_all():
        return remote(fed, buf.at[:, partner], sends.at[1], recvs.at[15], (mate, other))

    def hand(s, k):
        return remote(fed.at[s, span(s, k)], buf.at[s, partner, span(s, k)],
                      sends.at[2], recvs.at[19 + s], (mate, col))

    def hand_arrival(s):
        return remote(fed.at[s], buf.at[s, partner], sends.at[2], recvs.at[19 + s], (mate, col))

    def hand_all():
        return remote(fed, buf.at[:, partner], sends.at[2], recvs.at[19], (mate, col))

    def result(part, src, target_row):
        rows = (pl.ds(0, W), pl.ds(W, B), pl.ds(low, W))[part]
        return remote(src, out.at[rows], sends.at[10 + part], recvs.at[5 + part], (target_row, partner))

    def vectors_of(s, g):
        return split(buf[s, 2 * g:2 * g + 2, :v_rows].reshape(B, W))

    def factor_of(s, g):
        return split(buf[s, 2 * g:2 * g + 2, v_rows:].reshape(W, W))

    def coeffs_of(vectors, factor, rows):
        coupling = product(vectors, split(rows), ((0,), (0,)))
        return split(product(factor, split(coupling), ((1,), (0,))))

    def load(zs, start, size):
        return jnp.concatenate([field[z, start:start + size] for z in zs], axis=1)

    def save(zs, start, value):
        cols = value.shape[1] // len(zs)
        for k, z in enumerate(zs):
            field[z, start:start + value.shape[0]] = value[:, k * cols:(k + 1) * cols]

    def apply_local(s, g, zs, start):
        vectors = vectors_of(s, g)
        rows = load(zs, start, B)
        coeffs = coeffs_of(vectors, factor_of(s, g), rows)
        save(zs, start, rows - product(vectors, coeffs, ((1,), (0,))))

    def up_copy(i, z):
        return remote(field.at[z, pl.ds(0, W)], inb.at[i, z], sends.at[3 + 2 * i + z], recvs.at[23 + 2 * i + z], (up, col))

    def down_copy(z):
        return remote(back.at[0, z], landed.at[z], sends.at[7 + z], recvs.at[27 + z], (down, col))

    def down_final():
        return remote(back.at[1, 0], out.at[pl.ds(0, W)], sends.at[9], recvs.at[29], (down, col))

    def send_up(s, zs):
        @pl.when(has_up)
        def _():
            for z in zs:
                up_copy(s // 2, z).start()

    def straddle_body(s, zs, send):
        i = s // 2
        vectors = vectors_of(s, 1)
        below = jnp.concatenate([inb[i, z] for z in zs], axis=1)
        rows = jnp.concatenate([load(zs, low, W), below], axis=0)
        coeffs = coeffs_of(vectors, factor_of(s, 1), rows)
        bottom = (vectors[0][W:], vectors[1][W:])
        value = rows[W:] - product(bottom, coeffs, ((1,), (0,)))
        cols = value.shape[1] // len(zs)
        for k, z in enumerate(zs):
            back[i, z] = value[:, k * cols:(k + 1) * cols]
        send()
        top = (vectors[0][:W], vectors[1][:W])
        save(zs, low, rows[:W] - product(top, coeffs, ((1,), (0,))))

    def straddle(s, zs, send):
        @pl.when(has_down)
        def _():
            for z in zs:
                up_copy(s // 2, z).wait_recv()
            straddle_body(s, zs, send)

    def settle(z):
        @pl.when(has_up)
        def _():
            up_copy(0, z).wait_send()
            down_copy(z).wait_recv()
            field[z, :W] = landed[z]

    def pass_chunk(s, k):
        feed(s, k).wait_recv()
        relay(s, k).start()
        hand(s, k).start()

    def passed(s):
        for k in range(cuts[s]):
            pass_chunk(s, k)

    def near(s):
        hand_arrival(s).wait_recv()

    def far(s):
        own_arrival(s).wait_recv()
        relay_arrival(s).wait_recv()

    def store(part):
        rows = (pl.ds(0, W), pl.ds(W, B), pl.ds(low, W))[part]
        return pltpu.make_async_copy(field.at[0, rows], out.at[rows], local.at[part])

    top_row = (col < 2) & (row == 0)
    share_slot = {last: 0, 0: 1, 2: 2}

    def share(s):
        part = buf.at[s, col]
        return remote(part, part, sends.at[13 + share_slot[s]], recvs.at[share_slot[s]], (row, partner))

    def share_arrival(s):
        part = buf.at[s, partner]
        return remote(part, part, sends.at[13 + share_slot[s]], recvs.at[share_slot[s]], (row, partner))

    def state(part, start):
        rows = pl.ds(start, W)
        return remote(field.at[1, rows], field.at[0, rows], sends.at[16 + part], recvs.at[3 + part], (row, partner))

    def state_up():
        return remote(field.at[1, pl.ds(0, W)], inb.at[1, 0], sends.at[17], recvs.at[4], (up, partner))

    def bottom_result():
        return remote(back.at[1, 0], out.at[pl.ds(0, W)], sends.at[10], recvs.at[5], (down, col))

    @pl.when(jnp.logical_not(inner))
    def _():
        def turn():
            pl.semaphore_signal(turn_sem, inc=1, device_id=(mate, col), device_id_type=MESH)

        for k in range(last):
            for c in range(cuts[k]):
                feed(k, c).start()
        columns(0).start()

        def wait_turn():
            pl.semaphore_wait(turn_sem, 1)

        def last_feed():
            for c in range(cuts[last]):
                feed(last, c).start()

        @pl.when(early)
        def _():
            wait_turn()

        columns(1).start()
        columns(2).start()
        columns(1).wait_send()

        @pl.when(late)
        def _():
            turn()
            columns(2).wait_send()
            wait_turn()

        last_feed()

        @pl.when(early)
        def _():
            columns(2).wait_send()

        feed(last, 0).wait_send()
        feed(last, 1).wait_send()

        @pl.when(early)
        def _():
            turn()

        feed(last, 2).wait_send()
        share_arrival(last).wait_recv()

        @pl.when(top_row)
        def _():
            share_arrival(0).wait_recv()
            share_arrival(2).wait_recv()
            top_load = pltpu.make_async_copy(eig.at[pl.ds(0, B)], field.at[1, pl.ds(0, B)], eig_sem)
            top_load.start()
            top_load.wait()
            apply_local(0, 0, (1,), 0)
            field[0, :W] = field[1, :W]
            state(1, W).wait_recv()
            apply_local(2, 0, (0,), 0)
            store(0).start()

        state(0, W).wait_recv()

        @pl.when(col == 0)
        def _():
            @pl.when(has_up)
            def _():
                state(1, W).wait_recv()

            apply_local(last, 0, (0,), W)
            store(1).start()

            @pl.when(has_up)
            def _():
                result(0, field.at[0, pl.ds(0, W)], row).wait_recv()

            @pl.when(jnp.logical_not(has_up))
            def _():
                store(0).wait()

            result(2, field.at[0, pl.ds(0, W)], row).wait_recv()
            store(1).wait()

        @pl.when(col == 3)
        def _():
            @pl.when(has_down)
            def _():
                state_up().wait_recv()
                straddle_body(last, (0,), lambda: bottom_result().start())

            store(2).start()
            result(0, field.at[0, pl.ds(0, W)], row).wait_recv()
            result(1, field.at[0, pl.ds(0, B)], row).wait_recv()
            store(2).wait()

            @pl.when(has_down)
            def _():
                bottom_result().wait_send()

        feeds().wait_send()
        columns(0).wait_send()

    @pl.when(inner)
    def _():
        own(0).start()
        passed(0)
        own(1).start()
        eig_load.wait()
        near(0)

        @pl.when(col == 1)
        def _():
            apply_local(0, 0, (0,), 0)
            send_up(0, (0,))

        @pl.when(col == 2)
        def _():
            apply_local(0, 1, (0,), B)

        passed(1)
        share(last).start()

        @pl.when(top_row)
        def _():
            share(0).start()
            share(2).start()


        @pl.when(early)
        def _():
            own(2).start()

        far(0)
        near(1)

        @pl.when(col == 1)
        def _():
            apply_local(0, 1, (0,), B)
            apply_local(1, 0, (0,), W)

        @pl.when(col == 2)
        def _():
            apply_local(0, 0, (0,), 0)
            send_up(0, (0,))
            straddle(1, (0,), lambda: down_copy(0).start())

        passed(2)

        @pl.when(early)
        def _():
            own(3).start()

        @pl.when(late)
        def _():
            own(2).start()

        far(1)

        @pl.when(col == 1)
        def _():
            straddle(1, (0,), lambda: down_copy(0).start())

        @pl.when(col == 2)
        def _():
            apply_local(1, 0, (0,), W)

        columns(0).wait_recv()
        apply_local(0, 0, (1,), 0)
        send_up(0, (1,))
        settle(0)
        near(2)

        @pl.when(col == 1)
        def _():
            apply_local(2, 0, (0,), 0)
            send_up(2, (0,))

        @pl.when(col == 2)
        def _():
            apply_local(2, 1, (0,), B)

        def far_even():
            @pl.when(col == 1)
            def _():
                apply_local(2, 1, (0,), B)

            @pl.when(col == 2)
            def _():
                apply_local(2, 0, (0,), 0)
                send_up(2, (0,))

        @pl.when(early)
        def _():
            far(2)
            far_even()

        columns(1).wait_recv()
        columns(2).wait_recv()
        apply_local(0, 1, (1,), B)
        straddle(1, (1,), lambda: down_copy(1).start())

        apply_local(1, 0, (1,), W)

        @pl.when(top_row)
        def _():
            state(1, W).start()

        @pl.when(late)
        def _():
            pass_chunk(3, 0)

        @pl.when(col == 2)
        def _():
            apply_local(2, 1, (1,), B)
            state(0, low).start()

        @pl.when(late)
        def _():
            far(2)

        @pl.when(col == 1)
        def _():
            apply_local(2, 1, (1,), B)
            state(0, B).start()


        @pl.when(late)
        def _():
            pass_chunk(3, 1)

        settle(1)

        @pl.when(late)
        def _():
            pass_chunk(3, 2)
            own(3).start()

        @pl.when(jnp.logical_not(top_row))
        def _():
            apply_local(2, 0, (1,), 0)

        @pl.when((col == 1) & has_up)
        def _():
            state(1, W).start()
            up_copy(1, 1).start()

        @pl.when((col == 2) & has_up)
        def _():
            state_up().start()


        @pl.when(early)
        def _():
            passed(3)


        @pl.when(late)
        def _():
            far_even()

        @pl.when(jnp.logical_not(has_up))
        def _():
            store(0).start()

        @pl.when((col == 2) & jnp.logical_not(has_up))
        def _():
            result(0, field.at[1, pl.ds(0, W)], row).start()

        def near_last():
            near(3)

            @pl.when(col == 1)
            def _():
                apply_local(last, 0, (0,), W)
                store(1).start()

            @pl.when(col == 2)
            def _():
                straddle(last, (0,), lambda: down_final().start())
                store(2).start()

        @pl.when(late)
        def _():
            near_last()

        far(3)

        @pl.when(col == 1)
        def _():
            straddle(last, (1,), lambda: result(0, back.at[1, 1], down).start())
            result(2, field.at[1, pl.ds(low, W)], row).start()

        @pl.when(col == 2)
        def _():
            apply_local(last, 0, (1,), W)
            result(1, field.at[1, pl.ds(W, B)], row).start()

        @pl.when(early)
        def _():
            near_last()

        @pl.when(col == 1)
        def _():
            straddle(last, (0,), lambda: down_final().start())
            store(2).start()

        @pl.when(col == 2)
        def _():
            apply_local(last, 0, (0,), W)
            store(1).start()

        share(last).wait_send()

        @pl.when(top_row)
        def _():
            share(0).wait_send()
            share(2).wait_send()

        state(0, W).wait_send()
        own_all().wait_send()
        relay_all().wait_send()
        hand_all().wait_send()

        @pl.when(has_up)
        def _():
            up_copy(last // 2, 0).wait_send()
            down_final().wait_recv()

        @pl.when(has_down)
        def _():
            down_copy(0).wait_send()
            down_copy(1).wait_send()
            down_final().wait_send()

        @pl.when(jnp.logical_not(has_up))
        def _():
            store(0).wait()

        @pl.when(col == 1)
        def _():
            state(1, W).wait_send()

            @pl.when(has_up)
            def _():
                up_copy(last // 2, 1).wait_send()

            @pl.when(has_down)
            def _():
                result(0, back.at[1, 1], down).wait_send()

            result(2, field.at[1, pl.ds(low, W)], row).wait_send()

        @pl.when(col == 2)
        def _():
            @pl.when(has_up)
            def _():
                state_up().wait_send()

            @pl.when(jnp.logical_not(has_up))
            def _():
                result(0, field.at[1, pl.ds(0, W)], row).wait_send()

            result(1, field.at[1, pl.ds(W, B)], row).wait_send()

        store(1).wait()
        store(2).wait()


def on_device(n, rows_n, eigvec, refl, tfac, sched):
    steps, v_rows, _ = refl.shape
    t_rows = tfac.shape[1]
    groups = sched.shape[0]
    evcount = eigvec.shape[1]
    piece = v_rows + t_rows
    hops = n // 2
    half_steps = steps // 2
    anywhere = pl.BlockSpec(memory_space=pl.ANY)
    if n == 4 and groups == 2 and steps == 4 and rows_n % 2 == 0:
        two = (half_steps, 2)
        dma = pltpu.SemaphoreType.DMA
        return pl.pallas_call(
            functools.partial(line_kernel, rows_n),
            out_shape=pltpu.VMEM(eigvec.shape, jnp.float32),
            in_specs=[anywhere, anywhere, anywhere, anywhere],
            out_specs=anywhere,
            scratch_shapes=[
                pltpu.SMEM(sched.shape, jnp.int32),
                pltpu.VMEM(refl.shape, jnp.float32),
                pltpu.VMEM(tfac.shape, jnp.float32),
                pltpu.VMEM((2, *eigvec.shape), jnp.float32),
                pltpu.VMEM((steps, n, piece, W), jnp.float32),
                pltpu.VMEM((steps, piece, W), jnp.float32),
                pltpu.VMEM((*two, W, evcount), jnp.float32),
                pltpu.VMEM((*two, W, evcount), jnp.float32),
                pltpu.VMEM((2, W, evcount), jnp.float32),
                dma((3,)),
                dma,
                dma((18,)),
                dma((30,)),
                pltpu.SemaphoreType.REGULAR,
            ],
            compiler_params=pltpu.CompilerParams(
                collective_id=0, has_side_effects=True, vmem_limit_bytes=60 << 20
            ),
            name="sweep",
        )(sched, refl, tfac, eigvec)
    owner = lax.axis_index("col") * v_rows // B
    slots = lax.dynamic_index_in_dim(sched, owner, 0, keepdims=False)
    packed = pl.pallas_call(
        pick_kernel,
        out_shape=jax.ShapeDtypeStruct((steps, piece, W), jnp.float32),
        in_specs=[pl.BlockSpec(memory_space=pltpu.SMEM), anywhere, anywhere],
        out_specs=anywhere,
        scratch_shapes=[
            pltpu.VMEM((steps, piece, W), jnp.float32),
            pltpu.SemaphoreType.DMA((steps, 2)),
            pltpu.SemaphoreType.DMA((steps,)),
        ],
        name="pick",
    )(slots, refl, tfac)
    return pl.pallas_call(
        functools.partial(main_kernel, n, rows_n, groups),
        out_shape=jax.ShapeDtypeStruct(eigvec.shape, jnp.float32),
        in_specs=[anywhere, anywhere],
        out_specs=anywhere,
        scratch_shapes=[
            pltpu.VMEM(eigvec.shape, jnp.float32),
            pltpu.VMEM((steps, n, piece, W), jnp.float32),
            pltpu.VMEM((half_steps, W, evcount), jnp.float32),
            pltpu.VMEM((half_steps, W, evcount), jnp.float32),
            pltpu.VMEM((half_steps, W, evcount), jnp.float32),
            pltpu.SemaphoreType.DMA((steps,)),
            pltpu.SemaphoreType.DMA,
            pltpu.SemaphoreType.DMA,
            pltpu.SemaphoreType.DMA((steps, 2, hops, 2)),
            pltpu.SemaphoreType.DMA((steps, 2, hops, 2)),
            pltpu.SemaphoreType.DMA((half_steps,)),
            pltpu.SemaphoreType.DMA((half_steps,)),
            pltpu.SemaphoreType.DMA((half_steps,)),
            pltpu.SemaphoreType.DMA((half_steps,)),
        ],
        compiler_params=pltpu.CompilerParams(
            collective_id=0, has_side_effects=True, vmem_limit_bytes=48 << 20
        ),
        name="sweep",
    )(packed, eigvec)


def solution(mesh):
    placed = (
        P("row", "col"),
        P(None, ("row", "col"), None),
        P(None, ("row", "col"), None),
        P("row", None),
    )
    body = functools.partial(on_device, mesh.shape["col"], mesh.shape["row"])
    return jax.shard_map(body, mesh=mesh, in_specs=placed, out_specs=P("row", "col"), check_vma=False)
```

```python
import functools

import jax
import jax.numpy as jnp
from jax import lax
from jax.experimental import pallas as pl
from jax.experimental.pallas import tpu as pltpu
from jax.sharding import PartitionSpec as P

B = 512
W = 256
MESH = pl.DeviceIdType.MESH


def split(x):
    high = x.astype(jnp.bfloat16)
    low = (x - high.astype(jnp.float32)).astype(jnp.bfloat16)
    return high, low


def product(left, right, dims):
    def one(a, b):
        return lax.dot_general(a, b, (dims, ((), ())), preferred_element_type=jnp.float32)

    return one(left[0], right[0]) + (one(left[0], right[1]) + one(left[1], right[0]))


def pick_kernel(slots, refl, tfac, packed, hold, in_sem, out_sem):
    steps = packed.shape[0]
    v_rows = refl.shape[1]
    t_rows = tfac.shape[1]
    loads, stores = [], []
    for s in range(steps):
        slot = slots[s]
        loads.append(
            (
                pltpu.make_async_copy(refl.at[slot], hold.at[s, pl.ds(0, v_rows)], in_sem.at[s, 0]),
                pltpu.make_async_copy(tfac.at[slot], hold.at[s, pl.ds(v_rows, t_rows)], in_sem.at[s, 1]),
            )
        )
        stores.append(pltpu.make_async_copy(hold.at[s], packed.at[s], out_sem.at[s]))
    for pair in loads:
        for copy in pair:
            copy.start()
    for pair, store in zip(loads, stores):
        for copy in pair:
            copy.wait()
        store.start()
    for store in stores:
        store.wait()


def main_kernel(n, rows_n, groups, packed, eig, out, field, buf, inb, back, landed, own_sem, eig_sem, out_sem,
                ring_send, ring_recv, up_send, up_recv, down_send, down_recv):
    steps, piece, _ = packed.shape
    v_rows = groups * B // n
    per_group = n // groups
    half = piece // 2
    hops = n // 2
    row = lax.axis_index("row")
    col = lax.axis_index("col")
    right = lax.rem(col + 1, n)
    left = lax.rem(col + n - 1, n)
    has_down = row < rows_n - 1
    has_up = row > 0
    down = jnp.minimum(row + 1, rows_n - 1)
    up = jnp.maximum(row - 1, 0)

    eig_copy = pltpu.make_async_copy(eig, field, eig_sem)
    eig_copy.start()

    barrier = pltpu.get_barrier_semaphore()
    pl.semaphore_signal(barrier, inc=1, device_id=(row, left), device_id_type=MESH)
    pl.semaphore_signal(barrier, inc=1, device_id=(row, right), device_id_type=MESH)

    @pl.when(has_up)
    def _():
        pl.semaphore_signal(barrier, inc=1, device_id=(up, col), device_id_type=MESH)

    @pl.when(has_down)
    def _():
        pl.semaphore_signal(barrier, inc=1, device_id=(down, col), device_id_type=MESH)

    pl.semaphore_wait(barrier, 2 + jnp.minimum(row, 1) + jnp.minimum(rows_n - 1 - row, 1))

    def ring_copy(s, way, hop, part):
        target = right if way == 0 else left
        owner = lax.rem(col + n - hop, n) if way == 0 else lax.rem(col + hop, n)
        span = pl.ds(part * half, half)
        src = packed.at[s, span] if hop == 0 else buf.at[s, owner, span]
        return pltpu.make_async_remote_copy(
            src_ref=src,
            dst_ref=buf.at[s, owner, span],
            send_sem=ring_send.at[s, way, hop, part],
            recv_sem=ring_recv.at[s, way, hop, part],
            device_id=(row, target),
            device_id_type=MESH,
        )

    def parts_of(way, hop):
        order = (0, 1) if way == 0 else (1, 0)
        return order[:1] if hop == hops - 1 else order

    def send_own(s):
        for k in range(len(parts_of(0, 0))):
            for way in (0, 1):
                ring_copy(s, way, 0, parts_of(way, 0)[k]).start()

    def forward(s):
        for hop in range(1, hops):
            for k in range(len(parts_of(0, hop))):
                for way in (0, 1):
                    part = parts_of(way, hop)[k]
                    ring_copy(s, way, hop - 1, part).wait_recv()
                    ring_copy(s, way, hop, part).start()

    def finish(s):
        for hop in range(hops):
            for way in (0, 1):
                done = parts_of(way, hop + 1) if hop + 1 < hops else ()
                for part in parts_of(way, hop):
                    if part not in done:
                        ring_copy(s, way, hop, part).wait_recv()

    def vectors_of(s, g):
        block = buf[s, g * per_group:(g + 1) * per_group, :v_rows]
        return split(block.reshape(B, W))

    def factor_of(s, g):
        block = buf[s, g * per_group:(g + 1) * per_group, v_rows:]
        return split(block.reshape(W, W))

    def coeffs_of(s, g, vectors, rows):
        coupling = product(vectors, split(rows), ((0,), (0,)))
        return split(product(factor_of(s, g), split(coupling), ((1,), (0,))))

    def apply_local(s, g, start):
        vectors = vectors_of(s, g)
        rows = field[start:start + B]
        coeffs = coeffs_of(s, g, vectors, rows)
        field[start:start + B] = rows - product(vectors, coeffs, ((1,), (0,)))

    def up_copy(i):
        return pltpu.make_async_remote_copy(
            src_ref=field.at[pl.ds(0, W)], dst_ref=inb.at[i],
            send_sem=up_send.at[i], recv_sem=up_recv.at[i],
            device_id=(up, col), device_id_type=MESH,
        )

    def down_copy(i):
        return pltpu.make_async_remote_copy(
            src_ref=back.at[i], dst_ref=landed.at[i],
            send_sem=down_send.at[i], recv_sem=down_recv.at[i],
            device_id=(down, col), device_id_type=MESH,
        )

    low = groups * B - W

    send_own(0)
    own = [pltpu.make_async_copy(packed.at[s], buf.at[s, col], own_sem.at[s]) for s in range(steps)]
    for copy in own:
        copy.start()
    eig_copy.wait()
    for s in range(steps):
        forward(s)
        if s + 1 < steps:
            send_own(s + 1)
        own[s].wait()
        finish(s)
        i = s // 2
        if s % 2 == 0:
            for g in range(groups):
                apply_local(s, g, g * B)
                if g == 0 and s + 1 < steps:
                    @pl.when(has_up)
                    def _():
                        up_copy(i).start()
        else:
            @pl.when(has_down)
            def _():
                up_copy(i).wait_recv()
                g = groups - 1
                vectors = vectors_of(s, g)
                rows = jnp.concatenate([field[low:], inb[i]], axis=0)
                coeffs = coeffs_of(s, g, vectors, rows)
                bottom = (vectors[0][W:], vectors[1][W:])
                back[i] = rows[W:] - product(bottom, coeffs, ((1,), (0,)))
                down_copy(i).start()
                top = (vectors[0][:W], vectors[1][:W])
                field[low:] = rows[:W] - product(top, coeffs, ((1,), (0,)))

            for g in range(groups - 1):
                apply_local(s, g, W + g * B)

            @pl.when(has_up)
            def _():
                up_copy(i).wait_send()
                down_copy(i).wait_recv()
                field[:W] = landed[i]

    store = pltpu.make_async_copy(field, out, out_sem)
    store.start()
    for s in range(steps):
        for way in (0, 1):
            for hop in range(hops):
                for part in parts_of(way, hop):
                    ring_copy(s, way, hop, part).wait_send()

    @pl.when(has_down)
    def _():
        for i in range(steps // 2):
            down_copy(i).wait_send()

    store.wait()


def line_kernel(rows_n, sched_all, refl, tfac, eig, out, sched, refl_in, tfac_in, field, buf, fed, inb, back, landed,
                local, eig_sem, sends, recvs, turn_sem):
    steps, v_rows, _ = refl.shape
    low = B + W
    last = steps - 1
    row = lax.axis_index("row")
    col = lax.axis_index("col")
    odd = lax.rem(row, 2)
    inner = (col == 1) | (col == 2)
    partner = col + 1 - 2 * lax.rem(col, 2)
    other = 3 - col
    mate = row + 1 - 2 * odd
    beyond = row - 1 + 2 * odd
    has_beyond = (beyond >= 0) & (beyond < rows_n)
    beyond = jnp.clip(beyond, 0, rows_n - 1)
    early = odd == 0
    late = odd == 1
    has_down = row < rows_n - 1
    has_up = row > 0
    down = jnp.minimum(row + 1, rows_n - 1)
    up = jnp.maximum(row - 1, 0)

    def remote(src, dst, send, recv, target):
        return pltpu.make_async_remote_copy(
            src_ref=src, dst_ref=dst, send_sem=send, recv_sem=recv,
            device_id=target, device_id_type=MESH,
        )

    refl_load = pltpu.make_async_copy(refl, refl_in, local.at[0])
    tfac_load = pltpu.make_async_copy(tfac, tfac_in, local.at[1])
    eig_load = pltpu.make_async_copy(eig, field.at[0], eig_sem)
    sched_load = pltpu.make_async_copy(sched_all, sched, local.at[2])
    sched_load.start()
    refl_load.start()
    tfac_load.start()

    barrier = pltpu.get_barrier_semaphore()

    def greet(target):
        pl.semaphore_signal(barrier, inc=1, device_id=target, device_id_type=MESH)

    greet((row, partner))
    greet((mate, partner))
    greet((mate, col))

    @pl.when(has_beyond)
    def _():
        greet((beyond, col))
        greet((beyond, partner))

    @pl.when(inner)
    def _():
        greet((row, other))
        greet((mate, other))

    sched_load.wait()
    refl_load.wait()
    tfac_load.wait()

    def pick(s):
        slot = sched[col // 2, s]
        buf[s, col, :v_rows] = refl_in[slot]
        buf[s, col, v_rows:] = tfac_in[slot]

    pick(0)

    pl.semaphore_wait(barrier, 3 + 2 * has_beyond.astype(jnp.int32) + 2 * inner.astype(jnp.int32))

    cuts = (3, 1, 1, 3)
    piece = buf.shape[2]

    def span(s, k):
        size = piece // cuts[s]
        return pl.ds((k + 2) % 3 * size if s == last else k * size, size)

    def feed(s, k):
        slot = sum(cuts[:s]) + k
        return remote(buf.at[s, col, span(s, k)], fed.at[s, span(s, k)],
                      sends.at[1 + k if s == last else 0], recvs.at[slot], (mate, partner))

    def feeds():
        return remote(buf.at[pl.ds(0, last), col], fed.at[pl.ds(0, last)], sends.at[0], recvs.at[0], (mate, partner))

    column_rows = ((0, B), (B, W), (B + W, W))

    def columns(g):
        rows = pl.ds(*column_rows[g])
        return remote(eig.at[rows], field.at[1, rows], sends.at[4 + g], recvs.at[8 + g], (row, partner))

    lead = piece // 3

    def own(s):
        return remote(buf.at[s, col], buf.at[s, col], sends.at[0], recvs.at[11 + s], (row, other))

    def own_arrival(s):
        return remote(buf.at[s, other], buf.at[s, other], sends.at[0], recvs.at[11 + s], (row, other))

    def own_last(k, owner):
        part = buf.at[last, owner, (pl.ds(lead, piece - lead), pl.ds(0, lead))[k]]
        return remote(part, part, sends.at[0], recvs.at[(11 + last, 30)[k]], (row, other))

    def send_last():
        own_last(0, col).start()
        own_last(1, col).start()

    def own_all():
        return remote(buf.at[:, col], buf.at[:, col], sends.at[0], recvs.at[11], (row, other))

    def relay(s, k):
        return remote(fed.at[s, span(s, k)], buf.at[s, partner, span(s, k)],
                      sends.at[1], recvs.at[31 if s == last and k == 2 else 15 + s], (mate, other))

    def relay_end():
        rows = pl.ds(lead, lead)
        return remote(fed.at[last, rows], buf.at[last, 3 - partner, rows],
                      sends.at[1], recvs.at[31], (mate, other))

    def relay_lead():
        rows = pl.ds(0, 2 * lead)
        return remote(fed.at[last, rows], buf.at[last, 3 - partner, rows],
                      sends.at[1], recvs.at[15 + last], (mate, other))

    def relay_arrival(s):
        return remote(fed.at[s], buf.at[s, 3 - partner], sends.at[1], recvs.at[15 + s], (mate, other))

    def relay_all():
        return remote(fed, buf.at[:, partner], sends.at[1], recvs.at[15], (mate, other))

    def hand(s, k):
        return remote(fed.at[s, span(s, k)], buf.at[s, partner, span(s, k)],
                      sends.at[2], recvs.at[19 + s], (mate, col))

    def hand_arrival(s):
        return remote(fed.at[s], buf.at[s, partner], sends.at[2], recvs.at[19 + s], (mate, col))

    def hand_all():
        return remote(fed, buf.at[:, partner], sends.at[2], recvs.at[19], (mate, col))

    def result(part, src, target_row):
        rows = (pl.ds(0, W), pl.ds(W, B), pl.ds(low, W))[part]
        return remote(src, out.at[rows], sends.at[10 + part], recvs.at[5 + part], (target_row, partner))

    def vectors_of(s, g):
        return split(buf[s, 2 * g:2 * g + 2, :v_rows].reshape(B, W))

    def factor_of(s, g):
        return split(buf[s, 2 * g:2 * g + 2, v_rows:].reshape(W, W))

    def coeffs_of(vectors, factor, rows):
        coupling = product(vectors, split(rows), ((0,), (0,)))
        return split(product(factor, split(coupling), ((1,), (0,))))

    def load(zs, start, size):
        return jnp.concatenate([field[z, start:start + size] for z in zs], axis=1)

    def save(zs, start, value):
        cols = value.shape[1] // len(zs)
        for k, z in enumerate(zs):
            field[z, start:start + value.shape[0]] = value[:, k * cols:(k + 1) * cols]

    def apply_local(s, g, zs, start):
        vectors = vectors_of(s, g)
        rows = load(zs, start, B)
        coeffs = coeffs_of(vectors, factor_of(s, g), rows)
        save(zs, start, rows - product(vectors, coeffs, ((1,), (0,))))

    def up_copy(i, z):
        return remote(field.at[z, pl.ds(0, W)], inb.at[i, z], sends.at[3 + 2 * i + z], recvs.at[23 + 2 * i + z], (up, col))

    def down_copy(z):
        return remote(back.at[0, z], landed.at[z], sends.at[7 + z], recvs.at[27 + z], (down, col))

    def down_final():
        return remote(back.at[1, 0], out.at[pl.ds(0, W)], sends.at[9], recvs.at[29], (down, col))

    def send_up(s, zs):
        @pl.when(has_up)
        def _():
            for z in zs:
                up_copy(s // 2, z).start()

    def straddle_body(s, zs, send):
        i = s // 2
        vectors = vectors_of(s, 1)
        below = jnp.concatenate([inb[i, z] for z in zs], axis=1)
        rows = jnp.concatenate([load(zs, low, W), below], axis=0)
        coeffs = coeffs_of(vectors, factor_of(s, 1), rows)
        bottom = (vectors[0][W:], vectors[1][W:])
        value = rows[W:] - product(bottom, coeffs, ((1,), (0,)))
        cols = value.shape[1] // len(zs)
        for k, z in enumerate(zs):
            back[i, z] = value[:, k * cols:(k + 1) * cols]
        send()
        top = (vectors[0][:W], vectors[1][:W])
        save(zs, low, rows[:W] - product(top, coeffs, ((1,), (0,))))

    def straddle(s, zs, send):
        @pl.when(has_down)
        def _():
            for z in zs:
                up_copy(s // 2, z).wait_recv()
            straddle_body(s, zs, send)

    def settle(z):
        @pl.when(has_up)
        def _():
            up_copy(0, z).wait_send()
            down_copy(z).wait_recv()
            field[z, :W] = landed[z]

    def pass_chunk(s, k):
        feed(s, k).wait_recv()
        relay(s, k).start()
        hand(s, k).start()

    def passed(s):
        for k in range(cuts[s]):
            pass_chunk(s, k)

    def near(s):
        hand_arrival(s).wait_recv()

    def far(s):
        own_arrival(s).wait_recv()
        relay_arrival(s).wait_recv()

    def far_lead():
        own_last(0, other).wait_recv()
        relay_lead().wait_recv()

    def far_end():
        own_last(1, other).wait_recv()
        relay_end().wait_recv()

    def store(part):
        rows = (pl.ds(0, W), pl.ds(W, B), pl.ds(low, W))[part]
        return pltpu.make_async_copy(field.at[0, rows], out.at[rows], local.at[part])

    top_row = (col < 2) & (row == 0)
    share_slot = {last: 0, 0: 1, 2: 2}

    def share(s):
        part = buf.at[s, col]
        return remote(part, part, sends.at[13 + share_slot[s]], recvs.at[share_slot[s]], (row, partner))

    def share_arrival(s):
        part = buf.at[s, partner]
        return remote(part, part, sends.at[13 + share_slot[s]], recvs.at[share_slot[s]], (row, partner))

    def half_result(part, half):
        start = (0, None, low)[part] + half * lead
        src = back.at[1, 1, pl.ds(half * lead, lead)] if part == 0 else field.at[1, pl.ds(start, lead)]
        return remote(src, out.at[pl.ds(start, lead)], sends.at[10 + part], recvs.at[5 + part],
                      (down if part == 0 else row, partner))

    def rows_of(owner, start):
        return split(buf[last, owner, start:start + lead])

    def joined(a, b):
        return jnp.concatenate([a[0], b[0]], axis=0), jnp.concatenate([a[1], b[1]], axis=0)

    def late_straddle():
        far_lead()

        @pl.when(jnp.logical_not(has_down))
        def _():
            far_end()
            half_result(2, 0).start()
            half_result(2, 1).start()

        @pl.when(has_down)
        def _():
            up_copy(1, 1).wait_recv()
            factor = factor_of(last, 1)
            inside = joined(rows_of(2, lead), rows_of(3, 0))
            rows_in = jnp.concatenate([field[1, low + lead:low + W], inb[1, 1, :lead]], axis=0)
            rows_out = jnp.concatenate([field[1, low:low + lead], inb[1, 1, lead:]], axis=0)
            part = product(inside, split(rows_in), ((0,), (0,)))
            scaled = split(product(inside, factor, ((1,), (0,))))
            far_end()
            outside = joined(rows_of(2, 0), rows_of(3, lead))
            coupling = split(part + product(outside, split(rows_out), ((0,), (0,))))
            value = rows_in - product(scaled, coupling, ((1,), (0,)))
            back[1, 1, :lead] = value[lead:]
            field[1, low + lead:low + W] = value[:lead]
            half_result(0, 0).start()
            half_result(2, 1).start()
            ends = split(product(outside, factor, ((1,), (0,))))
            value = rows_out - product(ends, coupling, ((1,), (0,)))
            back[1, 1, lead:] = value[lead:]
            field[1, low:low + lead] = value[:lead]
            half_result(0, 1).start()
            half_result(2, 0).start()

    def state(part, start):
        rows = pl.ds(start, W)
        return remote(field.at[1, rows], field.at[0, rows], sends.at[16 + part], recvs.at[3 + part], (row, partner))

    def state_up():
        return remote(field.at[1, pl.ds(0, W)], inb.at[1, 0], sends.at[17], recvs.at[4], (up, partner))

    def bottom_result():
        return remote(back.at[1, 0], out.at[pl.ds(0, W)], sends.at[10], recvs.at[5], (down, col))

    @pl.when(jnp.logical_not(inner))
    def _():
        def turn():
            pl.semaphore_signal(turn_sem, inc=1, device_id=(mate, col), device_id_type=MESH)

        for k in range(last):
            if k > 0:
                pick(k)
            for c in range(cuts[k]):
                feed(k, c).start()
        columns(0).start()
        pick(last)

        def wait_turn():
            pl.semaphore_wait(turn_sem, 1)

        def last_feed():
            for c in range(cuts[last]):
                feed(last, c).start()

        @pl.when(late)
        def _():
            wait_turn()

        columns(1).start()
        columns(2).start()
        columns(1).wait_send()

        @pl.when(early)
        def _():
            turn()
            columns(2).wait_send()
            wait_turn()

        @pl.when(late)
        def _():
            columns(2).wait_send()
            turn()
            wait_turn()

        last_feed()
        feed(last, 0).wait_send()
        feed(last, 1).wait_send()

        @pl.when(early)
        def _():
            turn()

        feed(last, 2).wait_send()
        share_arrival(last).wait_recv()

        @pl.when(top_row)
        def _():
            share_arrival(0).wait_recv()
            share_arrival(2).wait_recv()
            top_load = pltpu.make_async_copy(eig.at[pl.ds(0, B)], field.at[1, pl.ds(0, B)], eig_sem)
            top_load.start()
            top_load.wait()
            apply_local(0, 0, (1,), 0)
            field[0, :W] = field[1, :W]
            state(1, W).wait_recv()
            apply_local(2, 0, (0,), 0)
            store(0).start()

        state(0, W).wait_recv()

        @pl.when(col == 0)
        def _():
            @pl.when(has_up)
            def _():
                state(1, W).wait_recv()

            apply_local(last, 0, (0,), W)
            store(1).start()

            @pl.when(has_up)
            def _():
                result(0, field.at[0, pl.ds(0, W)], row).wait_recv()

            @pl.when(jnp.logical_not(has_up))
            def _():
                store(0).wait()

            result(2, field.at[0, pl.ds(0, W)], row).wait_recv()
            store(1).wait()

        @pl.when(col == 3)
        def _():
            @pl.when(has_down)
            def _():
                state_up().wait_recv()
                straddle_body(last, (0,), lambda: bottom_result().start())

            store(2).start()
            result(0, field.at[0, pl.ds(0, W)], row).wait_recv()
            result(1, field.at[0, pl.ds(0, B)], row).wait_recv()
            store(2).wait()

            @pl.when(has_down)
            def _():
                bottom_result().wait_send()

        feeds().wait_send()
        columns(0).wait_send()

    @pl.when(inner)
    def _():
        own(0).start()
        eig_load.start()
        for s in range(1, steps):
            pick(s)
        passed(0)
        own(1).start()
        eig_load.wait()
        near(0)

        @pl.when(col == 1)
        def _():
            apply_local(0, 0, (0,), 0)
            send_up(0, (0,))

        @pl.when(col == 2)
        def _():
            apply_local(0, 1, (0,), B)

        passed(1)
        share(last).start()

        @pl.when(top_row)
        def _():
            share(0).start()
            share(2).start()


        @pl.when(early)
        def _():
            own(2).start()

        far(0)
        near(1)

        @pl.when(col == 1)
        def _():
            apply_local(0, 1, (0,), B)
            apply_local(1, 0, (0,), W)

        @pl.when(col == 2)
        def _():
            apply_local(0, 0, (0,), 0)
            send_up(0, (0,))
            straddle(1, (0,), lambda: down_copy(0).start())

        passed(2)

        @pl.when(early)
        def _():
            send_last()

        @pl.when(late)
        def _():
            own(2).start()

        far(1)

        @pl.when(col == 1)
        def _():
            straddle(1, (0,), lambda: down_copy(0).start())

        @pl.when(col == 2)
        def _():
            apply_local(1, 0, (0,), W)

        columns(0).wait_recv()
        apply_local(0, 0, (1,), 0)
        send_up(0, (1,))
        settle(0)
        near(2)

        @pl.when(col == 1)
        def _():
            apply_local(2, 0, (0,), 0)
            send_up(2, (0,))

        @pl.when(col == 2)
        def _():
            apply_local(2, 1, (0,), B)

        def far_even():
            @pl.when(col == 1)
            def _():
                apply_local(2, 1, (0,), B)

            @pl.when(col == 2)
            def _():
                apply_local(2, 0, (0,), 0)
                send_up(2, (0,))

        @pl.when(early)
        def _():
            far(2)
            far_even()

        columns(1).wait_recv()
        columns(2).wait_recv()
        apply_local(0, 1, (1,), B)
        straddle(1, (1,), lambda: down_copy(1).start())

        apply_local(1, 0, (1,), W)

        @pl.when(top_row)
        def _():
            state(1, W).start()

        @pl.when(late)
        def _():
            pass_chunk(3, 0)

        @pl.when(col == 2)
        def _():
            apply_local(2, 1, (1,), B)
            state(0, low).start()

        @pl.when(late)
        def _():
            far(2)

        @pl.when(col == 1)
        def _():
            apply_local(2, 1, (1,), B)
            state(0, B).start()


        @pl.when(late)
        def _():
            pass_chunk(3, 1)

        settle(1)

        @pl.when(late)
        def _():
            pass_chunk(3, 2)
            send_last()

        @pl.when(jnp.logical_not(top_row))
        def _():
            apply_local(2, 0, (1,), 0)

        @pl.when((col == 1) & has_up)
        def _():
            state(1, W).start()
            up_copy(1, 1).start()

        @pl.when((col == 2) & has_up)
        def _():
            state_up().start()


        @pl.when(early)
        def _():
            passed(3)


        @pl.when(late)
        def _():
            far_even()

        @pl.when(jnp.logical_not(has_up))
        def _():
            store(0).start()

        @pl.when((col == 2) & jnp.logical_not(has_up))
        def _():
            result(0, field.at[1, pl.ds(0, W)], row).start()

        def near_last():
            near(3)

            @pl.when(col == 1)
            def _():
                apply_local(last, 0, (0,), W)
                store(1).start()

            @pl.when(col == 2)
            def _():
                straddle(last, (0,), lambda: down_final().start())
                store(2).start()

        @pl.when(late)
        def _():
            near_last()

        @pl.when(early | (col == 2))
        def _():
            far_lead()
            far_end()

        @pl.when((col == 1) & early)
        def _():
            straddle(last, (1,), lambda: result(0, back.at[1, 1], down).start())
            result(2, field.at[1, pl.ds(low, W)], row).start()

        @pl.when((col == 1) & late)
        def _():
            late_straddle()

        @pl.when(col == 2)
        def _():
            apply_local(last, 0, (1,), W)
            result(1, field.at[1, pl.ds(W, B)], row).start()

        @pl.when(early)
        def _():
            near_last()

        @pl.when(col == 1)
        def _():
            straddle(last, (0,), lambda: down_final().start())
            store(2).start()

        @pl.when(col == 2)
        def _():
            apply_local(last, 0, (0,), W)
            store(1).start()

        share(last).wait_send()

        @pl.when(top_row)
        def _():
            share(0).wait_send()
            share(2).wait_send()

        state(0, W).wait_send()
        own_all().wait_send()
        relay_all().wait_send()
        hand_all().wait_send()

        @pl.when(has_up)
        def _():
            up_copy(last // 2, 0).wait_send()
            down_final().wait_recv()

        @pl.when(has_down)
        def _():
            down_copy(0).wait_send()
            down_copy(1).wait_send()
            down_final().wait_send()

        @pl.when(jnp.logical_not(has_up))
        def _():
            store(0).wait()

        @pl.when(col == 1)
        def _():
            state(1, W).wait_send()

            @pl.when(has_up)
            def _():
                up_copy(last // 2, 1).wait_send()

            @pl.when(has_down)
            def _():
                result(0, back.at[1, 1], down).wait_send()

            result(2, field.at[1, pl.ds(low, W)], row).wait_send()

        @pl.when(col == 2)
        def _():
            @pl.when(has_up)
            def _():
                state_up().wait_send()

            @pl.when(jnp.logical_not(has_up))
            def _():
                result(0, field.at[1, pl.ds(0, W)], row).wait_send()

            result(1, field.at[1, pl.ds(W, B)], row).wait_send()

        store(1).wait()
        store(2).wait()


def on_device(n, rows_n, eigvec, refl, tfac, sched):
    steps, v_rows, _ = refl.shape
    t_rows = tfac.shape[1]
    groups = sched.shape[0]
    evcount = eigvec.shape[1]
    piece = v_rows + t_rows
    hops = n // 2
    half_steps = steps // 2
    anywhere = pl.BlockSpec(memory_space=pl.ANY)
    if n == 4 and groups == 2 and steps == 4 and rows_n % 2 == 0:
        two = (half_steps, 2)
        dma = pltpu.SemaphoreType.DMA
        return pl.pallas_call(
            functools.partial(line_kernel, rows_n),
            out_shape=pltpu.VMEM(eigvec.shape, jnp.float32),
            in_specs=[anywhere, anywhere, anywhere, anywhere],
            out_specs=anywhere,
            scratch_shapes=[
                pltpu.SMEM(sched.shape, jnp.int32),
                pltpu.VMEM(refl.shape, jnp.float32),
                pltpu.VMEM(tfac.shape, jnp.float32),
                pltpu.VMEM((2, *eigvec.shape), jnp.float32),
                pltpu.VMEM((steps, n, piece, W), jnp.float32),
                pltpu.VMEM((steps, piece, W), jnp.float32),
                pltpu.VMEM((*two, W, evcount), jnp.float32),
                pltpu.VMEM((*two, W, evcount), jnp.float32),
                pltpu.VMEM((2, W, evcount), jnp.float32),
                dma((3,)),
                dma,
                dma((18,)),
                dma((32,)),
                pltpu.SemaphoreType.REGULAR,
            ],
            compiler_params=pltpu.CompilerParams(
                collective_id=0, has_side_effects=True, vmem_limit_bytes=60 << 20
            ),
            name="sweep",
        )(sched, refl, tfac, eigvec)
    owner = lax.axis_index("col") * v_rows // B
    slots = lax.dynamic_index_in_dim(sched, owner, 0, keepdims=False)
    packed = pl.pallas_call(
        pick_kernel,
        out_shape=jax.ShapeDtypeStruct((steps, piece, W), jnp.float32),
        in_specs=[pl.BlockSpec(memory_space=pltpu.SMEM), anywhere, anywhere],
        out_specs=anywhere,
        scratch_shapes=[
            pltpu.VMEM((steps, piece, W), jnp.float32),
            pltpu.SemaphoreType.DMA((steps, 2)),
            pltpu.SemaphoreType.DMA((steps,)),
        ],
        name="pick",
    )(slots, refl, tfac)
    return pl.pallas_call(
        functools.partial(main_kernel, n, rows_n, groups),
        out_shape=jax.ShapeDtypeStruct(eigvec.shape, jnp.float32),
        in_specs=[anywhere, anywhere],
        out_specs=anywhere,
        scratch_shapes=[
            pltpu.VMEM(eigvec.shape, jnp.float32),
            pltpu.VMEM((steps, n, piece, W), jnp.float32),
            pltpu.VMEM((half_steps, W, evcount), jnp.float32),
            pltpu.VMEM((half_steps, W, evcount), jnp.float32),
            pltpu.VMEM((half_steps, W, evcount), jnp.float32),
            pltpu.SemaphoreType.DMA((steps,)),
            pltpu.SemaphoreType.DMA,
            pltpu.SemaphoreType.DMA,
            pltpu.SemaphoreType.DMA((steps, 2, hops, 2)),
            pltpu.SemaphoreType.DMA((steps, 2, hops, 2)),
            pltpu.SemaphoreType.DMA((half_steps,)),
            pltpu.SemaphoreType.DMA((half_steps,)),
            pltpu.SemaphoreType.DMA((half_steps,)),
            pltpu.SemaphoreType.DMA((half_steps,)),
        ],
        compiler_params=pltpu.CompilerParams(
            collective_id=0, has_side_effects=True, vmem_limit_bytes=48 << 20
        ),
        name="sweep",
    )(packed, eigvec)


def solution(mesh):
    placed = (
        P("row", "col"),
        P(None, ("row", "col"), None),
        P(None, ("row", "col"), None),
        P("row", None),
    )
    body = functools.partial(on_device, mesh.shape["col"], mesh.shape["row"])
    return jax.shard_map(body, mesh=mesh, in_specs=placed, out_specs=P("row", "col"), check_vma=False)
```

```python
import functools

import jax
import jax.numpy as jnp
from jax import lax
from jax.experimental import pallas as pl
from jax.experimental.pallas import tpu as pltpu
from jax.sharding import PartitionSpec as P

B = 512
W = 256
MESH = pl.DeviceIdType.MESH


def split(x):
    high = x.astype(jnp.bfloat16)
    low = (x - high.astype(jnp.float32)).astype(jnp.bfloat16)
    return high, low


def product(left, right, dims):
    def one(a, b):
        return lax.dot_general(a, b, (dims, ((), ())), preferred_element_type=jnp.float32)

    return one(left[0], right[0]) + (one(left[0], right[1]) + one(left[1], right[0]))


def pick_kernel(slots, refl, tfac, packed, hold, in_sem, out_sem):
    steps = packed.shape[0]
    v_rows = refl.shape[1]
    t_rows = tfac.shape[1]
    loads, stores = [], []
    for s in range(steps):
        slot = slots[s]
        loads.append(
            (
                pltpu.make_async_copy(refl.at[slot], hold.at[s, pl.ds(0, v_rows)], in_sem.at[s, 0]),
                pltpu.make_async_copy(tfac.at[slot], hold.at[s, pl.ds(v_rows, t_rows)], in_sem.at[s, 1]),
            )
        )
        stores.append(pltpu.make_async_copy(hold.at[s], packed.at[s], out_sem.at[s]))
    for pair in loads:
        for copy in pair:
            copy.start()
    for pair, store in zip(loads, stores):
        for copy in pair:
            copy.wait()
        store.start()
    for store in stores:
        store.wait()


def main_kernel(n, rows_n, groups, packed, eig, out, field, buf, inb, back, landed, own_sem, eig_sem, out_sem,
                ring_send, ring_recv, up_send, up_recv, down_send, down_recv):
    steps, piece, _ = packed.shape
    v_rows = groups * B // n
    per_group = n // groups
    half = piece // 2
    hops = n // 2
    row = lax.axis_index("row")
    col = lax.axis_index("col")
    right = lax.rem(col + 1, n)
    left = lax.rem(col + n - 1, n)
    has_down = row < rows_n - 1
    has_up = row > 0
    down = jnp.minimum(row + 1, rows_n - 1)
    up = jnp.maximum(row - 1, 0)

    eig_copy = pltpu.make_async_copy(eig, field, eig_sem)
    eig_copy.start()

    barrier = pltpu.get_barrier_semaphore()
    pl.semaphore_signal(barrier, inc=1, device_id=(row, left), device_id_type=MESH)
    pl.semaphore_signal(barrier, inc=1, device_id=(row, right), device_id_type=MESH)

    @pl.when(has_up)
    def _():
        pl.semaphore_signal(barrier, inc=1, device_id=(up, col), device_id_type=MESH)

    @pl.when(has_down)
    def _():
        pl.semaphore_signal(barrier, inc=1, device_id=(down, col), device_id_type=MESH)

    pl.semaphore_wait(barrier, 2 + jnp.minimum(row, 1) + jnp.minimum(rows_n - 1 - row, 1))

    def ring_copy(s, way, hop, part):
        target = right if way == 0 else left
        owner = lax.rem(col + n - hop, n) if way == 0 else lax.rem(col + hop, n)
        span = pl.ds(part * half, half)
        src = packed.at[s, span] if hop == 0 else buf.at[s, owner, span]
        return pltpu.make_async_remote_copy(
            src_ref=src,
            dst_ref=buf.at[s, owner, span],
            send_sem=ring_send.at[s, way, hop, part],
            recv_sem=ring_recv.at[s, way, hop, part],
            device_id=(row, target),
            device_id_type=MESH,
        )

    def parts_of(way, hop):
        order = (0, 1) if way == 0 else (1, 0)
        return order[:1] if hop == hops - 1 else order

    def send_own(s):
        for k in range(len(parts_of(0, 0))):
            for way in (0, 1):
                ring_copy(s, way, 0, parts_of(way, 0)[k]).start()

    def forward(s):
        for hop in range(1, hops):
            for k in range(len(parts_of(0, hop))):
                for way in (0, 1):
                    part = parts_of(way, hop)[k]
                    ring_copy(s, way, hop - 1, part).wait_recv()
                    ring_copy(s, way, hop, part).start()

    def finish(s):
        for hop in range(hops):
            for way in (0, 1):
                done = parts_of(way, hop + 1) if hop + 1 < hops else ()
                for part in parts_of(way, hop):
                    if part not in done:
                        ring_copy(s, way, hop, part).wait_recv()

    def vectors_of(s, g):
        block = buf[s, g * per_group:(g + 1) * per_group, :v_rows]
        return split(block.reshape(B, W))

    def factor_of(s, g):
        block = buf[s, g * per_group:(g + 1) * per_group, v_rows:]
        return split(block.reshape(W, W))

    def coeffs_of(s, g, vectors, rows):
        coupling = product(vectors, split(rows), ((0,), (0,)))
        return split(product(factor_of(s, g), split(coupling), ((1,), (0,))))

    def apply_local(s, g, start):
        vectors = vectors_of(s, g)
        rows = field[start:start + B]
        coeffs = coeffs_of(s, g, vectors, rows)
        field[start:start + B] = rows - product(vectors, coeffs, ((1,), (0,)))

    def up_copy(i):
        return pltpu.make_async_remote_copy(
            src_ref=field.at[pl.ds(0, W)], dst_ref=inb.at[i],
            send_sem=up_send.at[i], recv_sem=up_recv.at[i],
            device_id=(up, col), device_id_type=MESH,
        )

    def down_copy(i):
        return pltpu.make_async_remote_copy(
            src_ref=back.at[i], dst_ref=landed.at[i],
            send_sem=down_send.at[i], recv_sem=down_recv.at[i],
            device_id=(down, col), device_id_type=MESH,
        )

    low = groups * B - W

    send_own(0)
    own = [pltpu.make_async_copy(packed.at[s], buf.at[s, col], own_sem.at[s]) for s in range(steps)]
    for copy in own:
        copy.start()
    eig_copy.wait()
    for s in range(steps):
        forward(s)
        if s + 1 < steps:
            send_own(s + 1)
        own[s].wait()
        finish(s)
        i = s // 2
        if s % 2 == 0:
            for g in range(groups):
                apply_local(s, g, g * B)
                if g == 0 and s + 1 < steps:
                    @pl.when(has_up)
                    def _():
                        up_copy(i).start()
        else:
            @pl.when(has_down)
            def _():
                up_copy(i).wait_recv()
                g = groups - 1
                vectors = vectors_of(s, g)
                rows = jnp.concatenate([field[low:], inb[i]], axis=0)
                coeffs = coeffs_of(s, g, vectors, rows)
                bottom = (vectors[0][W:], vectors[1][W:])
                back[i] = rows[W:] - product(bottom, coeffs, ((1,), (0,)))
                down_copy(i).start()
                top = (vectors[0][:W], vectors[1][:W])
                field[low:] = rows[:W] - product(top, coeffs, ((1,), (0,)))

            for g in range(groups - 1):
                apply_local(s, g, W + g * B)

            @pl.when(has_up)
            def _():
                up_copy(i).wait_send()
                down_copy(i).wait_recv()
                field[:W] = landed[i]

    store = pltpu.make_async_copy(field, out, out_sem)
    store.start()
    for s in range(steps):
        for way in (0, 1):
            for hop in range(hops):
                for part in parts_of(way, hop):
                    ring_copy(s, way, hop, part).wait_send()

    @pl.when(has_down)
    def _():
        for i in range(steps // 2):
            down_copy(i).wait_send()

    store.wait()


def line_kernel(rows_n, sched_all, refl, tfac, eig, out, sched, refl_in, tfac_in, field, buf, fed, inb, back, landed,
                local, eig_sem, sends, recvs, turn_sem):
    steps, v_rows, _ = refl.shape
    low = B + W
    last = steps - 1
    row = lax.axis_index("row")
    col = lax.axis_index("col")
    odd = lax.rem(row, 2)
    inner = (col == 1) | (col == 2)
    partner = col + 1 - 2 * lax.rem(col, 2)
    other = 3 - col
    mate = row + 1 - 2 * odd
    beyond = row - 1 + 2 * odd
    has_beyond = (beyond >= 0) & (beyond < rows_n)
    beyond = jnp.clip(beyond, 0, rows_n - 1)
    early = odd == 0
    late = odd == 1
    has_down = row < rows_n - 1
    has_up = row > 0
    down = jnp.minimum(row + 1, rows_n - 1)
    up = jnp.maximum(row - 1, 0)

    def remote(src, dst, send, recv, target):
        return pltpu.make_async_remote_copy(
            src_ref=src, dst_ref=dst, send_sem=send, recv_sem=recv,
            device_id=target, device_id_type=MESH,
        )

    refl_load = pltpu.make_async_copy(refl, refl_in, local.at[0])
    tfac_load = pltpu.make_async_copy(tfac, tfac_in, local.at[1])
    eig_load = pltpu.make_async_copy(eig, field.at[0], eig_sem)
    sched_load = pltpu.make_async_copy(sched_all, sched, local.at[2])
    sched_load.start()
    refl_load.start()
    tfac_load.start()

    barrier = pltpu.get_barrier_semaphore()

    def greet(target):
        pl.semaphore_signal(barrier, inc=1, device_id=target, device_id_type=MESH)

    greet((row, partner))
    greet((mate, partner))
    greet((mate, col))

    @pl.when(has_beyond)
    def _():
        greet((beyond, col))
        greet((beyond, partner))

    @pl.when(inner)
    def _():
        greet((row, other))
        greet((mate, other))

    sched_load.wait()
    refl_load.wait()
    tfac_load.wait()

    def pick(s):
        slot = sched[col // 2, s]
        buf[s, col, :v_rows] = refl_in[slot]
        buf[s, col, v_rows:] = tfac_in[slot]

    pick(0)

    pl.semaphore_wait(barrier, 3 + 2 * has_beyond.astype(jnp.int32) + 2 * inner.astype(jnp.int32))

    cuts = (3, 1, 1, 3)
    piece = buf.shape[2]

    def span(s, k):
        size = piece // cuts[s]
        return pl.ds((k + 2) % 3 * size if s == last else k * size, size)

    def feed(s, k):
        slot = sum(cuts[:s]) + k
        return remote(buf.at[s, col, span(s, k)], fed.at[s, span(s, k)],
                      sends.at[1 + k if s == last else 0], recvs.at[slot], (mate, partner))

    def feeds():
        return remote(buf.at[pl.ds(0, last), col], fed.at[pl.ds(0, last)], sends.at[0], recvs.at[0], (mate, partner))

    column_rows = ((0, B), (B, W), (B + W, W))

    def columns(g):
        rows = pl.ds(*column_rows[g])
        return remote(eig.at[rows], field.at[1, rows], sends.at[4 + g], recvs.at[8 + g], (row, partner))

    lead = piece // 3

    def own(s):
        return remote(buf.at[s, col], buf.at[s, col], sends.at[0], recvs.at[11 + s], (row, other))

    def own_arrival(s):
        return remote(buf.at[s, other], buf.at[s, other], sends.at[0], recvs.at[11 + s], (row, other))

    def own_last(k, owner):
        part = buf.at[last, owner, (pl.ds(lead, piece - lead), pl.ds(0, lead))[k]]
        return remote(part, part, sends.at[0], recvs.at[(11 + last, 30)[k]], (row, other))

    def send_last():
        own_last(0, col).start()
        own_last(1, col).start()

    def own_all():
        return remote(buf.at[:, col], buf.at[:, col], sends.at[0], recvs.at[11], (row, other))

    def relay(s, k):
        return remote(fed.at[s, span(s, k)], buf.at[s, partner, span(s, k)],
                      sends.at[1], recvs.at[31 if s == last and k == 2 else 15 + s], (mate, other))

    def relay_end():
        rows = pl.ds(lead, lead)
        return remote(fed.at[last, rows], buf.at[last, 3 - partner, rows],
                      sends.at[1], recvs.at[31], (mate, other))

    def relay_lead():
        rows = pl.ds(0, 2 * lead)
        return remote(fed.at[last, rows], buf.at[last, 3 - partner, rows],
                      sends.at[1], recvs.at[15 + last], (mate, other))

    def relay_arrival(s):
        return remote(fed.at[s], buf.at[s, 3 - partner], sends.at[1], recvs.at[15 + s], (mate, other))

    def relay_all():
        return remote(fed, buf.at[:, partner], sends.at[1], recvs.at[15], (mate, other))

    def hand(s, k):
        return remote(fed.at[s, span(s, k)], buf.at[s, partner, span(s, k)],
                      sends.at[2], recvs.at[19 + s], (mate, col))

    def hand_arrival(s):
        return remote(fed.at[s], buf.at[s, partner], sends.at[2], recvs.at[19 + s], (mate, col))

    def hand_all():
        return remote(fed, buf.at[:, partner], sends.at[2], recvs.at[19], (mate, col))

    def result(part, src, target_row):
        rows = (pl.ds(0, W), pl.ds(W, B), pl.ds(low, W))[part]
        return remote(src, out.at[rows], sends.at[10 + part], recvs.at[5 + part], (target_row, partner))

    def vectors_of(s, g):
        return split(buf[s, 2 * g:2 * g + 2, :v_rows].reshape(B, W))

    def factor_of(s, g):
        return split(buf[s, 2 * g:2 * g + 2, v_rows:].reshape(W, W))

    def coeffs_of(vectors, factor, rows):
        coupling = product(vectors, split(rows), ((0,), (0,)))
        return split(product(factor, split(coupling), ((1,), (0,))))

    def load(zs, start, size):
        return jnp.concatenate([field[z, start:start + size] for z in zs], axis=1)

    def save(zs, start, value):
        cols = value.shape[1] // len(zs)
        for k, z in enumerate(zs):
            field[z, start:start + value.shape[0]] = value[:, k * cols:(k + 1) * cols]

    def apply_local(s, g, zs, start):
        vectors = vectors_of(s, g)
        rows = load(zs, start, B)
        coeffs = coeffs_of(vectors, factor_of(s, g), rows)
        save(zs, start, rows - product(vectors, coeffs, ((1,), (0,))))

    def up_copy(i, z):
        return remote(field.at[z, pl.ds(0, W)], inb.at[i, z], sends.at[3 + 2 * i + z], recvs.at[23 + 2 * i + z], (up, col))

    def down_copy(z):
        return remote(back.at[0, z], landed.at[z], sends.at[7 + z], recvs.at[27 + z], (down, col))

    def down_final():
        return remote(back.at[1, 0], out.at[pl.ds(0, W)], sends.at[9], recvs.at[29], (down, col))

    def send_up(s, zs):
        @pl.when(has_up)
        def _():
            for z in zs:
                up_copy(s // 2, z).start()

    def straddle_body(s, zs, send):
        i = s // 2
        vectors = vectors_of(s, 1)
        below = jnp.concatenate([inb[i, z] for z in zs], axis=1)
        rows = jnp.concatenate([load(zs, low, W), below], axis=0)
        coeffs = coeffs_of(vectors, factor_of(s, 1), rows)
        bottom = (vectors[0][W:], vectors[1][W:])
        value = rows[W:] - product(bottom, coeffs, ((1,), (0,)))
        cols = value.shape[1] // len(zs)
        for k, z in enumerate(zs):
            back[i, z] = value[:, k * cols:(k + 1) * cols]
        send()
        top = (vectors[0][:W], vectors[1][:W])
        save(zs, low, rows[:W] - product(top, coeffs, ((1,), (0,))))

    def straddle(s, zs, send):
        @pl.when(has_down)
        def _():
            for z in zs:
                up_copy(s // 2, z).wait_recv()
            straddle_body(s, zs, send)

    def settle(z):
        @pl.when(has_up)
        def _():
            up_copy(0, z).wait_send()
            down_copy(z).wait_recv()
            field[z, :W] = landed[z]

    def pass_chunk(s, k):
        feed(s, k).wait_recv()
        relay(s, k).start()
        hand(s, k).start()

    def passed(s):
        for k in range(cuts[s]):
            pass_chunk(s, k)

    def near(s):
        hand_arrival(s).wait_recv()

    def far(s):
        own_arrival(s).wait_recv()
        relay_arrival(s).wait_recv()

    def far_lead():
        own_last(0, other).wait_recv()
        relay_lead().wait_recv()

    def far_end():
        own_last(1, other).wait_recv()
        relay_end().wait_recv()

    def store(part):
        rows = (pl.ds(0, W), pl.ds(W, B), pl.ds(low, W))[part]
        return pltpu.make_async_copy(field.at[0, rows], out.at[rows], local.at[part])

    top_row = (col < 2) & (row == 0)
    share_slot = {last: 0, 0: 1, 2: 2}

    def share(s):
        part = buf.at[s, col]
        return remote(part, part, sends.at[13 + share_slot[s]], recvs.at[share_slot[s]], (row, partner))

    def share_arrival(s):
        part = buf.at[s, partner]
        return remote(part, part, sends.at[13 + share_slot[s]], recvs.at[share_slot[s]], (row, partner))

    def half_result(part, half):
        start = (0, None, low)[part] + half * lead
        src = back.at[1, 1, pl.ds(half * lead, lead)] if part == 0 else field.at[1, pl.ds(start, lead)]
        return remote(src, out.at[pl.ds(start, lead)], sends.at[10 + part], recvs.at[5 + part],
                      (down if part == 0 else row, partner))

    def rows_of(owner, start):
        return split(buf[last, owner, start:start + lead])

    def joined(a, b):
        return jnp.concatenate([a[0], b[0]], axis=0), jnp.concatenate([a[1], b[1]], axis=0)

    def late_straddle():
        far_lead()

        @pl.when(jnp.logical_not(has_down))
        def _():
            far_end()
            half_result(2, 0).start()
            half_result(2, 1).start()

        @pl.when(has_down)
        def _():
            up_copy(1, 1).wait_recv()
            factor = factor_of(last, 1)
            inside = joined(rows_of(2, lead), rows_of(3, 0))
            rows_in = jnp.concatenate([field[1, low + lead:low + W], inb[1, 1, :lead]], axis=0)
            rows_out = jnp.concatenate([field[1, low:low + lead], inb[1, 1, lead:]], axis=0)
            part = product(inside, split(rows_in), ((0,), (0,)))
            scaled = split(product(inside, factor, ((1,), (0,))))
            far_end()
            outside = joined(rows_of(2, 0), rows_of(3, lead))
            coupling = split(part + product(outside, split(rows_out), ((0,), (0,))))
            value = rows_in - product(scaled, coupling, ((1,), (0,)))
            back[1, 1, :lead] = value[lead:]
            field[1, low + lead:low + W] = value[:lead]

            @pl.when(row != 1)
            def _():
                half_result(0, 0).start()

            half_result(2, 1).start()
            ends = split(product(outside, factor, ((1,), (0,))))
            value = rows_out - product(ends, coupling, ((1,), (0,)))
            back[1, 1, lead:] = value[lead:]
            field[1, low:low + lead] = value[:lead]

            @pl.when(row == 1)
            def _():
                half_result(2, 0).start()
                half_result(0, 0).start()
                half_result(0, 1).start()

            @pl.when(row != 1)
            def _():
                half_result(0, 1).start()
                half_result(2, 0).start()

    def state(part, start):
        rows = pl.ds(start, W)
        return remote(field.at[1, rows], field.at[0, rows], sends.at[16 + part], recvs.at[3 + part], (row, partner))

    def state_up():
        return remote(field.at[1, pl.ds(0, W)], inb.at[1, 0], sends.at[17], recvs.at[4], (up, partner))

    def bottom_result():
        return remote(back.at[1, 0], out.at[pl.ds(0, W)], sends.at[10], recvs.at[5], (down, col))

    @pl.when(jnp.logical_not(inner))
    def _():
        def turn():
            pl.semaphore_signal(turn_sem, inc=1, device_id=(mate, col), device_id_type=MESH)

        for k in range(last):
            if k > 0:
                pick(k)
            for c in range(cuts[k]):
                feed(k, c).start()
        columns(0).start()
        pick(last)

        def wait_turn():
            pl.semaphore_wait(turn_sem, 1)

        def last_feed():
            for c in range(cuts[last]):
                feed(last, c).start()

        @pl.when(late)
        def _():
            wait_turn()

        columns(1).start()
        columns(2).start()
        columns(1).wait_send()

        @pl.when(early)
        def _():
            turn()
            columns(2).wait_send()
            wait_turn()

        @pl.when(late)
        def _():
            columns(2).wait_send()
            turn()
            wait_turn()

        last_feed()
        feed(last, 0).wait_send()
        feed(last, 1).wait_send()

        @pl.when(early)
        def _():
            turn()

        feed(last, 2).wait_send()
        share_arrival(last).wait_recv()

        @pl.when(top_row)
        def _():
            share_arrival(0).wait_recv()
            share_arrival(2).wait_recv()
            top_load = pltpu.make_async_copy(eig.at[pl.ds(0, B)], field.at[1, pl.ds(0, B)], eig_sem)
            top_load.start()
            top_load.wait()
            apply_local(0, 0, (1,), 0)
            field[0, :W] = field[1, :W]
            state(1, W).wait_recv()
            apply_local(2, 0, (0,), 0)
            store(0).start()

        state(0, W).wait_recv()

        @pl.when(col == 0)
        def _():
            @pl.when(has_up)
            def _():
                state(1, W).wait_recv()

            apply_local(last, 0, (0,), W)
            store(1).start()

            @pl.when(has_up)
            def _():
                result(0, field.at[0, pl.ds(0, W)], row).wait_recv()

            @pl.when(jnp.logical_not(has_up))
            def _():
                store(0).wait()

            result(2, field.at[0, pl.ds(0, W)], row).wait_recv()
            store(1).wait()

        @pl.when(col == 3)
        def _():
            @pl.when(has_down)
            def _():
                state_up().wait_recv()
                straddle_body(last, (0,), lambda: bottom_result().start())

            store(2).start()
            result(0, field.at[0, pl.ds(0, W)], row).wait_recv()
            result(1, field.at[0, pl.ds(0, B)], row).wait_recv()
            store(2).wait()

            @pl.when(has_down)
            def _():
                bottom_result().wait_send()

        feeds().wait_send()
        columns(0).wait_send()

    @pl.when(inner)
    def _():
        own(0).start()
        eig_load.start()
        for s in range(1, steps):
            pick(s)
        passed(0)
        own(1).start()
        eig_load.wait()
        near(0)

        @pl.when(col == 1)
        def _():
            apply_local(0, 0, (0,), 0)
            send_up(0, (0,))

        @pl.when(col == 2)
        def _():
            apply_local(0, 1, (0,), B)

        passed(1)
        share(last).start()

        @pl.when(top_row)
        def _():
            share(0).start()
            share(2).start()


        @pl.when(early)
        def _():
            own(2).start()

        far(0)
        near(1)

        @pl.when(col == 1)
        def _():
            apply_local(0, 1, (0,), B)
            apply_local(1, 0, (0,), W)

        @pl.when(col == 2)
        def _():
            apply_local(0, 0, (0,), 0)
            send_up(0, (0,))
            straddle(1, (0,), lambda: down_copy(0).start())

        passed(2)

        @pl.when(early)
        def _():
            send_last()

        @pl.when(late)
        def _():
            own(2).start()

        far(1)

        @pl.when(col == 1)
        def _():
            straddle(1, (0,), lambda: down_copy(0).start())

        @pl.when(col == 2)
        def _():
            apply_local(1, 0, (0,), W)

        columns(0).wait_recv()
        apply_local(0, 0, (1,), 0)
        send_up(0, (1,))
        settle(0)
        near(2)

        @pl.when(col == 1)
        def _():
            apply_local(2, 0, (0,), 0)
            send_up(2, (0,))

        @pl.when(col == 2)
        def _():
            apply_local(2, 1, (0,), B)

        def far_even():
            @pl.when(col == 1)
            def _():
                apply_local(2, 1, (0,), B)

            @pl.when(col == 2)
            def _():
                apply_local(2, 0, (0,), 0)
                send_up(2, (0,))

        @pl.when(early)
        def _():
            far(2)
            far_even()

        columns(1).wait_recv()
        columns(2).wait_recv()
        apply_local(0, 1, (1,), B)
        straddle(1, (1,), lambda: down_copy(1).start())

        apply_local(1, 0, (1,), W)

        @pl.when(top_row)
        def _():
            state(1, W).start()

        @pl.when(late)
        def _():
            pass_chunk(3, 0)

        @pl.when(col == 2)
        def _():
            apply_local(2, 1, (1,), B)
            state(0, low).start()

        @pl.when(late)
        def _():
            far(2)

        @pl.when(col == 1)
        def _():
            apply_local(2, 1, (1,), B)
            state(0, B).start()


        @pl.when(late)
        def _():
            pass_chunk(3, 1)

        settle(1)

        @pl.when(late)
        def _():
            pass_chunk(3, 2)
            send_last()

        @pl.when(jnp.logical_not(top_row))
        def _():
            apply_local(2, 0, (1,), 0)

        @pl.when((col == 1) & has_up)
        def _():
            state(1, W).start()
            up_copy(1, 1).start()

        @pl.when((col == 2) & has_up)
        def _():
            state_up().start()


        @pl.when(early)
        def _():
            passed(3)


        @pl.when(late)
        def _():
            far_even()

        @pl.when(jnp.logical_not(has_up))
        def _():
            store(0).start()

        @pl.when((col == 2) & jnp.logical_not(has_up))
        def _():
            result(0, field.at[1, pl.ds(0, W)], row).start()

        def near_last():
            near(3)

            @pl.when(col == 1)
            def _():
                apply_local(last, 0, (0,), W)
                store(1).start()

            @pl.when(col == 2)
            def _():
                straddle(last, (0,), lambda: down_final().start())
                store(2).start()

        @pl.when(late)
        def _():
            near_last()

        @pl.when(early | (col == 2))
        def _():
            far_lead()
            far_end()

        @pl.when((col == 1) & early)
        def _():
            straddle(last, (1,), lambda: result(0, back.at[1, 1], down).start())
            result(2, field.at[1, pl.ds(low, W)], row).start()

        @pl.when((col == 1) & late)
        def _():
            late_straddle()

        @pl.when(col == 2)
        def _():
            apply_local(last, 0, (1,), W)
            result(1, field.at[1, pl.ds(W, B)], row).start()

        @pl.when(early)
        def _():
            near_last()

        @pl.when(col == 1)
        def _():
            straddle(last, (0,), lambda: down_final().start())
            store(2).start()

        @pl.when(col == 2)
        def _():
            apply_local(last, 0, (0,), W)
            store(1).start()

        share(last).wait_send()

        @pl.when(top_row)
        def _():
            share(0).wait_send()
            share(2).wait_send()

        state(0, W).wait_send()
        own_all().wait_send()
        relay_all().wait_send()
        hand_all().wait_send()

        @pl.when(has_up)
        def _():
            up_copy(last // 2, 0).wait_send()
            down_final().wait_recv()

        @pl.when(has_down)
        def _():
            down_copy(0).wait_send()
            down_copy(1).wait_send()
            down_final().wait_send()

        @pl.when(jnp.logical_not(has_up))
        def _():
            store(0).wait()

        @pl.when(col == 1)
        def _():
            state(1, W).wait_send()

            @pl.when(has_up)
            def _():
                up_copy(last // 2, 1).wait_send()

            @pl.when(has_down)
            def _():
                result(0, back.at[1, 1], down).wait_send()

            result(2, field.at[1, pl.ds(low, W)], row).wait_send()

        @pl.when(col == 2)
        def _():
            @pl.when(has_up)
            def _():
                state_up().wait_send()

            @pl.when(jnp.logical_not(has_up))
            def _():
                result(0, field.at[1, pl.ds(0, W)], row).wait_send()

            result(1, field.at[1, pl.ds(W, B)], row).wait_send()

        store(1).wait()
        store(2).wait()


def on_device(n, rows_n, eigvec, refl, tfac, sched):
    steps, v_rows, _ = refl.shape
    t_rows = tfac.shape[1]
    groups = sched.shape[0]
    evcount = eigvec.shape[1]
    piece = v_rows + t_rows
    hops = n // 2
    half_steps = steps // 2
    anywhere = pl.BlockSpec(memory_space=pl.ANY)
    if n == 4 and groups == 2 and steps == 4 and rows_n % 2 == 0:
        two = (half_steps, 2)
        dma = pltpu.SemaphoreType.DMA
        return pl.pallas_call(
            functools.partial(line_kernel, rows_n),
            out_shape=pltpu.VMEM(eigvec.shape, jnp.float32),
            in_specs=[anywhere, anywhere, anywhere, anywhere],
            out_specs=anywhere,
            scratch_shapes=[
                pltpu.SMEM(sched.shape, jnp.int32),
                pltpu.VMEM(refl.shape, jnp.float32),
                pltpu.VMEM(tfac.shape, jnp.float32),
                pltpu.VMEM((2, *eigvec.shape), jnp.float32),
                pltpu.VMEM((steps, n, piece, W), jnp.float32),
                pltpu.VMEM((steps, piece, W), jnp.float32),
                pltpu.VMEM((*two, W, evcount), jnp.float32),
                pltpu.VMEM((*two, W, evcount), jnp.float32),
                pltpu.VMEM((2, W, evcount), jnp.float32),
                dma((3,)),
                dma,
                dma((18,)),
                dma((32,)),
                pltpu.SemaphoreType.REGULAR,
            ],
            compiler_params=pltpu.CompilerParams(
                collective_id=0, has_side_effects=True, vmem_limit_bytes=60 << 20
            ),
            name="sweep",
        )(sched, refl, tfac, eigvec)
    owner = lax.axis_index("col") * v_rows // B
    slots = lax.dynamic_index_in_dim(sched, owner, 0, keepdims=False)
    packed = pl.pallas_call(
        pick_kernel,
        out_shape=jax.ShapeDtypeStruct((steps, piece, W), jnp.float32),
        in_specs=[pl.BlockSpec(memory_space=pltpu.SMEM), anywhere, anywhere],
        out_specs=anywhere,
        scratch_shapes=[
            pltpu.VMEM((steps, piece, W), jnp.float32),
            pltpu.SemaphoreType.DMA((steps, 2)),
            pltpu.SemaphoreType.DMA((steps,)),
        ],
        name="pick",
    )(slots, refl, tfac)
    return pl.pallas_call(
        functools.partial(main_kernel, n, rows_n, groups),
        out_shape=jax.ShapeDtypeStruct(eigvec.shape, jnp.float32),
        in_specs=[anywhere, anywhere],
        out_specs=anywhere,
        scratch_shapes=[
            pltpu.VMEM(eigvec.shape, jnp.float32),
            pltpu.VMEM((steps, n, piece, W), jnp.float32),
            pltpu.VMEM((half_steps, W, evcount), jnp.float32),
            pltpu.VMEM((half_steps, W, evcount), jnp.float32),
            pltpu.VMEM((half_steps, W, evcount), jnp.float32),
            pltpu.SemaphoreType.DMA((steps,)),
            pltpu.SemaphoreType.DMA,
            pltpu.SemaphoreType.DMA,
            pltpu.SemaphoreType.DMA((steps, 2, hops, 2)),
            pltpu.SemaphoreType.DMA((steps, 2, hops, 2)),
            pltpu.SemaphoreType.DMA((half_steps,)),
            pltpu.SemaphoreType.DMA((half_steps,)),
            pltpu.SemaphoreType.DMA((half_steps,)),
            pltpu.SemaphoreType.DMA((half_steps,)),
        ],
        compiler_params=pltpu.CompilerParams(
            collective_id=0, has_side_effects=True, vmem_limit_bytes=48 << 20
        ),
        name="sweep",
    )(packed, eigvec)


def solution(mesh):
    placed = (
        P("row", "col"),
        P(None, ("row", "col"), None),
        P(None, ("row", "col"), None),
        P("row", None),
    )
    body = functools.partial(on_device, mesh.shape["col"], mesh.shape["row"])
    return jax.shard_map(body, mesh=mesh, in_specs=placed, out_specs=P("row", "col"), check_vma=False)
```

```python
import functools

import jax
import jax.numpy as jnp
from jax import lax
from jax.experimental import pallas as pl
from jax.experimental.pallas import tpu as pltpu
from jax.sharding import PartitionSpec as P

B = 512
W = 256
MESH = pl.DeviceIdType.MESH


def split(x):
    high = x.astype(jnp.bfloat16)
    low = (x - high.astype(jnp.float32)).astype(jnp.bfloat16)
    return high, low


def product(left, right, dims):
    def one(a, b):
        return lax.dot_general(a, b, (dims, ((), ())), preferred_element_type=jnp.float32)

    return one(left[0], right[0]) + (one(left[0], right[1]) + one(left[1], right[0]))


def pick_kernel(slots, refl, tfac, packed, hold, in_sem, out_sem):
    steps = packed.shape[0]
    v_rows = refl.shape[1]
    t_rows = tfac.shape[1]
    loads, stores = [], []
    for s in range(steps):
        slot = slots[s]
        loads.append(
            (
                pltpu.make_async_copy(refl.at[slot], hold.at[s, pl.ds(0, v_rows)], in_sem.at[s, 0]),
                pltpu.make_async_copy(tfac.at[slot], hold.at[s, pl.ds(v_rows, t_rows)], in_sem.at[s, 1]),
            )
        )
        stores.append(pltpu.make_async_copy(hold.at[s], packed.at[s], out_sem.at[s]))
    for pair in loads:
        for copy in pair:
            copy.start()
    for pair, store in zip(loads, stores):
        for copy in pair:
            copy.wait()
        store.start()
    for store in stores:
        store.wait()


def main_kernel(n, rows_n, groups, packed, eig, out, field, buf, inb, back, landed, own_sem, eig_sem, out_sem,
                ring_send, ring_recv, up_send, up_recv, down_send, down_recv):
    steps, piece, _ = packed.shape
    v_rows = groups * B // n
    per_group = n // groups
    half = piece // 2
    hops = n // 2
    row = lax.axis_index("row")
    col = lax.axis_index("col")
    right = lax.rem(col + 1, n)
    left = lax.rem(col + n - 1, n)
    has_down = row < rows_n - 1
    has_up = row > 0
    down = jnp.minimum(row + 1, rows_n - 1)
    up = jnp.maximum(row - 1, 0)

    eig_copy = pltpu.make_async_copy(eig, field, eig_sem)
    eig_copy.start()

    barrier = pltpu.get_barrier_semaphore()
    pl.semaphore_signal(barrier, inc=1, device_id=(row, left), device_id_type=MESH)
    pl.semaphore_signal(barrier, inc=1, device_id=(row, right), device_id_type=MESH)

    @pl.when(has_up)
    def _():
        pl.semaphore_signal(barrier, inc=1, device_id=(up, col), device_id_type=MESH)

    @pl.when(has_down)
    def _():
        pl.semaphore_signal(barrier, inc=1, device_id=(down, col), device_id_type=MESH)

    pl.semaphore_wait(barrier, 2 + jnp.minimum(row, 1) + jnp.minimum(rows_n - 1 - row, 1))

    def ring_copy(s, way, hop, part):
        target = right if way == 0 else left
        owner = lax.rem(col + n - hop, n) if way == 0 else lax.rem(col + hop, n)
        span = pl.ds(part * half, half)
        src = packed.at[s, span] if hop == 0 else buf.at[s, owner, span]
        return pltpu.make_async_remote_copy(
            src_ref=src,
            dst_ref=buf.at[s, owner, span],
            send_sem=ring_send.at[s, way, hop, part],
            recv_sem=ring_recv.at[s, way, hop, part],
            device_id=(row, target),
            device_id_type=MESH,
        )

    def parts_of(way, hop):
        order = (0, 1) if way == 0 else (1, 0)
        return order[:1] if hop == hops - 1 else order

    def send_own(s):
        for k in range(len(parts_of(0, 0))):
            for way in (0, 1):
                ring_copy(s, way, 0, parts_of(way, 0)[k]).start()

    def forward(s):
        for hop in range(1, hops):
            for k in range(len(parts_of(0, hop))):
                for way in (0, 1):
                    part = parts_of(way, hop)[k]
                    ring_copy(s, way, hop - 1, part).wait_recv()
                    ring_copy(s, way, hop, part).start()

    def finish(s):
        for hop in range(hops):
            for way in (0, 1):
                done = parts_of(way, hop + 1) if hop + 1 < hops else ()
                for part in parts_of(way, hop):
                    if part not in done:
                        ring_copy(s, way, hop, part).wait_recv()

    def vectors_of(s, g):
        block = buf[s, g * per_group:(g + 1) * per_group, :v_rows]
        return split(block.reshape(B, W))

    def factor_of(s, g):
        block = buf[s, g * per_group:(g + 1) * per_group, v_rows:]
        return split(block.reshape(W, W))

    def coeffs_of(s, g, vectors, rows):
        coupling = product(vectors, split(rows), ((0,), (0,)))
        return split(product(factor_of(s, g), split(coupling), ((1,), (0,))))

    def apply_local(s, g, start):
        vectors = vectors_of(s, g)
        rows = field[start:start + B]
        coeffs = coeffs_of(s, g, vectors, rows)
        field[start:start + B] = rows - product(vectors, coeffs, ((1,), (0,)))

    def up_copy(i):
        return pltpu.make_async_remote_copy(
            src_ref=field.at[pl.ds(0, W)], dst_ref=inb.at[i],
            send_sem=up_send.at[i], recv_sem=up_recv.at[i],
            device_id=(up, col), device_id_type=MESH,
        )

    def down_copy(i):
        return pltpu.make_async_remote_copy(
            src_ref=back.at[i], dst_ref=landed.at[i],
            send_sem=down_send.at[i], recv_sem=down_recv.at[i],
            device_id=(down, col), device_id_type=MESH,
        )

    low = groups * B - W

    send_own(0)
    own = [pltpu.make_async_copy(packed.at[s], buf.at[s, col], own_sem.at[s]) for s in range(steps)]
    for copy in own:
        copy.start()
    eig_copy.wait()
    for s in range(steps):
        forward(s)
        if s + 1 < steps:
            send_own(s + 1)
        own[s].wait()
        finish(s)
        i = s // 2
        if s % 2 == 0:
            for g in range(groups):
                apply_local(s, g, g * B)
                if g == 0 and s + 1 < steps:
                    @pl.when(has_up)
                    def _():
                        up_copy(i).start()
        else:
            @pl.when(has_down)
            def _():
                up_copy(i).wait_recv()
                g = groups - 1
                vectors = vectors_of(s, g)
                rows = jnp.concatenate([field[low:], inb[i]], axis=0)
                coeffs = coeffs_of(s, g, vectors, rows)
                bottom = (vectors[0][W:], vectors[1][W:])
                back[i] = rows[W:] - product(bottom, coeffs, ((1,), (0,)))
                down_copy(i).start()
                top = (vectors[0][:W], vectors[1][:W])
                field[low:] = rows[:W] - product(top, coeffs, ((1,), (0,)))

            for g in range(groups - 1):
                apply_local(s, g, W + g * B)

            @pl.when(has_up)
            def _():
                up_copy(i).wait_send()
                down_copy(i).wait_recv()
                field[:W] = landed[i]

    store = pltpu.make_async_copy(field, out, out_sem)
    store.start()
    for s in range(steps):
        for way in (0, 1):
            for hop in range(hops):
                for part in parts_of(way, hop):
                    ring_copy(s, way, hop, part).wait_send()

    @pl.when(has_down)
    def _():
        for i in range(steps // 2):
            down_copy(i).wait_send()

    store.wait()


def line_kernel(rows_n, sched_all, refl, tfac, eig, out, sched, refl_in, tfac_in, field, buf, fed, inb, back, landed,
                local, eig_sem, sends, recvs, turn_sem):
    steps, v_rows, _ = refl.shape
    low = B + W
    last = steps - 1
    row = lax.axis_index("row")
    col = lax.axis_index("col")
    odd = lax.rem(row, 2)
    inner = (col == 1) | (col == 2)
    partner = col + 1 - 2 * lax.rem(col, 2)
    other = 3 - col
    mate = row + 1 - 2 * odd
    beyond = row - 1 + 2 * odd
    has_beyond = (beyond >= 0) & (beyond < rows_n)
    beyond = jnp.clip(beyond, 0, rows_n - 1)
    early = odd == 0
    late = odd == 1
    has_down = row < rows_n - 1
    has_up = row > 0
    down = jnp.minimum(row + 1, rows_n - 1)
    up = jnp.maximum(row - 1, 0)

    def remote(src, dst, send, recv, target):
        return pltpu.make_async_remote_copy(
            src_ref=src, dst_ref=dst, send_sem=send, recv_sem=recv,
            device_id=target, device_id_type=MESH,
        )

    refl_load = pltpu.make_async_copy(refl, refl_in, local.at[0])
    tfac_load = pltpu.make_async_copy(tfac, tfac_in, local.at[1])
    eig_load = pltpu.make_async_copy(eig, field.at[0], eig_sem)
    sched_load = pltpu.make_async_copy(sched_all, sched, local.at[2])
    sched_load.start()
    refl_load.start()
    tfac_load.start()

    barrier = pltpu.get_barrier_semaphore()

    def greet(target):
        pl.semaphore_signal(barrier, inc=1, device_id=target, device_id_type=MESH)

    greet((row, partner))
    greet((mate, partner))
    greet((mate, col))

    @pl.when(has_beyond)
    def _():
        greet((beyond, col))
        greet((beyond, partner))

    @pl.when(inner)
    def _():
        greet((row, other))
        greet((mate, other))

    sched_load.wait()
    refl_load.wait()
    tfac_load.wait()

    def pick(s):
        slot = sched[col // 2, s]
        buf[s, col, :v_rows] = refl_in[slot]
        buf[s, col, v_rows:] = tfac_in[slot]

    pick(0)

    pl.semaphore_wait(barrier, 3 + 2 * has_beyond.astype(jnp.int32) + 2 * inner.astype(jnp.int32))

    cuts = (2, 2, 1, 3)
    piece = buf.shape[2]

    def span(s, k):
        size = piece // cuts[s]
        return pl.ds((k + 2) % 3 * size if s == last else k * size, size)

    def feed(s, k):
        slot = sum(cuts[:s]) + k
        return remote(buf.at[s, col, span(s, k)], fed.at[s, span(s, k)],
                      sends.at[1 + k if s == last else 0], recvs.at[slot], (mate, partner))

    def feeds():
        return remote(buf.at[pl.ds(0, last), col], fed.at[pl.ds(0, last)], sends.at[0], recvs.at[0], (mate, partner))

    column_rows = ((0, B), (B, W), (B + W, W))

    def columns(g):
        rows = pl.ds(*column_rows[g])
        return remote(eig.at[rows], field.at[1, rows], sends.at[4 + g], recvs.at[8 + g], (row, partner))

    lead = piece // 3

    def own(s):
        return remote(buf.at[s, col], buf.at[s, col], sends.at[0], recvs.at[11 + s], (row, other))

    def own_arrival(s):
        return remote(buf.at[s, other], buf.at[s, other], sends.at[0], recvs.at[11 + s], (row, other))

    def own_last(k, owner):
        part = buf.at[last, owner, (pl.ds(lead, piece - lead), pl.ds(0, lead))[k]]
        return remote(part, part, sends.at[0], recvs.at[(11 + last, 30)[k]], (row, other))

    def send_last():
        own_last(0, col).start()
        own_last(1, col).start()

    def own_all():
        return remote(buf.at[:, col], buf.at[:, col], sends.at[0], recvs.at[11], (row, other))

    def relay(s, k):
        return remote(fed.at[s, span(s, k)], buf.at[s, partner, span(s, k)],
                      sends.at[1], recvs.at[31 if s == last and k == 2 else 15 + s], (mate, other))

    def relay_end():
        rows = pl.ds(lead, lead)
        return remote(fed.at[last, rows], buf.at[last, 3 - partner, rows],
                      sends.at[1], recvs.at[31], (mate, other))

    def relay_lead():
        rows = pl.ds(0, 2 * lead)
        return remote(fed.at[last, rows], buf.at[last, 3 - partner, rows],
                      sends.at[1], recvs.at[15 + last], (mate, other))

    def relay_arrival(s):
        return remote(fed.at[s], buf.at[s, 3 - partner], sends.at[1], recvs.at[15 + s], (mate, other))

    def relay_all():
        return remote(fed, buf.at[:, partner], sends.at[1], recvs.at[15], (mate, other))

    def hand(s, k):
        return remote(fed.at[s, span(s, k)], buf.at[s, partner, span(s, k)],
                      sends.at[2], recvs.at[19 + s], (mate, col))

    def hand_arrival(s):
        return remote(fed.at[s], buf.at[s, partner], sends.at[2], recvs.at[19 + s], (mate, col))

    def hand_all():
        return remote(fed, buf.at[:, partner], sends.at[2], recvs.at[19], (mate, col))

    def result(part, src, target_row):
        rows = (pl.ds(0, W), pl.ds(W, B), pl.ds(low, W))[part]
        return remote(src, out.at[rows], sends.at[10 + part], recvs.at[5 + part], (target_row, partner))

    def vectors_of(s, g):
        return split(buf[s, 2 * g:2 * g + 2, :v_rows].reshape(B, W))

    def factor_of(s, g):
        return split(buf[s, 2 * g:2 * g + 2, v_rows:].reshape(W, W))

    def coeffs_of(vectors, factor, rows):
        coupling = product(vectors, split(rows), ((0,), (0,)))
        return split(product(factor, split(coupling), ((1,), (0,))))

    def load(zs, start, size):
        return jnp.concatenate([field[z, start:start + size] for z in zs], axis=1)

    def save(zs, start, value):
        cols = value.shape[1] // len(zs)
        for k, z in enumerate(zs):
            field[z, start:start + value.shape[0]] = value[:, k * cols:(k + 1) * cols]

    def apply_local(s, g, zs, start):
        vectors = vectors_of(s, g)
        rows = load(zs, start, B)
        coeffs = coeffs_of(vectors, factor_of(s, g), rows)
        save(zs, start, rows - product(vectors, coeffs, ((1,), (0,))))

    def up_copy(i, z):
        return remote(field.at[z, pl.ds(0, W)], inb.at[i, z], sends.at[3 + z], recvs.at[23 + z], (up, col))

    def down_copy(z):
        return remote(back.at[0, z], landed.at[z], sends.at[7 + z], recvs.at[27 + z], (down, col))

    def down_final():
        return remote(back.at[1, 0], out.at[pl.ds(0, W)], sends.at[9], recvs.at[29], (down, col))

    def send_up(s, zs):
        @pl.when(has_up)
        def _():
            for z in zs:
                up_copy(s // 2, z).start()

    def straddle_body(s, zs, send):
        i = s // 2
        vectors = vectors_of(s, 1)
        below = jnp.concatenate([inb[i, z] for z in zs], axis=1)
        rows = jnp.concatenate([load(zs, low, W), below], axis=0)
        coeffs = coeffs_of(vectors, factor_of(s, 1), rows)
        bottom = (vectors[0][W:], vectors[1][W:])
        value = rows[W:] - product(bottom, coeffs, ((1,), (0,)))
        cols = value.shape[1] // len(zs)
        for k, z in enumerate(zs):
            back[i, z] = value[:, k * cols:(k + 1) * cols]
        send()
        top = (vectors[0][:W], vectors[1][:W])
        save(zs, low, rows[:W] - product(top, coeffs, ((1,), (0,))))

    def straddle(s, zs, send):
        @pl.when(has_down)
        def _():
            for z in zs:
                up_copy(s // 2, z).wait_recv()
            straddle_body(s, zs, send)

    def settle(z):
        @pl.when(has_up)
        def _():
            up_copy(0, z).wait_send()
            down_copy(z).wait_recv()
            field[z, :W] = landed[z]

    def pass_chunk(s, k):
        feed(s, k).wait_recv()
        relay(s, k).start()
        hand(s, k).start()

    def passed(s):
        for k in range(cuts[s]):
            pass_chunk(s, k)

    def near(s):
        hand_arrival(s).wait_recv()

    def far(s):
        own_arrival(s).wait_recv()
        relay_arrival(s).wait_recv()

    def far_lead():
        own_last(0, other).wait_recv()
        relay_lead().wait_recv()

    def far_end():
        own_last(1, other).wait_recv()
        relay_end().wait_recv()

    def store(part):
        rows = (pl.ds(0, W), pl.ds(W, B), pl.ds(low, W))[part]
        return pltpu.make_async_copy(field.at[0, rows], out.at[rows], local.at[part])

    top_row = (col < 2) & (row == 0)
    share_slot = {last: 0, 0: 1, 2: 2}

    def share(s):
        part = buf.at[s, col]
        return remote(part, part, sends.at[13 + share_slot[s]], recvs.at[share_slot[s]], (row, partner))

    def share_arrival(s):
        part = buf.at[s, partner]
        return remote(part, part, sends.at[13 + share_slot[s]], recvs.at[share_slot[s]], (row, partner))

    def half_result(part, half):
        start = (0, None, low)[part] + half * lead
        src = back.at[1, 1, pl.ds(half * lead, lead)] if part == 0 else field.at[1, pl.ds(start, lead)]
        return remote(src, out.at[pl.ds(start, lead)], sends.at[10 + part], recvs.at[5 + part],
                      (down if part == 0 else row, partner))

    def rows_of(owner, start):
        return split(buf[last, owner, start:start + lead])

    def joined(a, b):
        return jnp.concatenate([a[0], b[0]], axis=0), jnp.concatenate([a[1], b[1]], axis=0)

    def late_straddle():
        far_lead()

        @pl.when(jnp.logical_not(has_down))
        def _():
            far_end()
            half_result(2, 0).start()
            half_result(2, 1).start()

        @pl.when(has_down)
        def _():
            up_copy(1, 1).wait_recv()
            factor = factor_of(last, 1)
            inside = joined(rows_of(2, lead), rows_of(3, 0))
            rows_in = jnp.concatenate([field[1, low + lead:low + W], inb[1, 1, :lead]], axis=0)
            rows_out = jnp.concatenate([field[1, low:low + lead], inb[1, 1, lead:]], axis=0)
            part = product(inside, split(rows_in), ((0,), (0,)))
            scaled = split(product(inside, factor, ((1,), (0,))))
            far_end()
            outside = joined(rows_of(2, 0), rows_of(3, lead))
            coupling = split(part + product(outside, split(rows_out), ((0,), (0,))))
            value = rows_in - product(scaled, coupling, ((1,), (0,)))
            back[1, 1, :lead] = value[lead:]
            field[1, low + lead:low + W] = value[:lead]

            @pl.when(row != 1)
            def _():
                half_result(0, 0).start()

            half_result(2, 1).start()
            ends = split(product(outside, factor, ((1,), (0,))))
            value = rows_out - product(ends, coupling, ((1,), (0,)))
            back[1, 1, lead:] = value[lead:]
            field[1, low:low + lead] = value[:lead]

            @pl.when(row == 1)
            def _():
                half_result(2, 0).start()
                half_result(0, 0).start()
                half_result(0, 1).start()

            @pl.when(row != 1)
            def _():
                half_result(0, 1).start()
                half_result(2, 0).start()

    def state(part, start):
        rows = pl.ds(start, W)
        return remote(field.at[1, rows], field.at[0, rows], sends.at[16 + part], recvs.at[3 + part], (row, partner))

    def state_up():
        return remote(field.at[1, pl.ds(0, W)], inb.at[1, 0], sends.at[17], recvs.at[4], (up, partner))

    def bottom_result():
        return remote(back.at[1, 0], out.at[pl.ds(0, W)], sends.at[10], recvs.at[5], (down, col))

    @pl.when(jnp.logical_not(inner))
    def _():
        def turn():
            pl.semaphore_signal(turn_sem, inc=1, device_id=(mate, col), device_id_type=MESH)

        for k in range(last):
            if k > 0:
                pick(k)
            for c in range(cuts[k]):
                feed(k, c).start()
        columns(0).start()
        pick(last)

        def wait_turn():
            pl.semaphore_wait(turn_sem, 1)

        def last_feed():
            for c in range(cuts[last]):
                feed(last, c).start()

        @pl.when(late)
        def _():
            wait_turn()

        columns(1).start()
        columns(2).start()
        columns(1).wait_send()

        @pl.when(early)
        def _():
            turn()
            columns(2).wait_send()
            wait_turn()

        @pl.when(late)
        def _():
            columns(2).wait_send()
            turn()
            wait_turn()

        last_feed()
        feed(last, 0).wait_send()
        feed(last, 1).wait_send()

        @pl.when(early)
        def _():
            turn()

        feed(last, 2).wait_send()
        share_arrival(last).wait_recv()

        @pl.when(top_row)
        def _():
            share_arrival(0).wait_recv()
            share_arrival(2).wait_recv()
            top_load = pltpu.make_async_copy(eig.at[pl.ds(0, B)], field.at[1, pl.ds(0, B)], eig_sem)
            top_load.start()
            top_load.wait()
            apply_local(0, 0, (1,), 0)
            field[0, :W] = field[1, :W]
            state(1, W).wait_recv()
            apply_local(2, 0, (0,), 0)
            store(0).start()

        state(0, W).wait_recv()

        @pl.when(col == 0)
        def _():
            @pl.when(has_up)
            def _():
                state(1, W).wait_recv()

            apply_local(last, 0, (0,), W)
            store(1).start()

            @pl.when(has_up)
            def _():
                result(0, field.at[0, pl.ds(0, W)], row).wait_recv()

            @pl.when(jnp.logical_not(has_up))
            def _():
                store(0).wait()

            result(2, field.at[0, pl.ds(0, W)], row).wait_recv()
            store(1).wait()

        @pl.when(col == 3)
        def _():
            @pl.when(has_down)
            def _():
                state_up().wait_recv()
                straddle_body(last, (0,), lambda: bottom_result().start())

            store(2).start()
            result(0, field.at[0, pl.ds(0, W)], row).wait_recv()
            result(1, field.at[0, pl.ds(0, B)], row).wait_recv()
            store(2).wait()

            @pl.when(has_down)
            def _():
                bottom_result().wait_send()

        feeds().wait_send()
        columns(0).wait_send()

    @pl.when(inner)
    def _():
        own(0).start()
        eig_load.start()
        for s in range(1, steps):
            pick(s)
        passed(0)
        own(1).start()
        eig_load.wait()
        near(0)

        @pl.when(col == 1)
        def _():
            apply_local(0, 0, (0,), 0)
            send_up(0, (0,))

        @pl.when(col == 2)
        def _():
            apply_local(0, 1, (0,), B)

        passed(1)
        share(last).start()

        @pl.when(top_row)
        def _():
            share(0).start()
            share(2).start()


        @pl.when(early)
        def _():
            own(2).start()

        far(0)
        near(1)

        @pl.when(col == 1)
        def _():
            apply_local(0, 1, (0,), B)
            apply_local(1, 0, (0,), W)

        @pl.when(col == 2)
        def _():
            apply_local(0, 0, (0,), 0)
            send_up(0, (0,))
            straddle(1, (0,), lambda: down_copy(0).start())

        passed(2)

        @pl.when(early)
        def _():
            send_last()

        @pl.when(late)
        def _():
            own(2).start()

        far(1)

        @pl.when(col == 1)
        def _():
            straddle(1, (0,), lambda: down_copy(0).start())

        @pl.when(col == 2)
        def _():
            apply_local(1, 0, (0,), W)

        columns(0).wait_recv()
        apply_local(0, 0, (1,), 0)
        send_up(0, (1,))
        settle(0)
        near(2)

        @pl.when(col == 1)
        def _():
            apply_local(2, 0, (0,), 0)
            send_up(2, (0,))

        @pl.when(col == 2)
        def _():
            apply_local(2, 1, (0,), B)

        def far_even():
            @pl.when(col == 1)
            def _():
                apply_local(2, 1, (0,), B)

            @pl.when(col == 2)
            def _():
                apply_local(2, 0, (0,), 0)
                send_up(2, (0,))

        @pl.when(early)
        def _():
            far(2)
            far_even()

        columns(1).wait_recv()
        columns(2).wait_recv()
        apply_local(0, 1, (1,), B)
        straddle(1, (1,), lambda: down_copy(1).start())

        apply_local(1, 0, (1,), W)

        @pl.when(top_row)
        def _():
            state(1, W).start()

        @pl.when(late)
        def _():
            pass_chunk(3, 0)

        @pl.when(col == 2)
        def _():
            apply_local(2, 1, (1,), B)
            state(0, low).start()

        @pl.when(late)
        def _():
            far(2)

        @pl.when(col == 1)
        def _():
            apply_local(2, 1, (1,), B)
            state(0, B).start()


        @pl.when(late)
        def _():
            pass_chunk(3, 1)

        settle(1)

        @pl.when(late)
        def _():
            pass_chunk(3, 2)
            send_last()

        @pl.when(jnp.logical_not(top_row))
        def _():
            apply_local(2, 0, (1,), 0)

        @pl.when((col == 1) & has_up)
        def _():
            state(1, W).start()
            up_copy(1, 1).start()

        @pl.when((col == 2) & has_up)
        def _():
            state_up().start()


        @pl.when(early)
        def _():
            passed(3)


        @pl.when(late)
        def _():
            far_even()

        @pl.when(jnp.logical_not(has_up))
        def _():
            store(0).start()

        @pl.when((col == 2) & jnp.logical_not(has_up))
        def _():
            result(0, field.at[1, pl.ds(0, W)], row).start()

        def near_last():
            near(3)

            @pl.when(col == 1)
            def _():
                apply_local(last, 0, (0,), W)
                store(1).start()

            @pl.when(col == 2)
            def _():
                straddle(last, (0,), lambda: down_final().start())
                store(2).start()

        @pl.when(late)
        def _():
            near_last()

        @pl.when(early | (col == 2))
        def _():
            far_lead()
            far_end()

        @pl.when((col == 1) & early)
        def _():
            straddle(last, (1,), lambda: result(0, back.at[1, 1], down).start())
            result(2, field.at[1, pl.ds(low, W)], row).start()

        @pl.when((col == 1) & late)
        def _():
            late_straddle()

        @pl.when(col == 2)
        def _():
            apply_local(last, 0, (1,), W)
            result(1, field.at[1, pl.ds(W, B)], row).start()

        @pl.when(early)
        def _():
            near_last()

        @pl.when(col == 1)
        def _():
            straddle(last, (0,), lambda: down_final().start())
            store(2).start()

        @pl.when(col == 2)
        def _():
            apply_local(last, 0, (0,), W)
            store(1).start()

        share(last).wait_send()

        @pl.when(top_row)
        def _():
            share(0).wait_send()
            share(2).wait_send()

        state(0, W).wait_send()
        own_all().wait_send()
        relay_all().wait_send()
        hand_all().wait_send()

        @pl.when(has_up)
        def _():
            up_copy(last // 2, 0).wait_send()
            down_final().wait_recv()

        @pl.when(has_down)
        def _():
            down_copy(0).wait_send()
            down_copy(1).wait_send()
            down_final().wait_send()

        @pl.when(jnp.logical_not(has_up))
        def _():
            store(0).wait()

        @pl.when(col == 1)
        def _():
            state(1, W).wait_send()

            @pl.when(has_up)
            def _():
                up_copy(last // 2, 1).wait_send()

            @pl.when(has_down)
            def _():
                result(0, back.at[1, 1], down).wait_send()

            result(2, field.at[1, pl.ds(low, W)], row).wait_send()

        @pl.when(col == 2)
        def _():
            @pl.when(has_up)
            def _():
                state_up().wait_send()

            @pl.when(jnp.logical_not(has_up))
            def _():
                result(0, field.at[1, pl.ds(0, W)], row).wait_send()

            result(1, field.at[1, pl.ds(W, B)], row).wait_send()

        store(1).wait()
        store(2).wait()


def on_device(n, rows_n, eigvec, refl, tfac, sched):
    steps, v_rows, _ = refl.shape
    t_rows = tfac.shape[1]
    groups = sched.shape[0]
    evcount = eigvec.shape[1]
    piece = v_rows + t_rows
    hops = n // 2
    half_steps = steps // 2
    anywhere = pl.BlockSpec(memory_space=pl.ANY)
    if n == 4 and groups == 2 and steps == 4 and rows_n % 2 == 0:
        two = (half_steps, 2)
        dma = pltpu.SemaphoreType.DMA
        return pl.pallas_call(
            functools.partial(line_kernel, rows_n),
            out_shape=pltpu.VMEM(eigvec.shape, jnp.float32),
            in_specs=[anywhere, anywhere, anywhere, anywhere],
            out_specs=anywhere,
            scratch_shapes=[
                pltpu.SMEM(sched.shape, jnp.int32),
                pltpu.VMEM(refl.shape, jnp.float32),
                pltpu.VMEM(tfac.shape, jnp.float32),
                pltpu.VMEM((2, *eigvec.shape), jnp.float32),
                pltpu.VMEM((steps, n, piece, W), jnp.float32),
                pltpu.VMEM((steps, piece, W), jnp.float32),
                pltpu.VMEM((*two, W, evcount), jnp.float32),
                pltpu.VMEM((*two, W, evcount), jnp.float32),
                pltpu.VMEM((2, W, evcount), jnp.float32),
                dma((3,)),
                dma,
                dma((18,)),
                dma((32,)),
                pltpu.SemaphoreType.REGULAR,
            ],
            compiler_params=pltpu.CompilerParams(
                collective_id=0, has_side_effects=True, vmem_limit_bytes=60 << 20
            ),
            name="sweep",
        )(sched, refl, tfac, eigvec)
    owner = lax.axis_index("col") * v_rows // B
    slots = lax.dynamic_index_in_dim(sched, owner, 0, keepdims=False)
    packed = pl.pallas_call(
        pick_kernel,
        out_shape=jax.ShapeDtypeStruct((steps, piece, W), jnp.float32),
        in_specs=[pl.BlockSpec(memory_space=pltpu.SMEM), anywhere, anywhere],
        out_specs=anywhere,
        scratch_shapes=[
            pltpu.VMEM((steps, piece, W), jnp.float32),
            pltpu.SemaphoreType.DMA((steps, 2)),
            pltpu.SemaphoreType.DMA((steps,)),
        ],
        name="pick",
    )(slots, refl, tfac)
    return pl.pallas_call(
        functools.partial(main_kernel, n, rows_n, groups),
        out_shape=jax.ShapeDtypeStruct(eigvec.shape, jnp.float32),
        in_specs=[anywhere, anywhere],
        out_specs=anywhere,
        scratch_shapes=[
            pltpu.VMEM(eigvec.shape, jnp.float32),
            pltpu.VMEM((steps, n, piece, W), jnp.float32),
            pltpu.VMEM((half_steps, W, evcount), jnp.float32),
            pltpu.VMEM((half_steps, W, evcount), jnp.float32),
            pltpu.VMEM((half_steps, W, evcount), jnp.float32),
            pltpu.SemaphoreType.DMA((steps,)),
            pltpu.SemaphoreType.DMA,
            pltpu.SemaphoreType.DMA,
            pltpu.SemaphoreType.DMA((steps, 2, hops, 2)),
            pltpu.SemaphoreType.DMA((steps, 2, hops, 2)),
            pltpu.SemaphoreType.DMA((half_steps,)),
            pltpu.SemaphoreType.DMA((half_steps,)),
            pltpu.SemaphoreType.DMA((half_steps,)),
            pltpu.SemaphoreType.DMA((half_steps,)),
        ],
        compiler_params=pltpu.CompilerParams(
            collective_id=0, has_side_effects=True, vmem_limit_bytes=48 << 20
        ),
        name="sweep",
    )(packed, eigvec)


def solution(mesh):
    placed = (
        P("row", "col"),
        P(None, ("row", "col"), None),
        P(None, ("row", "col"), None),
        P("row", None),
    )
    body = functools.partial(on_device, mesh.shape["col"], mesh.shape["row"])
    return jax.shard_map(body, mesh=mesh, in_specs=placed, out_specs=P("row", "col"), check_vma=False)
```

```python
import functools

import jax
import jax.numpy as jnp
from jax import lax
from jax.experimental import pallas as pl
from jax.experimental.pallas import tpu as pltpu
from jax.sharding import PartitionSpec as P

B = 512
W = 256
MESH = pl.DeviceIdType.MESH


def split(x):
    high = x.astype(jnp.bfloat16)
    low = (x - high.astype(jnp.float32)).astype(jnp.bfloat16)
    return high, low


def product(left, right, dims):
    def one(a, b):
        return lax.dot_general(a, b, (dims, ((), ())), preferred_element_type=jnp.float32)

    return one(left[0], right[0]) + (one(left[0], right[1]) + one(left[1], right[0]))


def pick_kernel(slots, refl, tfac, packed, hold, in_sem, out_sem):
    steps = packed.shape[0]
    v_rows = refl.shape[1]
    t_rows = tfac.shape[1]
    loads, stores = [], []
    for s in range(steps):
        slot = slots[s]
        loads.append(
            (
                pltpu.make_async_copy(refl.at[slot], hold.at[s, pl.ds(0, v_rows)], in_sem.at[s, 0]),
                pltpu.make_async_copy(tfac.at[slot], hold.at[s, pl.ds(v_rows, t_rows)], in_sem.at[s, 1]),
            )
        )
        stores.append(pltpu.make_async_copy(hold.at[s], packed.at[s], out_sem.at[s]))
    for pair in loads:
        for copy in pair:
            copy.start()
    for pair, store in zip(loads, stores):
        for copy in pair:
            copy.wait()
        store.start()
    for store in stores:
        store.wait()


def main_kernel(n, rows_n, groups, packed, eig, out, field, buf, inb, back, landed, own_sem, eig_sem, out_sem,
                ring_send, ring_recv, up_send, up_recv, down_send, down_recv):
    steps, piece, _ = packed.shape
    v_rows = groups * B // n
    per_group = n // groups
    half = piece // 2
    hops = n // 2
    row = lax.axis_index("row")
    col = lax.axis_index("col")
    right = lax.rem(col + 1, n)
    left = lax.rem(col + n - 1, n)
    has_down = row < rows_n - 1
    has_up = row > 0
    down = jnp.minimum(row + 1, rows_n - 1)
    up = jnp.maximum(row - 1, 0)

    eig_copy = pltpu.make_async_copy(eig, field, eig_sem)
    eig_copy.start()

    barrier = pltpu.get_barrier_semaphore()
    pl.semaphore_signal(barrier, inc=1, device_id=(row, left), device_id_type=MESH)
    pl.semaphore_signal(barrier, inc=1, device_id=(row, right), device_id_type=MESH)

    @pl.when(has_up)
    def _():
        pl.semaphore_signal(barrier, inc=1, device_id=(up, col), device_id_type=MESH)

    @pl.when(has_down)
    def _():
        pl.semaphore_signal(barrier, inc=1, device_id=(down, col), device_id_type=MESH)

    pl.semaphore_wait(barrier, 2 + jnp.minimum(row, 1) + jnp.minimum(rows_n - 1 - row, 1))

    def ring_copy(s, way, hop, part):
        target = right if way == 0 else left
        owner = lax.rem(col + n - hop, n) if way == 0 else lax.rem(col + hop, n)
        span = pl.ds(part * half, half)
        src = packed.at[s, span] if hop == 0 else buf.at[s, owner, span]
        return pltpu.make_async_remote_copy(
            src_ref=src,
            dst_ref=buf.at[s, owner, span],
            send_sem=ring_send.at[s, way, hop, part],
            recv_sem=ring_recv.at[s, way, hop, part],
            device_id=(row, target),
            device_id_type=MESH,
        )

    def parts_of(way, hop):
        order = (0, 1) if way == 0 else (1, 0)
        return order[:1] if hop == hops - 1 else order

    def send_own(s):
        for k in range(len(parts_of(0, 0))):
            for way in (0, 1):
                ring_copy(s, way, 0, parts_of(way, 0)[k]).start()

    def forward(s):
        for hop in range(1, hops):
            for k in range(len(parts_of(0, hop))):
                for way in (0, 1):
                    part = parts_of(way, hop)[k]
                    ring_copy(s, way, hop - 1, part).wait_recv()
                    ring_copy(s, way, hop, part).start()

    def finish(s):
        for hop in range(hops):
            for way in (0, 1):
                done = parts_of(way, hop + 1) if hop + 1 < hops else ()
                for part in parts_of(way, hop):
                    if part not in done:
                        ring_copy(s, way, hop, part).wait_recv()

    def vectors_of(s, g):
        block = buf[s, g * per_group:(g + 1) * per_group, :v_rows]
        return split(block.reshape(B, W))

    def factor_of(s, g):
        block = buf[s, g * per_group:(g + 1) * per_group, v_rows:]
        return split(block.reshape(W, W))

    def coeffs_of(s, g, vectors, rows):
        coupling = product(vectors, split(rows), ((0,), (0,)))
        return split(product(factor_of(s, g), split(coupling), ((1,), (0,))))

    def apply_local(s, g, start):
        vectors = vectors_of(s, g)
        rows = field[start:start + B]
        coeffs = coeffs_of(s, g, vectors, rows)
        field[start:start + B] = rows - product(vectors, coeffs, ((1,), (0,)))

    def up_copy(i):
        return pltpu.make_async_remote_copy(
            src_ref=field.at[pl.ds(0, W)], dst_ref=inb.at[i],
            send_sem=up_send.at[i], recv_sem=up_recv.at[i],
            device_id=(up, col), device_id_type=MESH,
        )

    def down_copy(i):
        return pltpu.make_async_remote_copy(
            src_ref=back.at[i], dst_ref=landed.at[i],
            send_sem=down_send.at[i], recv_sem=down_recv.at[i],
            device_id=(down, col), device_id_type=MESH,
        )

    low = groups * B - W

    send_own(0)
    own = [pltpu.make_async_copy(packed.at[s], buf.at[s, col], own_sem.at[s]) for s in range(steps)]
    for copy in own:
        copy.start()
    eig_copy.wait()
    for s in range(steps):
        forward(s)
        if s + 1 < steps:
            send_own(s + 1)
        own[s].wait()
        finish(s)
        i = s // 2
        if s % 2 == 0:
            for g in range(groups):
                apply_local(s, g, g * B)
                if g == 0 and s + 1 < steps:
                    @pl.when(has_up)
                    def _():
                        up_copy(i).start()
        else:
            @pl.when(has_down)
            def _():
                up_copy(i).wait_recv()
                g = groups - 1
                vectors = vectors_of(s, g)
                rows = jnp.concatenate([field[low:], inb[i]], axis=0)
                coeffs = coeffs_of(s, g, vectors, rows)
                bottom = (vectors[0][W:], vectors[1][W:])
                back[i] = rows[W:] - product(bottom, coeffs, ((1,), (0,)))
                down_copy(i).start()
                top = (vectors[0][:W], vectors[1][:W])
                field[low:] = rows[:W] - product(top, coeffs, ((1,), (0,)))

            for g in range(groups - 1):
                apply_local(s, g, W + g * B)

            @pl.when(has_up)
            def _():
                up_copy(i).wait_send()
                down_copy(i).wait_recv()
                field[:W] = landed[i]

    store = pltpu.make_async_copy(field, out, out_sem)
    store.start()
    for s in range(steps):
        for way in (0, 1):
            for hop in range(hops):
                for part in parts_of(way, hop):
                    ring_copy(s, way, hop, part).wait_send()

    @pl.when(has_down)
    def _():
        for i in range(steps // 2):
            down_copy(i).wait_send()

    store.wait()


def line_kernel(rows_n, sched_all, refl, tfac, eig, out, sched, refl_in, tfac_in, field, buf, fed, inb, back, landed,
                local, eig_sem, sends, recvs, turn_sem):
    steps, v_rows, _ = refl.shape
    low = B + W
    last = steps - 1
    row = lax.axis_index("row")
    col = lax.axis_index("col")
    odd = lax.rem(row, 2)
    inner = (col == 1) | (col == 2)
    partner = col + 1 - 2 * lax.rem(col, 2)
    other = 3 - col
    mate = row + 1 - 2 * odd
    beyond = row - 1 + 2 * odd
    has_beyond = (beyond >= 0) & (beyond < rows_n)
    beyond = jnp.clip(beyond, 0, rows_n - 1)
    early = odd == 0
    late = odd == 1
    has_down = row < rows_n - 1
    has_up = row > 0
    down = jnp.minimum(row + 1, rows_n - 1)
    up = jnp.maximum(row - 1, 0)

    def remote(src, dst, send, recv, target):
        return pltpu.make_async_remote_copy(
            src_ref=src, dst_ref=dst, send_sem=send, recv_sem=recv,
            device_id=target, device_id_type=MESH,
        )

    refl_load = pltpu.make_async_copy(refl, refl_in, local.at[0])
    tfac_load = pltpu.make_async_copy(tfac, tfac_in, local.at[1])
    eig_load = pltpu.make_async_copy(eig, field.at[0], eig_sem)
    sched_load = pltpu.make_async_copy(sched_all, sched, local.at[2])
    sched_load.start()
    refl_load.start()
    tfac_load.start()

    barrier = pltpu.get_barrier_semaphore()

    def greet(target):
        pl.semaphore_signal(barrier, inc=1, device_id=target, device_id_type=MESH)

    greet((row, partner))
    greet((mate, partner))
    greet((mate, col))

    @pl.when(has_beyond)
    def _():
        greet((beyond, col))
        greet((beyond, partner))

    @pl.when(inner)
    def _():
        greet((row, other))
        greet((mate, other))

    sched_load.wait()
    refl_load.wait()
    tfac_load.wait()

    def pick(s):
        slot = sched[col // 2, s]
        buf[s, col, :v_rows] = refl_in[slot]
        buf[s, col, v_rows:] = tfac_in[slot]

    pick(0)

    pl.semaphore_wait(barrier, 3 + 2 * has_beyond.astype(jnp.int32) + 2 * inner.astype(jnp.int32))

    cuts = (2, 2, 1, 3)
    piece = buf.shape[2]

    def span(s, k):
        size = piece // cuts[s]
        return pl.ds((k + 2) % 3 * size if s == last else k * size, size)

    def feed(s, k):
        slot = sum(cuts[:s]) + k
        return remote(buf.at[s, col, span(s, k)], fed.at[s, span(s, k)],
                      sends.at[1 + k if s == last else 0], recvs.at[slot], (mate, partner))

    def feeds():
        return remote(buf.at[pl.ds(0, last), col], fed.at[pl.ds(0, last)], sends.at[0], recvs.at[0], (mate, partner))

    column_rows = ((0, B), (B, W), (B + W, W))

    def columns(g):
        rows = pl.ds(*column_rows[g])
        return remote(eig.at[rows], field.at[1, rows], sends.at[4 + g], recvs.at[8 + g], (row, partner))

    lead = piece // 3

    def own(s):
        return remote(buf.at[s, col], buf.at[s, col], sends.at[0], recvs.at[11 + s], (row, other))

    def own_arrival(s):
        return remote(buf.at[s, other], buf.at[s, other], sends.at[0], recvs.at[11 + s], (row, other))

    def own_last(k, owner):
        part = buf.at[last, owner, (pl.ds(lead, piece - lead), pl.ds(0, lead))[k]]
        return remote(part, part, sends.at[0], recvs.at[(11 + last, 25)[k]], (row, other))

    def send_last():
        own_last(0, col).start()
        own_last(1, col).start()

    def own_all():
        return remote(buf.at[:, col], buf.at[:, col], sends.at[0], recvs.at[11], (row, other))

    def relay(s, k):
        return remote(fed.at[s, span(s, k)], buf.at[s, partner, span(s, k)],
                      sends.at[1], recvs.at[26 if s == last and k == 2 else 15 + s], (mate, other))

    def relay_end():
        rows = pl.ds(lead, lead)
        return remote(fed.at[last, rows], buf.at[last, 3 - partner, rows],
                      sends.at[1], recvs.at[26], (mate, other))

    def relay_lead():
        rows = pl.ds(0, 2 * lead)
        return remote(fed.at[last, rows], buf.at[last, 3 - partner, rows],
                      sends.at[1], recvs.at[15 + last], (mate, other))

    def relay_arrival(s):
        return remote(fed.at[s], buf.at[s, 3 - partner], sends.at[1], recvs.at[15 + s], (mate, other))

    def relay_all():
        return remote(fed, buf.at[:, partner], sends.at[1], recvs.at[15], (mate, other))

    def hand(s, k):
        return remote(fed.at[s, span(s, k)], buf.at[s, partner, span(s, k)],
                      sends.at[2], recvs.at[19 + s], (mate, col))

    def hand_arrival(s):
        return remote(fed.at[s], buf.at[s, partner], sends.at[2], recvs.at[19 + s], (mate, col))

    def hand_all():
        return remote(fed, buf.at[:, partner], sends.at[2], recvs.at[19], (mate, col))

    def result(part, src, target_row):
        rows = (pl.ds(0, W), pl.ds(W, B), pl.ds(low, W))[part]
        return remote(src, out.at[rows], sends.at[10 + part], recvs.at[5 + part], (target_row, partner))

    def vectors_of(s, g):
        return split(buf[s, 2 * g:2 * g + 2, :v_rows].reshape(B, W))

    def factor_of(s, g):
        return split(buf[s, 2 * g:2 * g + 2, v_rows:].reshape(W, W))

    def coeffs_of(vectors, factor, rows):
        coupling = product(vectors, split(rows), ((0,), (0,)))
        return split(product(factor, split(coupling), ((1,), (0,))))

    def load(zs, start, size):
        return jnp.concatenate([field[z, start:start + size] for z in zs], axis=1)

    def save(zs, start, value):
        cols = value.shape[1] // len(zs)
        for k, z in enumerate(zs):
            field[z, start:start + value.shape[0]] = value[:, k * cols:(k + 1) * cols]

    def apply_local(s, g, zs, start):
        vectors = vectors_of(s, g)
        rows = load(zs, start, B)
        coeffs = coeffs_of(vectors, factor_of(s, g), rows)
        save(zs, start, rows - product(vectors, coeffs, ((1,), (0,))))

    def up_copy(i, z):
        return remote(field.at[z, pl.ds(0, W)], inb.at[i, z], sends.at[3 + z], recvs.at[23 + z], (up, col))

    def down_copy(z):
        return remote(back.at[0, z], landed.at[z], sends.at[7 + z], recvs.at[27 + z], (down, col))

    def down_final():
        return remote(back.at[1, 0], out.at[pl.ds(0, W)], sends.at[9], recvs.at[29], (down, col))

    def send_up(s, zs):
        @pl.when(has_up)
        def _():
            for z in zs:
                up_copy(s // 2, z).start()

    def straddle_body(s, zs, send):
        i = s // 2
        vectors = vectors_of(s, 1)
        below = jnp.concatenate([inb[i, z] for z in zs], axis=1)
        rows = jnp.concatenate([load(zs, low, W), below], axis=0)
        coeffs = coeffs_of(vectors, factor_of(s, 1), rows)
        bottom = (vectors[0][W:], vectors[1][W:])
        value = rows[W:] - product(bottom, coeffs, ((1,), (0,)))
        cols = value.shape[1] // len(zs)
        for k, z in enumerate(zs):
            back[i, z] = value[:, k * cols:(k + 1) * cols]
        send()
        top = (vectors[0][:W], vectors[1][:W])
        save(zs, low, rows[:W] - product(top, coeffs, ((1,), (0,))))

    def straddle(s, zs, send):
        @pl.when(has_down)
        def _():
            for z in zs:
                up_copy(s // 2, z).wait_recv()
            straddle_body(s, zs, send)

    def settle(z):
        @pl.when(has_up)
        def _():
            up_copy(0, z).wait_send()
            down_copy(z).wait_recv()
            field[z, :W] = landed[z]

    def pass_chunk(s, k):
        feed(s, k).wait_recv()
        relay(s, k).start()
        hand(s, k).start()

    def passed(s):
        for k in range(cuts[s]):
            pass_chunk(s, k)

    def near(s):
        hand_arrival(s).wait_recv()

    def far(s):
        own_arrival(s).wait_recv()
        relay_arrival(s).wait_recv()

    def far_lead():
        own_last(0, other).wait_recv()
        relay_lead().wait_recv()

    def far_end():
        own_last(1, other).wait_recv()
        relay_end().wait_recv()

    def store(part):
        rows = (pl.ds(0, W), pl.ds(W, B), pl.ds(low, W))[part]
        return pltpu.make_async_copy(field.at[0, rows], out.at[rows], local.at[part])

    top_row = (col < 2) & (row == 0)
    share_slot = {last: 0, 0: 1, 2: 2}

    def share(s):
        part = buf.at[s, col]
        return remote(part, part, sends.at[13 if s == last else 2 + share_slot[s]], recvs.at[share_slot[s]], (row, partner))

    def share_arrival(s):
        part = buf.at[s, partner]
        return remote(part, part, sends.at[13 if s == last else 2 + share_slot[s]], recvs.at[share_slot[s]], (row, partner))

    def half_result(part, half):
        start = (0, None, low)[part] + half * lead
        src = back.at[1, 1, pl.ds(half * lead, lead)] if part == 0 else field.at[1, pl.ds(start, lead)]
        return remote(src, out.at[pl.ds(start, lead)], sends.at[10 + part], recvs.at[5 + part],
                      (down if part == 0 else row, partner))

    def rows_of(owner, start):
        return split(buf[last, owner, start:start + lead])

    def joined(a, b):
        return jnp.concatenate([a[0], b[0]], axis=0), jnp.concatenate([a[1], b[1]], axis=0)

    def late_straddle():
        far_lead()

        @pl.when(jnp.logical_not(has_down))
        def _():
            far_end()
            half_result(2, 0).start()
            half_result(2, 1).start()

        @pl.when(has_down)
        def _():
            up_copy(1, 1).wait_recv()
            factor = factor_of(last, 1)
            inside = joined(rows_of(2, lead), rows_of(3, 0))
            rows_in = jnp.concatenate([field[1, low + lead:low + W], inb[1, 1, :lead]], axis=0)
            rows_out = jnp.concatenate([field[1, low:low + lead], inb[1, 1, lead:]], axis=0)
            part = product(inside, split(rows_in), ((0,), (0,)))
            scaled = split(product(inside, factor, ((1,), (0,))))
            far_end()
            outside = joined(rows_of(2, 0), rows_of(3, lead))
            coupling = split(part + product(outside, split(rows_out), ((0,), (0,))))
            value = rows_in - product(scaled, coupling, ((1,), (0,)))
            back[1, 1, :lead] = value[lead:]
            field[1, low + lead:low + W] = value[:lead]

            @pl.when(row != 1)
            def _():
                half_result(0, 0).start()

            half_result(2, 1).start()
            ends = split(product(outside, factor, ((1,), (0,))))
            value = rows_out - product(ends, coupling, ((1,), (0,)))
            back[1, 1, lead:] = value[lead:]
            field[1, low:low + lead] = value[:lead]

            @pl.when(row == 1)
            def _():
                half_result(2, 0).start()
                half_result(0, 0).start()
                half_result(0, 1).start()

            @pl.when(row != 1)
            def _():
                half_result(0, 1).start()
                half_result(2, 0).start()

    def state(part, start):
        rows = pl.ds(start, W)
        return remote(field.at[1, rows], field.at[0, rows], sends.at[5 + part], recvs.at[3 + part], (row, partner))

    def state_up():
        return remote(field.at[1, pl.ds(0, W)], inb.at[1, 0], sends.at[6], recvs.at[4], (up, partner))

    def bottom_result():
        return remote(back.at[1, 0], out.at[pl.ds(0, W)], sends.at[10], recvs.at[5], (down, col))

    @pl.when(jnp.logical_not(inner))
    def _():
        def turn():
            pl.semaphore_signal(turn_sem, inc=1, device_id=(mate, col), device_id_type=MESH)

        for k in range(last):
            if k > 0:
                pick(k)
            for c in range(cuts[k]):
                feed(k, c).start()
        columns(0).start()
        pick(last)

        def wait_turn():
            pl.semaphore_wait(turn_sem, 1)

        def last_feed():
            for c in range(cuts[last]):
                feed(last, c).start()

        @pl.when(late)
        def _():
            wait_turn()

        columns(1).start()
        columns(2).start()
        columns(1).wait_send()

        @pl.when(early)
        def _():
            turn()
            columns(2).wait_send()
            wait_turn()

        @pl.when(late)
        def _():
            columns(2).wait_send()
            turn()
            wait_turn()

        last_feed()
        feed(last, 0).wait_send()
        feed(last, 1).wait_send()

        @pl.when(early)
        def _():
            turn()

        feed(last, 2).wait_send()
        share_arrival(last).wait_recv()

        @pl.when(top_row)
        def _():
            share_arrival(0).wait_recv()
            share_arrival(2).wait_recv()
            top_load = pltpu.make_async_copy(eig.at[pl.ds(0, B)], field.at[1, pl.ds(0, B)], eig_sem)
            top_load.start()
            top_load.wait()
            apply_local(0, 0, (1,), 0)
            field[0, :W] = field[1, :W]
            state(1, W).wait_recv()
            apply_local(2, 0, (0,), 0)
            store(0).start()

        state(0, W).wait_recv()

        @pl.when(col == 0)
        def _():
            @pl.when(has_up)
            def _():
                state(1, W).wait_recv()

            apply_local(last, 0, (0,), W)
            store(1).start()

            @pl.when(has_up)
            def _():
                result(0, field.at[0, pl.ds(0, W)], row).wait_recv()

            @pl.when(jnp.logical_not(has_up))
            def _():
                store(0).wait()

            result(2, field.at[0, pl.ds(0, W)], row).wait_recv()
            store(1).wait()

        @pl.when(col == 3)
        def _():
            @pl.when(has_down)
            def _():
                state_up().wait_recv()
                straddle_body(last, (0,), lambda: bottom_result().start())

            store(2).start()
            result(0, field.at[0, pl.ds(0, W)], row).wait_recv()
            result(1, field.at[0, pl.ds(0, B)], row).wait_recv()
            store(2).wait()

            @pl.when(has_down)
            def _():
                bottom_result().wait_send()

        feeds().wait_send()
        columns(0).wait_send()

    @pl.when(inner)
    def _():
        own(0).start()
        eig_load.start()
        for s in range(1, steps):
            pick(s)
        passed(0)
        own(1).start()
        eig_load.wait()
        near(0)

        @pl.when(col == 1)
        def _():
            apply_local(0, 0, (0,), 0)
            send_up(0, (0,))

        @pl.when(col == 2)
        def _():
            apply_local(0, 1, (0,), B)

        passed(1)
        share(last).start()

        @pl.when(top_row)
        def _():
            share(0).start()
            share(2).start()


        @pl.when(early)
        def _():
            own(2).start()

        far(0)
        near(1)

        @pl.when(col == 1)
        def _():
            apply_local(0, 1, (0,), B)
            apply_local(1, 0, (0,), W)

        @pl.when(col == 2)
        def _():
            apply_local(0, 0, (0,), 0)
            send_up(0, (0,))
            straddle(1, (0,), lambda: down_copy(0).start())

        passed(2)

        @pl.when(early)
        def _():
            send_last()

        @pl.when(late)
        def _():
            own(2).start()

        far(1)

        @pl.when(col == 1)
        def _():
            straddle(1, (0,), lambda: down_copy(0).start())

        @pl.when(col == 2)
        def _():
            apply_local(1, 0, (0,), W)

        columns(0).wait_recv()
        apply_local(0, 0, (1,), 0)
        send_up(0, (1,))
        settle(0)
        near(2)

        @pl.when(col == 1)
        def _():
            apply_local(2, 0, (0,), 0)
            send_up(2, (0,))

        @pl.when(col == 2)
        def _():
            apply_local(2, 1, (0,), B)

        def far_even():
            @pl.when(col == 1)
            def _():
                apply_local(2, 1, (0,), B)

            @pl.when(col == 2)
            def _():
                apply_local(2, 0, (0,), 0)
                send_up(2, (0,))

        @pl.when(early)
        def _():
            far(2)
            far_even()

        columns(1).wait_recv()
        columns(2).wait_recv()
        apply_local(0, 1, (1,), B)
        straddle(1, (1,), lambda: down_copy(1).start())

        apply_local(1, 0, (1,), W)

        @pl.when(top_row)
        def _():
            state(1, W).start()

        @pl.when(late)
        def _():
            pass_chunk(3, 0)

        @pl.when(col == 2)
        def _():
            apply_local(2, 1, (1,), B)
            state(0, low).start()

        @pl.when(late)
        def _():
            far(2)

        @pl.when(col == 1)
        def _():
            apply_local(2, 1, (1,), B)
            state(0, B).start()


        @pl.when(late)
        def _():
            pass_chunk(3, 1)

        settle(1)

        @pl.when(late)
        def _():
            pass_chunk(3, 2)
            send_last()

        @pl.when(jnp.logical_not(top_row))
        def _():
            apply_local(2, 0, (1,), 0)

        @pl.when((col == 1) & has_up)
        def _():
            state(1, W).start()
            up_copy(1, 1).start()

        @pl.when((col == 2) & has_up)
        def _():
            state_up().start()


        @pl.when(early)
        def _():
            passed(3)


        @pl.when(late)
        def _():
            far_even()

        @pl.when(jnp.logical_not(has_up))
        def _():
            store(0).start()

        @pl.when((col == 2) & jnp.logical_not(has_up))
        def _():
            result(0, field.at[1, pl.ds(0, W)], row).start()

        def near_last():
            near(3)

            @pl.when(col == 1)
            def _():
                apply_local(last, 0, (0,), W)
                store(1).start()

            @pl.when(col == 2)
            def _():
                straddle(last, (0,), lambda: down_final().start())
                store(2).start()

        @pl.when(late)
        def _():
            near_last()

        @pl.when(early | (col == 2))
        def _():
            far_lead()
            far_end()

        @pl.when((col == 1) & early)
        def _():
            straddle(last, (1,), lambda: result(0, back.at[1, 1], down).start())
            result(2, field.at[1, pl.ds(low, W)], row).start()

        @pl.when((col == 1) & late)
        def _():
            late_straddle()

        @pl.when(col == 2)
        def _():
            apply_local(last, 0, (1,), W)
            result(1, field.at[1, pl.ds(W, B)], row).start()

        @pl.when(early)
        def _():
            near_last()

        @pl.when(col == 1)
        def _():
            straddle(last, (0,), lambda: down_final().start())
            store(2).start()

        @pl.when(col == 2)
        def _():
            apply_local(last, 0, (0,), W)
            store(1).start()

        share(last).wait_send()

        @pl.when(top_row)
        def _():
            share(0).wait_send()
            share(2).wait_send()

        state(0, W).wait_send()
        own_all().wait_send()
        relay_all().wait_send()
        hand_all().wait_send()

        @pl.when(has_up)
        def _():
            up_copy(last // 2, 0).wait_send()
            down_final().wait_recv()

        @pl.when(has_down)
        def _():
            down_copy(0).wait_send()
            down_copy(1).wait_send()
            down_final().wait_send()

        @pl.when(jnp.logical_not(has_up))
        def _():
            store(0).wait()

        @pl.when(col == 1)
        def _():
            state(1, W).wait_send()

            @pl.when(has_up)
            def _():
                up_copy(last // 2, 1).wait_send()

            @pl.when(has_down)
            def _():
                result(0, back.at[1, 1], down).wait_send()

            result(2, field.at[1, pl.ds(low, W)], row).wait_send()

        @pl.when(col == 2)
        def _():
            @pl.when(has_up)
            def _():
                state_up().wait_send()

            @pl.when(jnp.logical_not(has_up))
            def _():
                result(0, field.at[1, pl.ds(0, W)], row).wait_send()

            result(1, field.at[1, pl.ds(W, B)], row).wait_send()

        store(1).wait()
        store(2).wait()


def on_device(n, rows_n, eigvec, refl, tfac, sched):
    steps, v_rows, _ = refl.shape
    t_rows = tfac.shape[1]
    groups = sched.shape[0]
    evcount = eigvec.shape[1]
    piece = v_rows + t_rows
    hops = n // 2
    half_steps = steps // 2
    anywhere = pl.BlockSpec(memory_space=pl.ANY)
    if n == 4 and groups == 2 and steps == 4 and rows_n % 2 == 0:
        two = (half_steps, 2)
        dma = pltpu.SemaphoreType.DMA
        return pl.pallas_call(
            functools.partial(line_kernel, rows_n),
            out_shape=pltpu.VMEM(eigvec.shape, jnp.float32),
            in_specs=[anywhere, anywhere, anywhere, anywhere],
            out_specs=anywhere,
            scratch_shapes=[
                pltpu.SMEM(sched.shape, jnp.int32),
                pltpu.VMEM(refl.shape, jnp.float32),
                pltpu.VMEM(tfac.shape, jnp.float32),
                pltpu.VMEM((2, *eigvec.shape), jnp.float32),
                pltpu.VMEM((steps, n, piece, W), jnp.float32),
                pltpu.VMEM((steps, piece, W), jnp.float32),
                pltpu.VMEM((*two, W, evcount), jnp.float32),
                pltpu.VMEM((*two, W, evcount), jnp.float32),
                pltpu.VMEM((2, W, evcount), jnp.float32),
                dma((3,)),
                dma,
                dma((14,)),
                dma((30,)),
                pltpu.SemaphoreType.REGULAR,
            ],
            compiler_params=pltpu.CompilerParams(
                collective_id=0, has_side_effects=True, vmem_limit_bytes=60 << 20
            ),
            name="sweep",
        )(sched, refl, tfac, eigvec)
    owner = lax.axis_index("col") * v_rows // B
    slots = lax.dynamic_index_in_dim(sched, owner, 0, keepdims=False)
    packed = pl.pallas_call(
        pick_kernel,
        out_shape=jax.ShapeDtypeStruct((steps, piece, W), jnp.float32),
        in_specs=[pl.BlockSpec(memory_space=pltpu.SMEM), anywhere, anywhere],
        out_specs=anywhere,
        scratch_shapes=[
            pltpu.VMEM((steps, piece, W), jnp.float32),
            pltpu.SemaphoreType.DMA((steps, 2)),
            pltpu.SemaphoreType.DMA((steps,)),
        ],
        name="pick",
    )(slots, refl, tfac)
    return pl.pallas_call(
        functools.partial(main_kernel, n, rows_n, groups),
        out_shape=jax.ShapeDtypeStruct(eigvec.shape, jnp.float32),
        in_specs=[anywhere, anywhere],
        out_specs=anywhere,
        scratch_shapes=[
            pltpu.VMEM(eigvec.shape, jnp.float32),
            pltpu.VMEM((steps, n, piece, W), jnp.float32),
            pltpu.VMEM((half_steps, W, evcount), jnp.float32),
            pltpu.VMEM((half_steps, W, evcount), jnp.float32),
            pltpu.VMEM((half_steps, W, evcount), jnp.float32),
            pltpu.SemaphoreType.DMA((steps,)),
            pltpu.SemaphoreType.DMA,
            pltpu.SemaphoreType.DMA,
            pltpu.SemaphoreType.DMA((steps, 2, hops, 2)),
            pltpu.SemaphoreType.DMA((steps, 2, hops, 2)),
            pltpu.SemaphoreType.DMA((half_steps,)),
            pltpu.SemaphoreType.DMA((half_steps,)),
            pltpu.SemaphoreType.DMA((half_steps,)),
            pltpu.SemaphoreType.DMA((half_steps,)),
        ],
        compiler_params=pltpu.CompilerParams(
            collective_id=0, has_side_effects=True, vmem_limit_bytes=48 << 20
        ),
        name="sweep",
    )(packed, eigvec)


def solution(mesh):
    placed = (
        P("row", "col"),
        P(None, ("row", "col"), None),
        P(None, ("row", "col"), None),
        P("row", None),
    )
    body = functools.partial(on_device, mesh.shape["col"], mesh.shape["row"])
    return jax.shard_map(body, mesh=mesh, in_specs=placed, out_specs=P("row", "col"), check_vma=False)
```

```python
import functools

import jax
import jax.numpy as jnp
from jax import lax
from jax.experimental import pallas as pl
from jax.experimental.pallas import tpu as pltpu
from jax.sharding import PartitionSpec as P

B = 512
W = 256
MESH = pl.DeviceIdType.MESH


def split(x):
    high = x.astype(jnp.bfloat16)
    low = (x - high.astype(jnp.float32)).astype(jnp.bfloat16)
    return high, low


def product(left, right, dims):
    def one(a, b):
        return lax.dot_general(a, b, (dims, ((), ())), preferred_element_type=jnp.float32)

    return one(left[0], right[0]) + (one(left[0], right[1]) + one(left[1], right[0]))


def pick_kernel(slots, refl, tfac, packed, hold, in_sem, out_sem):
    steps = packed.shape[0]
    v_rows = refl.shape[1]
    t_rows = tfac.shape[1]
    loads, stores = [], []
    for s in range(steps):
        slot = slots[s]
        loads.append(
            (
                pltpu.make_async_copy(refl.at[slot], hold.at[s, pl.ds(0, v_rows)], in_sem.at[s, 0]),
                pltpu.make_async_copy(tfac.at[slot], hold.at[s, pl.ds(v_rows, t_rows)], in_sem.at[s, 1]),
            )
        )
        stores.append(pltpu.make_async_copy(hold.at[s], packed.at[s], out_sem.at[s]))
    for pair in loads:
        for copy in pair:
            copy.start()
    for pair, store in zip(loads, stores):
        for copy in pair:
            copy.wait()
        store.start()
    for store in stores:
        store.wait()


def main_kernel(n, rows_n, groups, packed, eig, out, field, buf, inb, back, landed, own_sem, eig_sem, out_sem,
                ring_send, ring_recv, up_send, up_recv, down_send, down_recv):
    steps, piece, _ = packed.shape
    v_rows = groups * B // n
    per_group = n // groups
    half = piece // 2
    hops = n // 2
    row = lax.axis_index("row")
    col = lax.axis_index("col")
    right = lax.rem(col + 1, n)
    left = lax.rem(col + n - 1, n)
    has_down = row < rows_n - 1
    has_up = row > 0
    down = jnp.minimum(row + 1, rows_n - 1)
    up = jnp.maximum(row - 1, 0)

    eig_copy = pltpu.make_async_copy(eig, field, eig_sem)
    eig_copy.start()

    barrier = pltpu.get_barrier_semaphore()
    pl.semaphore_signal(barrier, inc=1, device_id=(row, left), device_id_type=MESH)
    pl.semaphore_signal(barrier, inc=1, device_id=(row, right), device_id_type=MESH)

    @pl.when(has_up)
    def _():
        pl.semaphore_signal(barrier, inc=1, device_id=(up, col), device_id_type=MESH)

    @pl.when(has_down)
    def _():
        pl.semaphore_signal(barrier, inc=1, device_id=(down, col), device_id_type=MESH)

    pl.semaphore_wait(barrier, 2 + jnp.minimum(row, 1) + jnp.minimum(rows_n - 1 - row, 1))

    def ring_copy(s, way, hop, part):
        target = right if way == 0 else left
        owner = lax.rem(col + n - hop, n) if way == 0 else lax.rem(col + hop, n)
        span = pl.ds(part * half, half)
        src = packed.at[s, span] if hop == 0 else buf.at[s, owner, span]
        return pltpu.make_async_remote_copy(
            src_ref=src,
            dst_ref=buf.at[s, owner, span],
            send_sem=ring_send.at[s, way, hop, part],
            recv_sem=ring_recv.at[s, way, hop, part],
            device_id=(row, target),
            device_id_type=MESH,
        )

    def parts_of(way, hop):
        order = (0, 1) if way == 0 else (1, 0)
        return order[:1] if hop == hops - 1 else order

    def send_own(s):
        for k in range(len(parts_of(0, 0))):
            for way in (0, 1):
                ring_copy(s, way, 0, parts_of(way, 0)[k]).start()

    def forward(s):
        for hop in range(1, hops):
            for k in range(len(parts_of(0, hop))):
                for way in (0, 1):
                    part = parts_of(way, hop)[k]
                    ring_copy(s, way, hop - 1, part).wait_recv()
                    ring_copy(s, way, hop, part).start()

    def finish(s):
        for hop in range(hops):
            for way in (0, 1):
                done = parts_of(way, hop + 1) if hop + 1 < hops else ()
                for part in parts_of(way, hop):
                    if part not in done:
                        ring_copy(s, way, hop, part).wait_recv()

    def vectors_of(s, g):
        block = buf[s, g * per_group:(g + 1) * per_group, :v_rows]
        return split(block.reshape(B, W))

    def factor_of(s, g):
        block = buf[s, g * per_group:(g + 1) * per_group, v_rows:]
        return split(block.reshape(W, W))

    def coeffs_of(s, g, vectors, rows):
        coupling = product(vectors, split(rows), ((0,), (0,)))
        return split(product(factor_of(s, g), split(coupling), ((1,), (0,))))

    def apply_local(s, g, start):
        vectors = vectors_of(s, g)
        rows = field[start:start + B]
        coeffs = coeffs_of(s, g, vectors, rows)
        field[start:start + B] = rows - product(vectors, coeffs, ((1,), (0,)))

    def up_copy(i):
        return pltpu.make_async_remote_copy(
            src_ref=field.at[pl.ds(0, W)], dst_ref=inb.at[i],
            send_sem=up_send.at[i], recv_sem=up_recv.at[i],
            device_id=(up, col), device_id_type=MESH,
        )

    def down_copy(i):
        return pltpu.make_async_remote_copy(
            src_ref=back.at[i], dst_ref=landed.at[i],
            send_sem=down_send.at[i], recv_sem=down_recv.at[i],
            device_id=(down, col), device_id_type=MESH,
        )

    low = groups * B - W

    send_own(0)
    own = [pltpu.make_async_copy(packed.at[s], buf.at[s, col], own_sem.at[s]) for s in range(steps)]
    for copy in own:
        copy.start()
    eig_copy.wait()
    for s in range(steps):
        forward(s)
        if s + 1 < steps:
            send_own(s + 1)
        own[s].wait()
        finish(s)
        i = s // 2
        if s % 2 == 0:
            for g in range(groups):
                apply_local(s, g, g * B)
                if g == 0 and s + 1 < steps:
                    @pl.when(has_up)
                    def _():
                        up_copy(i).start()
        else:
            @pl.when(has_down)
            def _():
                up_copy(i).wait_recv()
                g = groups - 1
                vectors = vectors_of(s, g)
                rows = jnp.concatenate([field[low:], inb[i]], axis=0)
                coeffs = coeffs_of(s, g, vectors, rows)
                bottom = (vectors[0][W:], vectors[1][W:])
                back[i] = rows[W:] - product(bottom, coeffs, ((1,), (0,)))
                down_copy(i).start()
                top = (vectors[0][:W], vectors[1][:W])
                field[low:] = rows[:W] - product(top, coeffs, ((1,), (0,)))

            for g in range(groups - 1):
                apply_local(s, g, W + g * B)

            @pl.when(has_up)
            def _():
                up_copy(i).wait_send()
                down_copy(i).wait_recv()
                field[:W] = landed[i]

    store = pltpu.make_async_copy(field, out, out_sem)
    store.start()
    for s in range(steps):
        for way in (0, 1):
            for hop in range(hops):
                for part in parts_of(way, hop):
                    ring_copy(s, way, hop, part).wait_send()

    @pl.when(has_down)
    def _():
        for i in range(steps // 2):
            down_copy(i).wait_send()

    store.wait()


def line_kernel(rows_n, sched_all, refl, tfac, eig, out, sched, refl_in, tfac_in, field, buf, fed, inb, back, landed,
                local, eig_sem, sends, recvs, turn_sem):
    steps, v_rows, _ = refl.shape
    low = B + W
    last = steps - 1
    row = lax.axis_index("row")
    col = lax.axis_index("col")
    odd = lax.rem(row, 2)
    inner = (col == 1) | (col == 2)
    partner = col + 1 - 2 * lax.rem(col, 2)
    other = 3 - col
    mate = row + 1 - 2 * odd
    beyond = row - 1 + 2 * odd
    has_beyond = (beyond >= 0) & (beyond < rows_n)
    beyond = jnp.clip(beyond, 0, rows_n - 1)
    early = odd == 0
    late = odd == 1
    has_down = row < rows_n - 1
    has_up = row > 0
    down = jnp.minimum(row + 1, rows_n - 1)
    up = jnp.maximum(row - 1, 0)

    def remote(src, dst, send, recv, target):
        return pltpu.make_async_remote_copy(
            src_ref=src, dst_ref=dst, send_sem=send, recv_sem=recv,
            device_id=target, device_id_type=MESH,
        )

    refl_load = pltpu.make_async_copy(refl, refl_in, local.at[0])
    tfac_load = pltpu.make_async_copy(tfac, tfac_in, local.at[1])
    eig_load = pltpu.make_async_copy(eig, field.at[0], eig_sem)
    sched_load = pltpu.make_async_copy(sched_all, sched, local.at[2])
    sched_load.start()
    refl_load.start()
    tfac_load.start()

    barrier = pltpu.get_barrier_semaphore()

    def greet(target):
        pl.semaphore_signal(barrier, inc=1, device_id=target, device_id_type=MESH)

    @pl.when(has_beyond)
    def _():
        greet((beyond, partner))
        greet((beyond, col))

    greet((row, partner))
    greet((mate, partner))
    greet((mate, col))

    @pl.when(inner)
    def _():
        greet((row, other))
        greet((mate, other))

    sched_load.wait()
    refl_load.wait()
    tfac_load.wait()

    def pick(s):
        slot = sched[col // 2, s]
        buf[s, col, :v_rows] = refl_in[slot]
        buf[s, col, v_rows:] = tfac_in[slot]

    pick(0)

    pl.semaphore_wait(barrier, 3 + 2 * has_beyond.astype(jnp.int32) + 2 * inner.astype(jnp.int32))

    cuts = (2, 2, 1, 3)
    piece = buf.shape[2]

    def span(s, k):
        size = piece // cuts[s]
        return pl.ds((k + 2) % 3 * size if s == last else k * size, size)

    def feed(s, k):
        slot = sum(cuts[:s]) + k
        return remote(buf.at[s, col, span(s, k)], fed.at[s, span(s, k)],
                      sends.at[1 + k if s == last else 0], recvs.at[slot], (mate, partner))

    def feeds():
        return remote(buf.at[pl.ds(0, last), col], fed.at[pl.ds(0, last)], sends.at[0], recvs.at[0], (mate, partner))

    column_rows = ((0, B), (B, W), (B + W, W))

    def columns(g):
        rows = pl.ds(*column_rows[g])
        return remote(eig.at[rows], field.at[1, rows], sends.at[4 + g], recvs.at[8 + g], (row, partner))

    lead = piece // 3

    def own(s):
        return remote(buf.at[s, col], buf.at[s, col], sends.at[0], recvs.at[11 + s], (row, other))

    def own_arrival(s):
        return remote(buf.at[s, other], buf.at[s, other], sends.at[0], recvs.at[11 + s], (row, other))

    def own_last(k, owner):
        part = buf.at[last, owner, (pl.ds(lead, piece - lead), pl.ds(0, lead))[k]]
        return remote(part, part, sends.at[0], recvs.at[(11 + last, 25)[k]], (row, other))

    def send_last():
        own_last(0, col).start()
        own_last(1, col).start()

    def own_all():
        return remote(buf.at[:, col], buf.at[:, col], sends.at[0], recvs.at[11], (row, other))

    def relay(s, k):
        return remote(fed.at[s, span(s, k)], buf.at[s, partner, span(s, k)],
                      sends.at[1], recvs.at[26 if s == last and k == 2 else 15 + s], (mate, other))

    def relay_end():
        rows = pl.ds(lead, lead)
        return remote(fed.at[last, rows], buf.at[last, 3 - partner, rows],
                      sends.at[1], recvs.at[26], (mate, other))

    def relay_lead():
        rows = pl.ds(0, 2 * lead)
        return remote(fed.at[last, rows], buf.at[last, 3 - partner, rows],
                      sends.at[1], recvs.at[15 + last], (mate, other))

    def relay_arrival(s):
        return remote(fed.at[s], buf.at[s, 3 - partner], sends.at[1], recvs.at[15 + s], (mate, other))

    def relay_all():
        return remote(fed, buf.at[:, partner], sends.at[1], recvs.at[15], (mate, other))

    def hand(s, k):
        return remote(fed.at[s, span(s, k)], buf.at[s, partner, span(s, k)],
                      sends.at[2], recvs.at[19 + s], (mate, col))

    def hand_arrival(s):
        return remote(fed.at[s], buf.at[s, partner], sends.at[2], recvs.at[19 + s], (mate, col))

    def hand_all():
        return remote(fed, buf.at[:, partner], sends.at[2], recvs.at[19], (mate, col))

    def result(part, src, target_row):
        rows = (pl.ds(0, W), pl.ds(W, B), pl.ds(low, W))[part]
        return remote(src, out.at[rows], sends.at[10 + part], recvs.at[5 + part], (target_row, partner))

    def vectors_of(s, g):
        return split(buf[s, 2 * g:2 * g + 2, :v_rows].reshape(B, W))

    def factor_of(s, g):
        return split(buf[s, 2 * g:2 * g + 2, v_rows:].reshape(W, W))

    def coeffs_of(vectors, factor, rows):
        coupling = product(vectors, split(rows), ((0,), (0,)))
        return split(product(factor, split(coupling), ((1,), (0,))))

    def load(zs, start, size):
        return jnp.concatenate([field[z, start:start + size] for z in zs], axis=1)

    def save(zs, start, value):
        cols = value.shape[1] // len(zs)
        for k, z in enumerate(zs):
            field[z, start:start + value.shape[0]] = value[:, k * cols:(k + 1) * cols]

    def apply_local(s, g, zs, start):
        vectors = vectors_of(s, g)
        rows = load(zs, start, B)
        coeffs = coeffs_of(vectors, factor_of(s, g), rows)
        save(zs, start, rows - product(vectors, coeffs, ((1,), (0,))))

    def up_copy(i, z):
        return remote(field.at[z, pl.ds(0, W)], inb.at[i, z], sends.at[3 + z], recvs.at[23 + z], (up, col))

    def down_copy(z):
        return remote(back.at[0, z], landed.at[z], sends.at[7 + z], recvs.at[27 + z], (down, col))

    def down_final():
        return remote(back.at[1, 0], out.at[pl.ds(0, W)], sends.at[9], recvs.at[29], (down, col))

    def send_up(s, zs):
        @pl.when(has_up)
        def _():
            for z in zs:
                up_copy(s // 2, z).start()

    def straddle_body(s, zs, send):
        i = s // 2
        vectors = vectors_of(s, 1)
        below = jnp.concatenate([inb[i, z] for z in zs], axis=1)
        rows = jnp.concatenate([load(zs, low, W), below], axis=0)
        coeffs = coeffs_of(vectors, factor_of(s, 1), rows)
        bottom = (vectors[0][W:], vectors[1][W:])
        value = rows[W:] - product(bottom, coeffs, ((1,), (0,)))
        cols = value.shape[1] // len(zs)
        for k, z in enumerate(zs):
            back[i, z] = value[:, k * cols:(k + 1) * cols]
        send()
        top = (vectors[0][:W], vectors[1][:W])
        save(zs, low, rows[:W] - product(top, coeffs, ((1,), (0,))))

    def straddle(s, zs, send):
        @pl.when(has_down)
        def _():
            for z in zs:
                up_copy(s // 2, z).wait_recv()
            straddle_body(s, zs, send)

    def settle(z):
        @pl.when(has_up)
        def _():
            up_copy(0, z).wait_send()
            down_copy(z).wait_recv()
            field[z, :W] = landed[z]

    def pass_chunk(s, k):
        feed(s, k).wait_recv()
        relay(s, k).start()
        hand(s, k).start()

    def passed(s):
        for k in range(cuts[s]):
            pass_chunk(s, k)

    def near(s):
        hand_arrival(s).wait_recv()

    def far(s):
        own_arrival(s).wait_recv()
        relay_arrival(s).wait_recv()

    def far_lead():
        own_last(0, other).wait_recv()
        relay_lead().wait_recv()

    def far_end():
        own_last(1, other).wait_recv()
        relay_end().wait_recv()

    def store(part):
        rows = (pl.ds(0, W), pl.ds(W, B), pl.ds(low, W))[part]
        return pltpu.make_async_copy(field.at[0, rows], out.at[rows], local.at[part])

    top_row = (col < 2) & (row == 0)
    share_slot = {last: 0, 0: 1, 2: 2}

    def share(s):
        part = buf.at[s, col]
        return remote(part, part, sends.at[13 if s == last else 2 + share_slot[s]], recvs.at[share_slot[s]], (row, partner))

    def share_arrival(s):
        part = buf.at[s, partner]
        return remote(part, part, sends.at[13 if s == last else 2 + share_slot[s]], recvs.at[share_slot[s]], (row, partner))

    def half_result(part, half):
        start = (0, None, low)[part] + half * lead
        src = back.at[1, 1, pl.ds(half * lead, lead)] if part == 0 else field.at[1, pl.ds(start, lead)]
        return remote(src, out.at[pl.ds(start, lead)], sends.at[10 + part], recvs.at[5 + part],
                      (down if part == 0 else row, partner))

    def rows_of(owner, start):
        return split(buf[last, owner, start:start + lead])

    def joined(a, b):
        return jnp.concatenate([a[0], b[0]], axis=0), jnp.concatenate([a[1], b[1]], axis=0)

    def late_straddle():
        far_lead()

        @pl.when(jnp.logical_not(has_down))
        def _():
            far_end()
            half_result(2, 0).start()
            half_result(2, 1).start()

        @pl.when(has_down)
        def _():
            up_copy(1, 1).wait_recv()
            factor = factor_of(last, 1)
            inside = joined(rows_of(2, lead), rows_of(3, 0))
            rows_in = jnp.concatenate([field[1, low + lead:low + W], inb[1, 1, :lead]], axis=0)
            rows_out = jnp.concatenate([field[1, low:low + lead], inb[1, 1, lead:]], axis=0)
            part = product(inside, split(rows_in), ((0,), (0,)))
            scaled = split(product(inside, factor, ((1,), (0,))))
            far_end()
            outside = joined(rows_of(2, 0), rows_of(3, lead))
            coupling = split(part + product(outside, split(rows_out), ((0,), (0,))))
            value = rows_in - product(scaled, coupling, ((1,), (0,)))
            back[1, 1, :lead] = value[lead:]
            field[1, low + lead:low + W] = value[:lead]

            @pl.when(row != 1)
            def _():
                half_result(0, 0).start()

            half_result(2, 1).start()
            ends = split(product(outside, factor, ((1,), (0,))))
            value = rows_out - product(ends, coupling, ((1,), (0,)))
            back[1, 1, lead:] = value[lead:]
            field[1, low:low + lead] = value[:lead]

            @pl.when(row == 1)
            def _():
                half_result(2, 0).start()
                half_result(0, 0).start()
                half_result(0, 1).start()

            @pl.when(row != 1)
            def _():
                half_result(0, 1).start()
                half_result(2, 0).start()

    def state(part, start):
        rows = pl.ds(start, W)
        return remote(field.at[1, rows], field.at[0, rows], sends.at[5 + part], recvs.at[3 + part], (row, partner))

    def state_up():
        return remote(field.at[1, pl.ds(0, W)], inb.at[1, 0], sends.at[6], recvs.at[4], (up, partner))

    def bottom_result():
        return remote(back.at[1, 0], out.at[pl.ds(0, W)], sends.at[10], recvs.at[5], (down, col))

    @pl.when(jnp.logical_not(inner))
    def _():
        def turn():
            pl.semaphore_signal(turn_sem, inc=1, device_id=(mate, col), device_id_type=MESH)

        for k in range(last):
            if k > 0:
                pick(k)
            for c in range(cuts[k]):
                feed(k, c).start()
        columns(0).start()
        pick(last)

        def wait_turn():
            pl.semaphore_wait(turn_sem, 1)

        def last_feed():
            for c in range(cuts[last]):
                feed(last, c).start()

        @pl.when(late)
        def _():
            wait_turn()

        columns(1).start()
        columns(2).start()
        columns(1).wait_send()

        @pl.when(early)
        def _():
            turn()
            columns(2).wait_send()
            wait_turn()

        @pl.when(late)
        def _():
            columns(2).wait_send()
            turn()
            wait_turn()

        last_feed()
        feed(last, 0).wait_send()
        feed(last, 1).wait_send()

        @pl.when(early)
        def _():
            turn()

        feed(last, 2).wait_send()
        share_arrival(last).wait_recv()

        @pl.when(top_row)
        def _():
            share_arrival(0).wait_recv()
            share_arrival(2).wait_recv()
            top_load = pltpu.make_async_copy(eig.at[pl.ds(0, B)], field.at[1, pl.ds(0, B)], eig_sem)
            top_load.start()
            top_load.wait()
            apply_local(0, 0, (1,), 0)
            field[0, :W] = field[1, :W]
            state(1, W).wait_recv()
            apply_local(2, 0, (0,), 0)
            store(0).start()

        state(0, W).wait_recv()

        @pl.when(col == 0)
        def _():
            @pl.when(has_up)
            def _():
                state(1, W).wait_recv()

            apply_local(last, 0, (0,), W)
            store(1).start()

            @pl.when(has_up)
            def _():
                result(0, field.at[0, pl.ds(0, W)], row).wait_recv()

            @pl.when(jnp.logical_not(has_up))
            def _():
                store(0).wait()

            result(2, field.at[0, pl.ds(0, W)], row).wait_recv()
            store(1).wait()

        @pl.when(col == 3)
        def _():
            @pl.when(has_down)
            def _():
                state_up().wait_recv()
                straddle_body(last, (0,), lambda: bottom_result().start())

            store(2).start()
            result(0, field.at[0, pl.ds(0, W)], row).wait_recv()
            result(1, field.at[0, pl.ds(0, B)], row).wait_recv()
            store(2).wait()

            @pl.when(has_down)
            def _():
                bottom_result().wait_send()

        feeds().wait_send()
        columns(0).wait_send()

    @pl.when(inner)
    def _():
        own(0).start()
        eig_load.start()
        for s in range(1, steps):
            pick(s)
        passed(0)
        own(1).start()
        eig_load.wait()
        near(0)

        @pl.when(col == 1)
        def _():
            apply_local(0, 0, (0,), 0)
            send_up(0, (0,))

        @pl.when(col == 2)
        def _():
            apply_local(0, 1, (0,), B)

        passed(1)
        share(last).start()

        @pl.when(top_row)
        def _():
            share(0).start()
            share(2).start()


        @pl.when(early)
        def _():
            own(2).start()

        far(0)
        near(1)

        @pl.when(col == 1)
        def _():
            apply_local(0, 1, (0,), B)
            apply_local(1, 0, (0,), W)

        @pl.when(col == 2)
        def _():
            apply_local(0, 0, (0,), 0)
            send_up(0, (0,))
            straddle(1, (0,), lambda: down_copy(0).start())

        passed(2)

        @pl.when(early)
        def _():
            send_last()

        @pl.when(late)
        def _():
            own(2).start()

        far(1)

        @pl.when(col == 1)
        def _():
            straddle(1, (0,), lambda: down_copy(0).start())

        @pl.when(col == 2)
        def _():
            apply_local(1, 0, (0,), W)

        columns(0).wait_recv()
        apply_local(0, 0, (1,), 0)
        send_up(0, (1,))
        settle(0)
        near(2)

        @pl.when(col == 1)
        def _():
            apply_local(2, 0, (0,), 0)
            send_up(2, (0,))

        @pl.when(col == 2)
        def _():
            apply_local(2, 1, (0,), B)

        def far_even():
            @pl.when(col == 1)
            def _():
                apply_local(2, 1, (0,), B)

            @pl.when(col == 2)
            def _():
                apply_local(2, 0, (0,), 0)
                send_up(2, (0,))

        @pl.when(early)
        def _():
            far(2)
            far_even()

        columns(1).wait_recv()
        columns(2).wait_recv()
        apply_local(0, 1, (1,), B)
        straddle(1, (1,), lambda: down_copy(1).start())

        apply_local(1, 0, (1,), W)

        @pl.when(top_row)
        def _():
            state(1, W).start()

        @pl.when(late)
        def _():
            pass_chunk(3, 0)

        @pl.when(col == 2)
        def _():
            apply_local(2, 1, (1,), B)
            state(0, low).start()

        @pl.when(late)
        def _():
            far(2)

        @pl.when(col == 1)
        def _():
            apply_local(2, 1, (1,), B)
            state(0, B).start()


        @pl.when(late)
        def _():
            pass_chunk(3, 1)

        settle(1)

        @pl.when(late)
        def _():
            pass_chunk(3, 2)
            send_last()

        @pl.when(jnp.logical_not(top_row))
        def _():
            apply_local(2, 0, (1,), 0)

        @pl.when((col == 1) & has_up)
        def _():
            state(1, W).start()
            up_copy(1, 1).start()

        @pl.when((col == 2) & has_up)
        def _():
            state_up().start()


        @pl.when(early)
        def _():
            passed(3)


        @pl.when(late)
        def _():
            far_even()

        @pl.when(jnp.logical_not(has_up))
        def _():
            store(0).start()

        @pl.when((col == 2) & jnp.logical_not(has_up))
        def _():
            result(0, field.at[1, pl.ds(0, W)], row).start()

        def near_last():
            near(3)

            @pl.when(col == 1)
            def _():
                apply_local(last, 0, (0,), W)
                store(1).start()

            @pl.when(col == 2)
            def _():
                straddle(last, (0,), lambda: down_final().start())
                store(2).start()

        @pl.when(late)
        def _():
            near_last()

        @pl.when(early | (col == 2))
        def _():
            far_lead()
            far_end()

        @pl.when((col == 1) & early)
        def _():
            straddle(last, (1,), lambda: result(0, back.at[1, 1], down).start())
            result(2, field.at[1, pl.ds(low, W)], row).start()

        @pl.when((col == 1) & late)
        def _():
            late_straddle()

        @pl.when(col == 2)
        def _():
            apply_local(last, 0, (1,), W)
            result(1, field.at[1, pl.ds(W, B)], row).start()

        @pl.when(early)
        def _():
            near_last()

        @pl.when(col == 1)
        def _():
            straddle(last, (0,), lambda: down_final().start())
            store(2).start()

        @pl.when(col == 2)
        def _():
            apply_local(last, 0, (0,), W)
            store(1).start()

        share(last).wait_send()

        @pl.when(top_row)
        def _():
            share(0).wait_send()
            share(2).wait_send()

        state(0, W).wait_send()
        own_all().wait_send()
        relay_all().wait_send()
        hand_all().wait_send()

        @pl.when(has_up)
        def _():
            up_copy(last // 2, 0).wait_send()
            down_final().wait_recv()

        @pl.when(has_down)
        def _():
            down_copy(0).wait_send()
            down_copy(1).wait_send()
            down_final().wait_send()

        @pl.when(jnp.logical_not(has_up))
        def _():
            store(0).wait()

        @pl.when(col == 1)
        def _():
            state(1, W).wait_send()

            @pl.when(has_up)
            def _():
                up_copy(last // 2, 1).wait_send()

            @pl.when(has_down)
            def _():
                result(0, back.at[1, 1], down).wait_send()

            result(2, field.at[1, pl.ds(low, W)], row).wait_send()

        @pl.when(col == 2)
        def _():
            @pl.when(has_up)
            def _():
                state_up().wait_send()

            @pl.when(jnp.logical_not(has_up))
            def _():
                result(0, field.at[1, pl.ds(0, W)], row).wait_send()

            result(1, field.at[1, pl.ds(W, B)], row).wait_send()

        store(1).wait()
        store(2).wait()


def on_device(n, rows_n, eigvec, refl, tfac, sched):
    steps, v_rows, _ = refl.shape
    t_rows = tfac.shape[1]
    groups = sched.shape[0]
    evcount = eigvec.shape[1]
    piece = v_rows + t_rows
    hops = n // 2
    half_steps = steps // 2
    anywhere = pl.BlockSpec(memory_space=pl.ANY)
    if n == 4 and groups == 2 and steps == 4 and rows_n % 2 == 0:
        two = (half_steps, 2)
        dma = pltpu.SemaphoreType.DMA
        return pl.pallas_call(
            functools.partial(line_kernel, rows_n),
            out_shape=pltpu.VMEM(eigvec.shape, jnp.float32),
            in_specs=[anywhere, anywhere, anywhere, anywhere],
            out_specs=anywhere,
            scratch_shapes=[
                pltpu.SMEM(sched.shape, jnp.int32),
                pltpu.VMEM(refl.shape, jnp.float32),
                pltpu.VMEM(tfac.shape, jnp.float32),
                pltpu.VMEM((2, *eigvec.shape), jnp.float32),
                pltpu.VMEM((steps, n, piece, W), jnp.float32),
                pltpu.VMEM((steps, piece, W), jnp.float32),
                pltpu.VMEM((*two, W, evcount), jnp.float32),
                pltpu.VMEM((*two, W, evcount), jnp.float32),
                pltpu.VMEM((2, W, evcount), jnp.float32),
                dma((3,)),
                dma,
                dma((14,)),
                dma((30,)),
                pltpu.SemaphoreType.REGULAR,
            ],
            compiler_params=pltpu.CompilerParams(
                collective_id=0, has_side_effects=True, vmem_limit_bytes=60 << 20
            ),
            name="sweep",
        )(sched, refl, tfac, eigvec)
    owner = lax.axis_index("col") * v_rows // B
    slots = lax.dynamic_index_in_dim(sched, owner, 0, keepdims=False)
    packed = pl.pallas_call(
        pick_kernel,
        out_shape=jax.ShapeDtypeStruct((steps, piece, W), jnp.float32),
        in_specs=[pl.BlockSpec(memory_space=pltpu.SMEM), anywhere, anywhere],
        out_specs=anywhere,
        scratch_shapes=[
            pltpu.VMEM((steps, piece, W), jnp.float32),
            pltpu.SemaphoreType.DMA((steps, 2)),
            pltpu.SemaphoreType.DMA((steps,)),
        ],
        name="pick",
    )(slots, refl, tfac)
    return pl.pallas_call(
        functools.partial(main_kernel, n, rows_n, groups),
        out_shape=jax.ShapeDtypeStruct(eigvec.shape, jnp.float32),
        in_specs=[anywhere, anywhere],
        out_specs=anywhere,
        scratch_shapes=[
            pltpu.VMEM(eigvec.shape, jnp.float32),
            pltpu.VMEM((steps, n, piece, W), jnp.float32),
            pltpu.VMEM((half_steps, W, evcount), jnp.float32),
            pltpu.VMEM((half_steps, W, evcount), jnp.float32),
            pltpu.VMEM((half_steps, W, evcount), jnp.float32),
            pltpu.SemaphoreType.DMA((steps,)),
            pltpu.SemaphoreType.DMA,
            pltpu.SemaphoreType.DMA,
            pltpu.SemaphoreType.DMA((steps, 2, hops, 2)),
            pltpu.SemaphoreType.DMA((steps, 2, hops, 2)),
            pltpu.SemaphoreType.DMA((half_steps,)),
            pltpu.SemaphoreType.DMA((half_steps,)),
            pltpu.SemaphoreType.DMA((half_steps,)),
            pltpu.SemaphoreType.DMA((half_steps,)),
        ],
        compiler_params=pltpu.CompilerParams(
            collective_id=0, has_side_effects=True, vmem_limit_bytes=48 << 20
        ),
        name="sweep",
    )(packed, eigvec)


def solution(mesh):
    placed = (
        P("row", "col"),
        P(None, ("row", "col"), None),
        P(None, ("row", "col"), None),
        P("row", None),
    )
    body = functools.partial(on_device, mesh.shape["col"], mesh.shape["row"])
    return jax.shard_map(body, mesh=mesh, in_specs=placed, out_specs=P("row", "col"), check_vma=False)
```
